256 devices in a mesh: gr: 8 (over y, core), gc: 32 (over x, z).
Axes of the slice: x: 4, y: 4, z: 8, core: 2. Of those that a mesh axis runs over, the one named last changes fastest.
Arguments:
- below_factor: bfloat16 [31, 8, 64, 2, 32, 128], P(None, 'gr', None, None, 'gc'), may hold values from -0.046875 to 0.046875
- panel_factor: bfloat16 [31, 8, 64, 512], P(None, 'gr', 'gc'), may hold values from -0.046875 to 0.046875
- prior_factor: bfloat16 [512, 2, 32, 128], P('gr', None, 'gc'), may hold values from -0.25 to 0.25
- diag_factor: float32 [512, 512], replicated, may hold values from -1 to 3, as said below
- diag_inverse: float32 [512, 512], replicated, may hold values from -2 to 1, as said below
- below_adjoint: bfloat16 [31, 8, 64, 2, 32, 128], P(None, 'gr', None, None, 'gc'), may hold values from -6 to 6
- panel_adjoint: bfloat16 [31, 8, 64, 512], P(None, 'gr', 'gc'), may hold values from -6 to 6
- prior_adjoint: bfloat16 [512, 2, 32, 128], P('gr', None, 'gc'), may hold values from -6 to 6
- diag_adjoint: float32 [512, 512], replicated, may hold values from -6 to 6
Outputs:
- below_update: bfloat16 [31, 8, 64, 2, 32, 128], P(None, 'gr', None, None, 'gc')
- panel_gradient: bfloat16 [31, 8, 64, 512], P(None, 'gr', 'gc')
- prior_update: bfloat16 [512, 2, 32, 128], P('gr', None, 'gc')
- diag_gradient: float32 [512, 512], replicated
The draws below stay inside these ranges and needn't reach their ends.
Inputs may be any that keep to these rules, and one draw needn't show every extreme that they name: `diag_factor`: lower triangular, diagonal entries positive. `diag_inverse`: the inverse of diag_factor.
All inputs are finite; a program needn't handle non-finite values.
Results may differ from the reference program's by a relative error of at most 0.015.
Values may be sent and summed in bfloat16 or wider, within the bound.
A program may use at most 64 MiB of HBM per device.

```python
import math
import jax
import jax.numpy as jnp
from jax import lax

NB = 512
RB = 64
CB = 128
RT = 31
CT = 2
MB = 15872
PRIOR = 8192
N_GR = 8
N_GC = 32


def lower_factor(key):
    inner_key = jax.random.fold_in(key, 7)
    diag_key, off_key = jax.random.split(inner_key)
    diagonal = jax.random.uniform(diag_key, (NB,), jnp.float32, 1.0, 2.0)
    offdiag = jax.random.normal(off_key, (NB, NB), jnp.float32) * (0.5 / math.sqrt(NB))
    return jnp.tril(offdiag, -1) + jnp.diag(diagonal)


def draw_diag_factor(key, part):
    return lower_factor(key)


def draw_diag_inverse(key, part):
    factor = lower_factor(key)
    return jax.scipy.linalg.solve_triangular(factor, jnp.eye(NB, dtype=jnp.float32), lower=True)


def levels(stream_key, dims, shards, low, largest):
    def one(position, blocks):
        draws = jax.random.uniform(jax.random.fold_in(jax.random.fold_in(stream_key, 6), position), (blocks,), jnp.float32, low / len(shards), largest / len(shards))
        return jnp.repeat(jnp.exp(draws), dims[position] // blocks).reshape((-1,) + (1,) * (len(dims) - position - 1))

    level = one(*shards[0])
    for cut in shards[1:]:
        level = level * one(*cut)
    return level


def noise(stream_key, extent, deviation, reach, cuts=(), kind=jnp.bfloat16):
    entries = deviation * jax.random.normal(stream_key, extent, jnp.float32)
    if cuts:
        entries = entries * levels(stream_key, extent, cuts, -0.22, 0.18)
    return jnp.clip(entries, -reach, reach).astype(kind)


def setup_inputs(seed: int = 0) -> dict:
    arg_keys = jax.random.split(jax.random.key(seed), 10)
    below_factor = noise(arg_keys[0], (RT, N_GR, RB, CT, N_GC, CB), MB ** -0.5, 0.046875, ((1, 8), (4, 32)))
    panel_factor = noise(arg_keys[1], (RT, N_GR, RB, NB), MB ** -0.5, 0.046875, ((1, 8), (2, 32)))
    prior_factor = noise(arg_keys[2], (NB, CT, N_GC, CB), NB ** -0.5, 0.25, ((0, 8), (2, 32)))
    diag_factor = draw_diag_factor(jax.random.fold_in(arg_keys[9], 71), 0)
    diag_inverse = draw_diag_inverse(jax.random.fold_in(arg_keys[9], 71), 0)
    below_adjoint = noise(arg_keys[5], (RT, N_GR, RB, CT, N_GC, CB), 1.0, 6.0, ((1, 8), (4, 32)))
    panel_adjoint = noise(arg_keys[6], (RT, N_GR, RB, NB), 1.0, 6.0, ((1, 8), (2, 32)))
    prior_adjoint = noise(arg_keys[7], (NB, CT, N_GC, CB), 1.0, 6.0, ((0, 8), (2, 32)))
    diag_adjoint = noise(arg_keys[8], (NB, NB), 1.0, 6.0, (), jnp.float32)
    return dict(below_factor=below_factor, panel_factor=panel_factor, prior_factor=prior_factor, diag_factor=diag_factor, diag_inverse=diag_inverse, below_adjoint=below_adjoint, panel_adjoint=panel_adjoint, prior_adjoint=prior_adjoint, diag_adjoint=diag_adjoint)


def row_product(left_rows, right_rows):
    return lax.dot_general(left_rows.astype(jnp.float32), right_rows.astype(jnp.float32), (((0,), (0,)), ((), ())), preferred_element_type=jnp.float32)

def diag_solve(diag_factor, diag_inverse, diag_reduced):
    highest = lax.Precision.HIGHEST
    chol_proj = jnp.dot(diag_factor.T, diag_reduced, precision=highest)
    phi_lower = jnp.tril(chol_proj) - 0.5 * jnp.diag(jnp.diagonal(chol_proj))
    symmetric = 0.5 * (phi_lower + phi_lower.T)
    left_side = jnp.dot(diag_inverse.T, symmetric, precision=highest)
    return jnp.dot(left_side, diag_inverse, precision=highest)

def reference(below_factor, panel_factor, prior_factor, diag_factor, diag_inverse, below_adjoint, panel_adjoint, prior_adjoint, diag_adjoint):
    below_mat = below_factor.reshape(MB, PRIOR)
    below_bar = below_adjoint.reshape(MB, PRIOR)
    panel_mat = panel_factor.reshape(MB, NB)
    panel_bar = panel_adjoint.reshape(MB, NB)
    prior_mat = prior_factor.reshape(NB, PRIOR)
    prior_bar = prior_adjoint.reshape(NB, PRIOR)
    inverse_bf = diag_inverse.astype(jnp.bfloat16)
    panel_grad = jnp.dot(panel_bar.astype(jnp.float32), inverse_bf.astype(jnp.float32), preferred_element_type=jnp.float32).astype(jnp.bfloat16)
    cross_diag = row_product(panel_grad, panel_mat)
    diag_reduced = jnp.tril(diag_adjoint - cross_diag)
    diag_gradient = diag_solve(diag_factor, diag_inverse, diag_reduced)
    twice_bf = (2.0 * diag_gradient).astype(jnp.bfloat16)
    below_new = (below_bar.astype(jnp.float32) - jnp.dot(panel_grad.astype(jnp.float32), prior_mat.astype(jnp.float32), preferred_element_type=jnp.float32)).astype(jnp.bfloat16)
    prior_new = (prior_bar.astype(jnp.float32) - row_product(panel_grad, below_mat) - jnp.dot(twice_bf.astype(jnp.float32), prior_mat.astype(jnp.float32), preferred_element_type=jnp.float32)).astype(jnp.bfloat16)
    return (below_new.reshape(below_adjoint.shape), panel_grad.reshape(panel_factor.shape), prior_new.reshape(prior_adjoint.shape), diag_gradient)
```

```python
import functools

import jax
import jax.numpy as jnp
from jax import lax
from jax.experimental import pallas as pl
from jax.experimental.pallas import tpu as pltpu
from jax.sharding import PartitionSpec as P

MESH_ID = pl.DeviceIdType.MESH


def row_product(left_rows, right_rows):
    return lax.dot_general(
        left_rows, right_rows, (((0,), (0,)), ((), ())), preferred_element_type=jnp.float32
    )


def diag_solve(diag_factor, diag_inverse, diag_reduced):
    highest = lax.Precision.HIGHEST
    chol_proj = jnp.dot(diag_factor.T, diag_reduced, precision=highest)
    phi_lower = jnp.tril(chol_proj) - 0.5 * jnp.diag(jnp.diagonal(chol_proj))
    symmetric = 0.5 * (phi_lower + phi_lower.T)
    left_side = jnp.dot(diag_inverse.T, symmetric, precision=highest)
    return jnp.dot(left_side, diag_inverse, precision=highest)


def gather_kernel(n, x_ref, out_ref, send_sem, recv_sem, local_sem):
    me = lax.axis_index("gc")
    row = lax.axis_index("gr")
    rows = x_ref.shape[1]

    barrier = pltpu.get_barrier_semaphore()

    def greet(k, carry):
        peer = lax.rem(me + k, n)
        pl.semaphore_signal(barrier, inc=1, device_id=(row, peer), device_id_type=MESH_ID)
        return carry

    lax.fori_loop(1, n, greet, 0)
    pl.semaphore_wait(barrier, n - 1)

    own = pltpu.make_async_copy(x_ref, out_ref.at[:, pl.ds(me * rows, rows), :], local_sem)
    own.start()

    def remote(k, sender):
        peer = lax.rem(me + k, n)
        return pltpu.make_async_remote_copy(
            src_ref=x_ref,
            dst_ref=out_ref.at[:, pl.ds(sender * rows, rows), :],
            send_sem=send_sem.at[k],
            recv_sem=recv_sem.at[sender],
            device_id=(row, peer),
            device_id_type=MESH_ID,
        )

    def send(k, carry):
        remote(k, me).start()
        return carry

    lax.fori_loop(1, n, send, 0)

    def wait(k, carry):
        remote(k, me).wait_send()
        remote(k, lax.rem(me + n - k, n)).wait_recv()
        return carry

    lax.fori_loop(1, n, wait, 0)
    own.wait()


def gather_gc(block, n):
    tiles, rows, width = block.shape
    return pl.pallas_call(
        functools.partial(gather_kernel, n),
        out_shape=jax.ShapeDtypeStruct((tiles, rows * n, width), block.dtype),
        in_specs=[pl.BlockSpec(memory_space=pl.ANY)],
        out_specs=pl.BlockSpec(memory_space=pl.ANY),
        scratch_shapes=[
            pltpu.SemaphoreType.DMA((n,)),
            pltpu.SemaphoreType.DMA((n,)),
            pltpu.SemaphoreType.DMA,
        ],
        compiler_params=pltpu.CompilerParams(collective_id=0, has_side_effects=True),
    )(block)


def local(
    n_gc,
    below_factor,
    panel_factor,
    prior_factor,
    diag_factor,
    diag_inverse,
    below_adjoint,
    panel_adjoint,
    prior_adjoint,
    diag_adjoint,
):
    tile_count = below_factor.shape[0]
    tile_rows = below_factor.shape[2]
    local_rows = tile_count * tile_rows
    local_cols = below_factor.shape[3] * below_factor.shape[5]
    own_rows = panel_factor.shape[2]
    width = panel_factor.shape[3]
    prior_local = prior_factor.shape[0]
    below_mat = below_factor.reshape(local_rows, local_cols)
    below_bar = below_adjoint.reshape(local_rows, local_cols)
    inverse_bf = diag_inverse.astype(jnp.bfloat16)
    own_grad = jnp.dot(
        panel_adjoint.reshape(tile_count * own_rows, width),
        inverse_bf,
        preferred_element_type=jnp.float32,
    ).astype(jnp.bfloat16)
    panel_grad = own_grad.reshape(panel_adjoint.shape)
    both = jnp.concatenate(
        [own_grad.reshape(tile_count, own_rows, width), panel_factor.reshape(tile_count, own_rows, width)],
        axis=2,
    )
    whole = gather_gc(both, n_gc)
    grad_rows = whole[:, :, :width].reshape(local_rows, width)
    whole_factor = whole[:, :, width:].reshape(local_rows, width)
    summed = lax.psum(row_product(grad_rows, whole_factor).astype(jnp.bfloat16), "gr").astype(
        jnp.float32
    )
    diag_reduced = jnp.tril(diag_adjoint - summed)
    diag_gradient = diag_solve(diag_factor, diag_inverse, diag_reduced)
    prior_here = prior_factor.reshape(prior_local, local_cols)
    prior_whole = lax.all_gather(prior_here, "gr", axis=0, tiled=True)
    below_new = (
        below_bar.astype(jnp.float32)
        - jnp.dot(grad_rows, prior_whole, preferred_element_type=jnp.float32)
    ).astype(jnp.bfloat16)
    crossing = lax.psum_scatter(
        row_product(grad_rows, below_mat).astype(jnp.bfloat16),
        "gr",
        scatter_dimension=0,
        tiled=True,
    ).astype(jnp.float32)
    grid_row = lax.axis_index("gr")
    twice_rows = lax.dynamic_slice_in_dim(
        2.0 * diag_gradient, grid_row * prior_local, prior_local, 0
    ).astype(jnp.bfloat16)
    curvature = jnp.dot(twice_rows, prior_whole, preferred_element_type=jnp.float32)
    prior_bar = prior_adjoint.reshape(prior_local, local_cols).astype(jnp.float32)
    prior_new = (prior_bar - crossing - curvature).astype(jnp.bfloat16)
    return (
        below_new.reshape(below_adjoint.shape),
        panel_grad,
        prior_new.reshape(prior_adjoint.shape),
        diag_gradient,
    )


def solution(mesh):
    in_specs = (
        P(None, "gr", None, None, "gc", None),
        P(None, "gr", "gc", None),
        P("gr", None, "gc", None),
        P(),
        P(),
        P(None, "gr", None, None, "gc", None),
        P(None, "gr", "gc", None),
        P("gr", None, "gc", None),
        P(),
    )
    out_specs = (
        P(None, "gr", None, None, "gc", None),
        P(None, "gr", "gc", None),
        P("gr", None, "gc", None),
        P(),
    )
    return jax.shard_map(
        functools.partial(local, mesh.shape["gc"]),
        mesh=mesh,
        in_specs=in_specs,
        out_specs=out_specs,
        check_vma=False,
    )
```

```python
import functools

import jax
import jax.numpy as jnp
from jax import lax
from jax.experimental import pallas as pl
from jax.experimental.pallas import tpu as pltpu
from jax.sharding import PartitionSpec as P

MESH_ID = pl.DeviceIdType.MESH


def row_product(left_rows, right_rows):
    return lax.dot_general(
        left_rows, right_rows, (((0,), (0,)), ((), ())), preferred_element_type=jnp.float32
    )


def diag_solve(diag_factor, diag_inverse, diag_reduced):
    highest = lax.Precision.HIGHEST
    chol_proj = jnp.dot(diag_factor.T, diag_reduced, precision=highest)
    phi_lower = jnp.tril(chol_proj) - 0.5 * jnp.diag(jnp.diagonal(chol_proj))
    symmetric = 0.5 * (phi_lower + phi_lower.T)
    left_side = jnp.dot(diag_inverse.T, symmetric, precision=highest)
    return jnp.dot(left_side, diag_inverse, precision=highest)


def gather_kernel(n, x_ref, out_ref, send_sem, recv_sem, local_sem):
    me = lax.axis_index("gc")
    row = lax.axis_index("gr")
    rows = x_ref.shape[1]

    barrier = pltpu.get_barrier_semaphore()

    def greet(k, carry):
        peer = lax.rem(me + k, n)
        pl.semaphore_signal(barrier, inc=1, device_id=(row, peer), device_id_type=MESH_ID)
        return carry

    lax.fori_loop(1, n, greet, 0)
    pl.semaphore_wait(barrier, n - 1)

    own = pltpu.make_async_copy(x_ref, out_ref.at[:, pl.ds(me * rows, rows), :], local_sem)
    own.start()

    def remote(k, sender):
        peer = lax.rem(me + k, n)
        return pltpu.make_async_remote_copy(
            src_ref=x_ref,
            dst_ref=out_ref.at[:, pl.ds(sender * rows, rows), :],
            send_sem=send_sem.at[k],
            recv_sem=recv_sem.at[sender],
            device_id=(row, peer),
            device_id_type=MESH_ID,
        )

    def send(k, carry):
        remote(k, me).start()
        return carry

    lax.fori_loop(1, n, send, 0)

    def wait(k, carry):
        remote(k, me).wait_send()
        remote(k, lax.rem(me + n - k, n)).wait_recv()
        return carry

    lax.fori_loop(1, n, wait, 0)
    own.wait()


def gather_gc(block, n):
    tiles, rows, width = block.shape
    return pl.pallas_call(
        functools.partial(gather_kernel, n),
        out_shape=jax.ShapeDtypeStruct((tiles, rows * n, width), block.dtype),
        in_specs=[pl.BlockSpec(memory_space=pl.ANY)],
        out_specs=pl.BlockSpec(memory_space=pl.ANY),
        scratch_shapes=[
            pltpu.SemaphoreType.DMA((n,)),
            pltpu.SemaphoreType.DMA((n,)),
            pltpu.SemaphoreType.DMA,
        ],
        compiler_params=pltpu.CompilerParams(collective_id=0, has_side_effects=True),
    )(block)


def reduce_kernel(n, part_ref, prior_ref, cross_out, prior_out, crossing_out,
                  recv_part, cross_slots, prior_slots, sems):
    me = lax.axis_index("gr")
    col = lax.axis_index("gc")
    rows = prior_ref.shape[0]
    wide = cross_out.shape[2]

    barrier = pltpu.get_barrier_semaphore()

    def greet(k, carry):
        peer = lax.rem(me + k, n)
        pl.semaphore_signal(barrier, inc=1, device_id=(peer, col), device_id_type=MESH_ID)
        return carry

    lax.fori_loop(1, n, greet, 0)
    pl.semaphore_wait(barrier, n - 1)

    def prior_copy(k, sender):
        return pltpu.make_async_remote_copy(
            src_ref=prior_ref,
            dst_ref=prior_slots.at[sender],
            send_sem=sems.at[0, k],
            recv_sem=sems.at[1, sender],
            device_id=(lax.rem(me + k, n), col),
            device_id_type=MESH_ID,
        )

    def part_copy(k, sender):
        peer = lax.rem(me + k, n)
        return pltpu.make_async_remote_copy(
            src_ref=part_ref.at[pl.ds(pl.multiple_of(peer * rows, rows), rows), :],
            dst_ref=recv_part.at[sender],
            send_sem=sems.at[2, k],
            recv_sem=sems.at[3, sender],
            device_id=(peer, col),
            device_id_type=MESH_ID,
        )

    def cross_copy(k, sender):
        return pltpu.make_async_remote_copy(
            src_ref=cross_slots.at[me],
            dst_ref=cross_slots.at[sender],
            send_sem=sems.at[4, k],
            recv_sem=sems.at[5, sender],
            device_id=(lax.rem(me + k, n), col),
            device_id_type=MESH_ID,
        )

    def send_first(k, carry):
        prior_copy(k, me).start()
        part_copy(k, me).start()
        return carry

    lax.fori_loop(1, n, send_first, 0)
    prior_slots[me] = prior_ref[...]

    acc = part_ref[pl.ds(pl.multiple_of(me * rows, rows), rows), :].astype(jnp.float32)

    def add(k, total):
        sender = lax.rem(me + n - k, n)
        part_copy(k, me).wait_send()
        part_copy(k, sender).wait_recv()
        return total + recv_part[sender].astype(jnp.float32)

    acc = lax.fori_loop(1, n, add, acc)
    crossing_out[...] = acc[:, wide:]
    cross_slots[me] = acc[:, :wide].astype(cross_slots.dtype)

    def send_second(k, carry):
        cross_copy(k, me).start()
        return carry

    lax.fori_loop(1, n, send_second, 0)

    def wait_second(k, carry):
        sender = lax.rem(me + n - k, n)
        cross_copy(k, me).wait_send()
        cross_copy(k, sender).wait_recv()
        prior_copy(k, me).wait_send()
        prior_copy(k, sender).wait_recv()
        return carry

    lax.fori_loop(1, n, wait_second, 0)
    cross_out[...] = cross_slots[...]
    prior_out[...] = prior_slots[...]


def reduce_gr(part, prior_rows, n):
    rows, cols = prior_rows.shape
    wide = part.shape[1] - cols
    vmem = pl.BlockSpec(memory_space=pltpu.VMEM)
    return pl.pallas_call(
        functools.partial(reduce_kernel, n),
        out_shape=(
            jax.ShapeDtypeStruct((n, rows, wide), part.dtype),
            jax.ShapeDtypeStruct((n, rows, cols), prior_rows.dtype),
            jax.ShapeDtypeStruct((rows, cols), jnp.float32),
        ),
        in_specs=[vmem, vmem],
        out_specs=(vmem, vmem, vmem),
        scratch_shapes=[
            pltpu.VMEM((n, rows, part.shape[1]), part.dtype),
            pltpu.VMEM((n, rows, wide), part.dtype),
            pltpu.VMEM((n, rows, cols), prior_rows.dtype),
            pltpu.SemaphoreType.DMA((6, n)),
        ],
        compiler_params=pltpu.CompilerParams(collective_id=1, has_side_effects=True),
    )(part, prior_rows)


def local(
    n_gc,
    n_gr,
    below_factor,
    panel_factor,
    prior_factor,
    diag_factor,
    diag_inverse,
    below_adjoint,
    panel_adjoint,
    prior_adjoint,
    diag_adjoint,
):
    tile_count = below_factor.shape[0]
    tile_rows = below_factor.shape[2]
    local_rows = tile_count * tile_rows
    local_cols = below_factor.shape[3] * below_factor.shape[5]
    own_rows = panel_factor.shape[2]
    width = panel_factor.shape[3]
    prior_local = prior_factor.shape[0]
    below_mat = below_factor.reshape(local_rows, local_cols)
    below_bar = below_adjoint.reshape(local_rows, local_cols)
    inverse_bf = diag_inverse.astype(jnp.bfloat16)
    own_grad = jnp.dot(
        panel_adjoint.reshape(tile_count * own_rows, width),
        inverse_bf,
        preferred_element_type=jnp.float32,
    ).astype(jnp.bfloat16)
    panel_grad = own_grad.reshape(panel_adjoint.shape)
    both = jnp.concatenate(
        [own_grad.reshape(tile_count, own_rows, width), panel_factor.reshape(tile_count, own_rows, width)],
        axis=2,
    )
    whole = gather_gc(both, n_gc)
    grad_rows = whole[:, :, :width].reshape(local_rows, width)
    whole_factor = whole[:, :, width:].reshape(local_rows, width)
    prior_here = prior_factor.reshape(prior_local, local_cols)
    part = jnp.concatenate(
        [row_product(grad_rows, whole_factor), row_product(grad_rows, below_mat)], axis=1
    ).astype(jnp.bfloat16)
    cross_rows, prior_rows, crossing = reduce_gr(part, prior_here, n_gr)
    summed = cross_rows.reshape(width, width).astype(jnp.float32)
    prior_whole = prior_rows.reshape(width, local_cols)
    diag_reduced = jnp.tril(diag_adjoint - summed)
    diag_gradient = diag_solve(diag_factor, diag_inverse, diag_reduced)
    below_new = (
        below_bar.astype(jnp.float32)
        - jnp.dot(grad_rows, prior_whole, preferred_element_type=jnp.float32)
    ).astype(jnp.bfloat16)
    grid_row = lax.axis_index("gr")
    twice_rows = lax.dynamic_slice_in_dim(
        2.0 * diag_gradient, grid_row * prior_local, prior_local, 0
    ).astype(jnp.bfloat16)
    curvature = jnp.dot(twice_rows, prior_whole, preferred_element_type=jnp.float32)
    prior_bar = prior_adjoint.reshape(prior_local, local_cols).astype(jnp.float32)
    prior_new = (prior_bar - crossing - curvature).astype(jnp.bfloat16)
    return (
        below_new.reshape(below_adjoint.shape),
        panel_grad,
        prior_new.reshape(prior_adjoint.shape),
        diag_gradient,
    )


def solution(mesh):
    in_specs = (
        P(None, "gr", None, None, "gc", None),
        P(None, "gr", "gc", None),
        P("gr", None, "gc", None),
        P(),
        P(),
        P(None, "gr", None, None, "gc", None),
        P(None, "gr", "gc", None),
        P("gr", None, "gc", None),
        P(),
    )
    out_specs = (
        P(None, "gr", None, None, "gc", None),
        P(None, "gr", "gc", None),
        P("gr", None, "gc", None),
        P(),
    )
    return jax.shard_map(
        functools.partial(local, mesh.shape["gc"], mesh.shape["gr"]),
        mesh=mesh,
        in_specs=in_specs,
        out_specs=out_specs,
        check_vma=False,
    )
```

```python
import functools

import jax
import jax.numpy as jnp
from jax import lax
from jax.experimental import pallas as pl
from jax.experimental.pallas import tpu as pltpu
from jax.sharding import PartitionSpec as P

MESH_ID = pl.DeviceIdType.MESH


def row_product(left_rows, right_rows):
    return lax.dot_general(
        left_rows, right_rows, (((0,), (0,)), ((), ())), preferred_element_type=jnp.float32
    )


def diag_solve(diag_factor, diag_inverse, diag_reduced):
    highest = lax.Precision.HIGHEST
    chol_proj = jnp.dot(diag_factor.T, diag_reduced, precision=highest)
    phi_lower = jnp.tril(chol_proj) - 0.5 * jnp.diag(jnp.diagonal(chol_proj))
    symmetric = 0.5 * (phi_lower + phi_lower.T)
    left_side = jnp.dot(diag_inverse.T, symmetric, precision=highest)
    return jnp.dot(left_side, diag_inverse, precision=highest)


def gather_kernel(n, line, x_ref, out_ref, sems, local_sem):
    me = lax.axis_index("gc")
    row = lax.axis_index("gr")
    rows = x_ref.shape[1]
    lines = n // line
    pos = lax.rem(me, line)
    grp = me // line
    base = grp * line

    def line_peer(k):
        return base + lax.rem(pos + k, line)

    def cross_peer(k):
        return lax.rem(grp + k, lines) * line + pos

    barrier = pltpu.get_barrier_semaphore()

    def greet_line(k, carry):
        pl.semaphore_signal(barrier, inc=1, device_id=(row, line_peer(k)), device_id_type=MESH_ID)
        return carry

    def greet_cross(k, carry):
        pl.semaphore_signal(barrier, inc=1, device_id=(row, cross_peer(k)), device_id_type=MESH_ID)
        return carry

    lax.fori_loop(1, line, greet_line, 0)
    lax.fori_loop(1, lines, greet_cross, 0)
    pl.semaphore_wait(barrier, line + lines - 2)

    own = pltpu.make_async_copy(x_ref, out_ref.at[:, pl.ds(me * rows, rows), :], local_sem)
    own.start()

    def first(k, sender_pos):
        return pltpu.make_async_remote_copy(
            src_ref=x_ref,
            dst_ref=out_ref.at[:, pl.ds((base + sender_pos) * rows, rows), :],
            send_sem=sems.at[0, k],
            recv_sem=sems.at[1, sender_pos],
            device_id=(row, line_peer(k)),
            device_id_type=MESH_ID,
        )

    def send_first(k, carry):
        first(k, pos).start()
        return carry

    lax.fori_loop(1, line, send_first, 0)

    def wait_first(k, carry):
        first(k, pos).wait_send()
        first(k, lax.rem(pos + line - k, line)).wait_recv()
        return carry

    lax.fori_loop(1, line, wait_first, 0)
    own.wait()

    span = line * rows

    def second(k, sender_grp):
        return pltpu.make_async_remote_copy(
            src_ref=out_ref.at[:, pl.ds(base * rows, span), :],
            dst_ref=out_ref.at[:, pl.ds(sender_grp * span, span), :],
            send_sem=sems.at[2, k],
            recv_sem=sems.at[3, sender_grp],
            device_id=(row, cross_peer(k)),
            device_id_type=MESH_ID,
        )

    def send_second(k, carry):
        second(k, grp).start()
        return carry

    lax.fori_loop(1, lines, send_second, 0)

    def wait_second(k, carry):
        second(k, grp).wait_send()
        second(k, lax.rem(grp + lines - k, lines)).wait_recv()
        return carry

    lax.fori_loop(1, lines, wait_second, 0)


def gather_gc(block, n, line):
    tiles, rows, width = block.shape
    return pl.pallas_call(
        functools.partial(gather_kernel, n, line),
        out_shape=jax.ShapeDtypeStruct((tiles, rows * n, width), block.dtype),
        in_specs=[pl.BlockSpec(memory_space=pl.ANY)],
        out_specs=pl.BlockSpec(memory_space=pl.ANY),
        scratch_shapes=[
            pltpu.SemaphoreType.DMA((4, max(line, n // line))),
            pltpu.SemaphoreType.DMA,
        ],
        compiler_params=pltpu.CompilerParams(collective_id=0, has_side_effects=True),
    )(block)


def reduce_kernel(n, part_ref, prior_ref, cross_out, prior_out, crossing_out,
                  recv_part, cross_slots, prior_slots, sems):
    me = lax.axis_index("gr")
    col = lax.axis_index("gc")
    rows = prior_ref.shape[0]
    wide = cross_out.shape[2]

    barrier = pltpu.get_barrier_semaphore()

    def greet(k, carry):
        peer = lax.rem(me + k, n)
        pl.semaphore_signal(barrier, inc=1, device_id=(peer, col), device_id_type=MESH_ID)
        return carry

    lax.fori_loop(1, n, greet, 0)
    pl.semaphore_wait(barrier, n - 1)

    def prior_copy(k, sender):
        return pltpu.make_async_remote_copy(
            src_ref=prior_ref,
            dst_ref=prior_slots.at[sender],
            send_sem=sems.at[0, k],
            recv_sem=sems.at[1, sender],
            device_id=(lax.rem(me + k, n), col),
            device_id_type=MESH_ID,
        )

    def part_copy(k, sender):
        peer = lax.rem(me + k, n)
        return pltpu.make_async_remote_copy(
            src_ref=part_ref.at[pl.ds(pl.multiple_of(peer * rows, rows), rows), :],
            dst_ref=recv_part.at[sender],
            send_sem=sems.at[2, k],
            recv_sem=sems.at[3, sender],
            device_id=(peer, col),
            device_id_type=MESH_ID,
        )

    def cross_copy(k, sender):
        return pltpu.make_async_remote_copy(
            src_ref=cross_slots.at[me],
            dst_ref=cross_slots.at[sender],
            send_sem=sems.at[4, k],
            recv_sem=sems.at[5, sender],
            device_id=(lax.rem(me + k, n), col),
            device_id_type=MESH_ID,
        )

    def send_first(k, carry):
        prior_copy(k, me).start()
        part_copy(k, me).start()
        return carry

    lax.fori_loop(1, n, send_first, 0)
    prior_slots[me] = prior_ref[...]

    acc = part_ref[pl.ds(pl.multiple_of(me * rows, rows), rows), :].astype(jnp.float32)

    def add(k, total):
        sender = lax.rem(me + n - k, n)
        part_copy(k, me).wait_send()
        part_copy(k, sender).wait_recv()
        return total + recv_part[sender].astype(jnp.float32)

    acc = lax.fori_loop(1, n, add, acc)
    crossing_out[...] = acc[:, wide:]
    cross_slots[me] = acc[:, :wide].astype(cross_slots.dtype)

    def send_second(k, carry):
        cross_copy(k, me).start()
        return carry

    lax.fori_loop(1, n, send_second, 0)

    def wait_second(k, carry):
        sender = lax.rem(me + n - k, n)
        cross_copy(k, me).wait_send()
        cross_copy(k, sender).wait_recv()
        prior_copy(k, me).wait_send()
        prior_copy(k, sender).wait_recv()
        return carry

    lax.fori_loop(1, n, wait_second, 0)
    cross_out[...] = cross_slots[...]
    prior_out[...] = prior_slots[...]


def reduce_gr(part, prior_rows, n):
    rows, cols = prior_rows.shape
    wide = part.shape[1] - cols
    vmem = pl.BlockSpec(memory_space=pltpu.VMEM)
    return pl.pallas_call(
        functools.partial(reduce_kernel, n),
        out_shape=(
            jax.ShapeDtypeStruct((n, rows, wide), part.dtype),
            jax.ShapeDtypeStruct((n, rows, cols), prior_rows.dtype),
            jax.ShapeDtypeStruct((rows, cols), jnp.float32),
        ),
        in_specs=[vmem, vmem],
        out_specs=(vmem, vmem, vmem),
        scratch_shapes=[
            pltpu.VMEM((n, rows, part.shape[1]), part.dtype),
            pltpu.VMEM((n, rows, wide), part.dtype),
            pltpu.VMEM((n, rows, cols), prior_rows.dtype),
            pltpu.SemaphoreType.DMA((6, n)),
        ],
        compiler_params=pltpu.CompilerParams(collective_id=1, has_side_effects=True),
    )(part, prior_rows)


def local(
    n_gc,
    n_gr,
    line,
    below_factor,
    panel_factor,
    prior_factor,
    diag_factor,
    diag_inverse,
    below_adjoint,
    panel_adjoint,
    prior_adjoint,
    diag_adjoint,
):
    tile_count = below_factor.shape[0]
    tile_rows = below_factor.shape[2]
    local_rows = tile_count * tile_rows
    local_cols = below_factor.shape[3] * below_factor.shape[5]
    own_rows = panel_factor.shape[2]
    width = panel_factor.shape[3]
    prior_local = prior_factor.shape[0]
    below_mat = below_factor.reshape(local_rows, local_cols)
    below_bar = below_adjoint.reshape(local_rows, local_cols)
    inverse_bf = diag_inverse.astype(jnp.bfloat16)
    own_grad = jnp.dot(
        panel_adjoint.reshape(tile_count * own_rows, width),
        inverse_bf,
        preferred_element_type=jnp.float32,
    ).astype(jnp.bfloat16)
    panel_grad = own_grad.reshape(panel_adjoint.shape)
    both = jnp.concatenate(
        [own_grad.reshape(tile_count, own_rows, width), panel_factor.reshape(tile_count, own_rows, width)],
        axis=2,
    )
    whole = gather_gc(both, n_gc, line)
    grad_rows = whole[:, :, :width].reshape(local_rows, width)
    whole_factor = whole[:, :, width:].reshape(local_rows, width)
    prior_here = prior_factor.reshape(prior_local, local_cols)
    part = jnp.concatenate(
        [row_product(grad_rows, whole_factor), row_product(grad_rows, below_mat)], axis=1
    ).astype(jnp.bfloat16)
    cross_rows, prior_rows, crossing = reduce_gr(part, prior_here, n_gr)
    summed = cross_rows.reshape(width, width).astype(jnp.float32)
    prior_whole = prior_rows.reshape(width, local_cols)
    diag_reduced = jnp.tril(diag_adjoint - summed)
    diag_gradient = diag_solve(diag_factor, diag_inverse, diag_reduced)
    below_new = (
        below_bar.astype(jnp.float32)
        - jnp.dot(grad_rows, prior_whole, preferred_element_type=jnp.float32)
    ).astype(jnp.bfloat16)
    grid_row = lax.axis_index("gr")
    twice_rows = lax.dynamic_slice_in_dim(
        2.0 * diag_gradient, grid_row * prior_local, prior_local, 0
    ).astype(jnp.bfloat16)
    curvature = jnp.dot(twice_rows, prior_whole, preferred_element_type=jnp.float32)
    prior_bar = prior_adjoint.reshape(prior_local, local_cols).astype(jnp.float32)
    prior_new = (prior_bar - crossing - curvature).astype(jnp.bfloat16)
    return (
        below_new.reshape(below_adjoint.shape),
        panel_grad,
        prior_new.reshape(prior_adjoint.shape),
        diag_gradient,
    )


def line_length(mesh):
    column = list(mesh.devices[0])
    coords = [getattr(d, "coords", None) for d in column]
    if any(c is None for c in coords):
        return 8 if len(column) % 8 == 0 else len(column)
    first = coords[0][0]
    count = 0
    for c in coords:
        if c[0] != first:
            break
        count += 1
    return count if len(column) % count == 0 else len(column)


def solution(mesh):
    in_specs = (
        P(None, "gr", None, None, "gc", None),
        P(None, "gr", "gc", None),
        P("gr", None, "gc", None),
        P(),
        P(),
        P(None, "gr", None, None, "gc", None),
        P(None, "gr", "gc", None),
        P("gr", None, "gc", None),
        P(),
    )
    out_specs = (
        P(None, "gr", None, None, "gc", None),
        P(None, "gr", "gc", None),
        P("gr", None, "gc", None),
        P(),
    )
    return jax.shard_map(
        functools.partial(local, mesh.shape["gc"], mesh.shape["gr"], line_length(mesh)),
        mesh=mesh,
        in_specs=in_specs,
        out_specs=out_specs,
        check_vma=False,
    )
```

```python
import functools

import jax
import jax.numpy as jnp
from jax import lax
from jax.experimental import pallas as pl
from jax.experimental.pallas import tpu as pltpu
from jax.sharding import PartitionSpec as P

MESH_ID = pl.DeviceIdType.MESH


def row_product(left_rows, right_rows):
    return lax.dot_general(
        left_rows, right_rows, (((0,), (0,)), ((), ())), preferred_element_type=jnp.float32
    )


def diag_solve(diag_factor, diag_inverse, diag_reduced):
    highest = lax.Precision.HIGHEST
    chol_proj = jnp.dot(diag_factor.T, diag_reduced, precision=highest)
    phi_lower = jnp.tril(chol_proj) - 0.5 * jnp.diag(jnp.diagonal(chol_proj))
    symmetric = 0.5 * (phi_lower + phi_lower.T)
    left_side = jnp.dot(diag_inverse.T, symmetric, precision=highest)
    return jnp.dot(left_side, diag_inverse, precision=highest)


def gather_kernel(n, line, x_ref, out_ref, sems, local_sem):
    me = lax.axis_index("gc")
    row = lax.axis_index("gr")
    rows = x_ref.shape[1]
    lines = n // line
    pos = lax.rem(me, line)
    grp = me // line
    base = grp * line

    def line_peer(k):
        return base + lax.rem(pos + k, line)

    def cross_peer(k):
        return lax.rem(grp + k, lines) * line + pos

    barrier = pltpu.get_barrier_semaphore()

    def greet_line(k, carry):
        pl.semaphore_signal(barrier, inc=1, device_id=(row, line_peer(k)), device_id_type=MESH_ID)
        return carry

    def greet_cross(k, carry):
        pl.semaphore_signal(barrier, inc=1, device_id=(row, cross_peer(k)), device_id_type=MESH_ID)
        return carry

    lax.fori_loop(1, line, greet_line, 0)
    lax.fori_loop(1, lines, greet_cross, 0)
    pl.semaphore_wait(barrier, line + lines - 2)

    own = pltpu.make_async_copy(x_ref, out_ref.at[:, pl.ds(me * rows, rows), :], local_sem)
    own.start()

    def first(k, sender_pos):
        return pltpu.make_async_remote_copy(
            src_ref=x_ref,
            dst_ref=out_ref.at[:, pl.ds((base + sender_pos) * rows, rows), :],
            send_sem=sems.at[0, k],
            recv_sem=sems.at[1, sender_pos],
            device_id=(row, line_peer(k)),
            device_id_type=MESH_ID,
        )

    def send_first(k, carry):
        first(k, pos).start()
        return carry

    lax.fori_loop(1, line, send_first, 0)

    span = line * rows

    def forward(k, block_pos, sender_grp):
        slot = pl.ds((grp * line + block_pos) * rows, rows)
        return pltpu.make_async_remote_copy(
            src_ref=out_ref.at[:, slot, :],
            dst_ref=out_ref.at[:, slot, :],
            send_sem=sems.at[2 + block_pos, k],
            recv_sem=sems.at[1, line + sender_grp],
            device_id=(row, cross_peer(k)),
            device_id_type=MESH_ID,
        )

    def whole_line(sender_grp):
        return pltpu.make_async_remote_copy(
            src_ref=out_ref.at[:, pl.ds(sender_grp * span, span), :],
            dst_ref=out_ref.at[:, pl.ds(sender_grp * span, span), :],
            send_sem=sems.at[0, 0],
            recv_sem=sems.at[1, line + sender_grp],
            device_id=(row, cross_peer(1)),
            device_id_type=MESH_ID,
        )

    own.wait()

    def send_own(k, carry):
        forward(k, pos, grp).start()
        return carry

    lax.fori_loop(1, lines, send_own, 0)

    def relay(k, carry):
        sender_pos = lax.rem(pos + line - k, line)
        first(k, sender_pos).wait_recv()

        def out(j, inner):
            forward(j, sender_pos, grp).start()
            return inner

        return lax.fori_loop(1, lines, out, carry)

    lax.fori_loop(1, line, relay, 0)

    def wait_first(k, carry):
        first(k, pos).wait_send()
        return carry

    lax.fori_loop(1, line, wait_first, 0)

    def wait_sent(k, carry):
        def done(j, inner):
            forward(j, k, grp).wait_send()
            return inner

        return lax.fori_loop(1, lines, done, carry)

    lax.fori_loop(0, line, wait_sent, 0)

    def wait_lines(k, carry):
        whole_line(lax.rem(grp + lines - k, lines)).wait_recv()
        return carry

    lax.fori_loop(1, lines, wait_lines, 0)


def gather_gc(block, n, line):
    tiles, rows, width = block.shape
    return pl.pallas_call(
        functools.partial(gather_kernel, n, line),
        out_shape=jax.ShapeDtypeStruct((tiles, rows * n, width), block.dtype),
        in_specs=[pl.BlockSpec(memory_space=pl.ANY)],
        out_specs=pl.BlockSpec(memory_space=pl.ANY),
        scratch_shapes=[
            pltpu.SemaphoreType.DMA((2 + line, line + n // line)),
            pltpu.SemaphoreType.DMA,
        ],
        compiler_params=pltpu.CompilerParams(collective_id=0, has_side_effects=True),
    )(block)


def reduce_kernel(n, part_ref, prior_ref, cross_out, prior_out, crossing_out,
                  recv_part, cross_slots, prior_slots, sems):
    me = lax.axis_index("gr")
    col = lax.axis_index("gc")
    rows = prior_ref.shape[0]
    wide = cross_out.shape[2]

    barrier = pltpu.get_barrier_semaphore()

    def greet(k, carry):
        peer = lax.rem(me + k, n)
        pl.semaphore_signal(barrier, inc=1, device_id=(peer, col), device_id_type=MESH_ID)
        return carry

    lax.fori_loop(1, n, greet, 0)
    pl.semaphore_wait(barrier, n - 1)

    def prior_copy(k, sender):
        return pltpu.make_async_remote_copy(
            src_ref=prior_ref,
            dst_ref=prior_slots.at[sender],
            send_sem=sems.at[0, k],
            recv_sem=sems.at[1, sender],
            device_id=(lax.rem(me + k, n), col),
            device_id_type=MESH_ID,
        )

    def part_copy(k, sender):
        peer = lax.rem(me + k, n)
        return pltpu.make_async_remote_copy(
            src_ref=part_ref.at[pl.ds(pl.multiple_of(peer * rows, rows), rows), :],
            dst_ref=recv_part.at[sender],
            send_sem=sems.at[2, k],
            recv_sem=sems.at[3, sender],
            device_id=(peer, col),
            device_id_type=MESH_ID,
        )

    def cross_copy(k, sender):
        return pltpu.make_async_remote_copy(
            src_ref=cross_slots.at[me],
            dst_ref=cross_slots.at[sender],
            send_sem=sems.at[4, k],
            recv_sem=sems.at[5, sender],
            device_id=(lax.rem(me + k, n), col),
            device_id_type=MESH_ID,
        )

    def send_first(k, carry):
        prior_copy(k, me).start()
        part_copy(k, me).start()
        return carry

    lax.fori_loop(1, n, send_first, 0)
    prior_slots[me] = prior_ref[...]

    acc = part_ref[pl.ds(pl.multiple_of(me * rows, rows), rows), :].astype(jnp.float32)

    def add(k, total):
        sender = lax.rem(me + n - k, n)
        part_copy(k, me).wait_send()
        part_copy(k, sender).wait_recv()
        return total + recv_part[sender].astype(jnp.float32)

    acc = lax.fori_loop(1, n, add, acc)
    crossing_out[...] = acc[:, wide:]
    cross_slots[me] = acc[:, :wide].astype(cross_slots.dtype)

    def send_second(k, carry):
        cross_copy(k, me).start()
        return carry

    lax.fori_loop(1, n, send_second, 0)

    def wait_second(k, carry):
        sender = lax.rem(me + n - k, n)
        cross_copy(k, me).wait_send()
        cross_copy(k, sender).wait_recv()
        prior_copy(k, me).wait_send()
        prior_copy(k, sender).wait_recv()
        return carry

    lax.fori_loop(1, n, wait_second, 0)
    cross_out[...] = cross_slots[...]
    prior_out[...] = prior_slots[...]


def reduce_gr(part, prior_rows, n):
    rows, cols = prior_rows.shape
    wide = part.shape[1] - cols
    vmem = pl.BlockSpec(memory_space=pltpu.VMEM)
    return pl.pallas_call(
        functools.partial(reduce_kernel, n),
        out_shape=(
            jax.ShapeDtypeStruct((n, rows, wide), part.dtype),
            jax.ShapeDtypeStruct((n, rows, cols), prior_rows.dtype),
            jax.ShapeDtypeStruct((rows, cols), jnp.float32),
        ),
        in_specs=[vmem, vmem],
        out_specs=(vmem, vmem, vmem),
        scratch_shapes=[
            pltpu.VMEM((n, rows, part.shape[1]), part.dtype),
            pltpu.VMEM((n, rows, wide), part.dtype),
            pltpu.VMEM((n, rows, cols), prior_rows.dtype),
            pltpu.SemaphoreType.DMA((6, n)),
        ],
        compiler_params=pltpu.CompilerParams(collective_id=1, has_side_effects=True),
    )(part, prior_rows)


def local(
    n_gc,
    n_gr,
    line,
    below_factor,
    panel_factor,
    prior_factor,
    diag_factor,
    diag_inverse,
    below_adjoint,
    panel_adjoint,
    prior_adjoint,
    diag_adjoint,
):
    tile_count = below_factor.shape[0]
    tile_rows = below_factor.shape[2]
    local_rows = tile_count * tile_rows
    local_cols = below_factor.shape[3] * below_factor.shape[5]
    own_rows = panel_factor.shape[2]
    width = panel_factor.shape[3]
    prior_local = prior_factor.shape[0]
    below_mat = below_factor.reshape(local_rows, local_cols)
    below_bar = below_adjoint.reshape(local_rows, local_cols)
    inverse_bf = diag_inverse.astype(jnp.bfloat16)
    own_grad = jnp.dot(
        panel_adjoint.reshape(tile_count * own_rows, width),
        inverse_bf,
        preferred_element_type=jnp.float32,
    ).astype(jnp.bfloat16)
    panel_grad = own_grad.reshape(panel_adjoint.shape)
    both = jnp.concatenate(
        [own_grad.reshape(tile_count, own_rows, width), panel_factor.reshape(tile_count, own_rows, width)],
        axis=2,
    )
    whole = gather_gc(both, n_gc, line)
    grad_rows = whole[:, :, :width].reshape(local_rows, width)
    whole_factor = whole[:, :, width:].reshape(local_rows, width)
    prior_here = prior_factor.reshape(prior_local, local_cols)
    part = jnp.concatenate(
        [row_product(grad_rows, whole_factor), row_product(grad_rows, below_mat)], axis=1
    ).astype(jnp.bfloat16)
    cross_rows, prior_rows, crossing = reduce_gr(part, prior_here, n_gr)
    summed = cross_rows.reshape(width, width).astype(jnp.float32)
    prior_whole = prior_rows.reshape(width, local_cols)
    diag_reduced = jnp.tril(diag_adjoint - summed)
    diag_gradient = diag_solve(diag_factor, diag_inverse, diag_reduced)
    below_new = (
        below_bar.astype(jnp.float32)
        - jnp.dot(grad_rows, prior_whole, preferred_element_type=jnp.float32)
    ).astype(jnp.bfloat16)
    grid_row = lax.axis_index("gr")
    twice_rows = lax.dynamic_slice_in_dim(
        2.0 * diag_gradient, grid_row * prior_local, prior_local, 0
    ).astype(jnp.bfloat16)
    curvature = jnp.dot(twice_rows, prior_whole, preferred_element_type=jnp.float32)
    prior_bar = prior_adjoint.reshape(prior_local, local_cols).astype(jnp.float32)
    prior_new = (prior_bar - crossing - curvature).astype(jnp.bfloat16)
    return (
        below_new.reshape(below_adjoint.shape),
        panel_grad,
        prior_new.reshape(prior_adjoint.shape),
        diag_gradient,
    )


def line_length(mesh):
    column = list(mesh.devices[0])
    coords = [getattr(d, "coords", None) for d in column]
    if any(c is None for c in coords):
        return 8 if len(column) % 8 == 0 else len(column)
    first = coords[0][0]
    count = 0
    for c in coords:
        if c[0] != first:
            break
        count += 1
    return count if len(column) % count == 0 else len(column)


def solution(mesh):
    in_specs = (
        P(None, "gr", None, None, "gc", None),
        P(None, "gr", "gc", None),
        P("gr", None, "gc", None),
        P(),
        P(),
        P(None, "gr", None, None, "gc", None),
        P(None, "gr", "gc", None),
        P("gr", None, "gc", None),
        P(),
    )
    out_specs = (
        P(None, "gr", None, None, "gc", None),
        P(None, "gr", "gc", None),
        P("gr", None, "gc", None),
        P(),
    )
    return jax.shard_map(
        functools.partial(local, mesh.shape["gc"], mesh.shape["gr"], line_length(mesh)),
        mesh=mesh,
        in_specs=in_specs,
        out_specs=out_specs,
        check_vma=False,
    )
```

```python
import functools

import jax
import jax.numpy as jnp
from jax import lax
from jax.experimental import pallas as pl
from jax.experimental.pallas import tpu as pltpu
from jax.sharding import PartitionSpec as P

MESH_ID = pl.DeviceIdType.MESH


def row_product(left_rows, right_rows):
    return lax.dot_general(
        left_rows, right_rows, (((0,), (0,)), ((), ())), preferred_element_type=jnp.float32
    )


def diag_solve(diag_factor, diag_inverse, diag_reduced):
    highest = lax.Precision.HIGHEST
    chol_proj = jnp.dot(diag_factor.T, diag_reduced, precision=highest)
    index_row = lax.broadcasted_iota(jnp.int32, chol_proj.shape, 0)
    index_col = lax.broadcasted_iota(jnp.int32, chol_proj.shape, 1)
    phi_lower = jnp.where(
        index_row > index_col,
        chol_proj,
        jnp.where(index_row == index_col, chol_proj - 0.5 * chol_proj, 0.0),
    )
    symmetric = 0.5 * (phi_lower + phi_lower.T)
    left_side = jnp.dot(diag_inverse.T, symmetric, precision=highest)
    return jnp.dot(left_side, diag_inverse, precision=highest)


def gather_kernel(n, line, x_ref, out_ref, sems, local_sem):
    me = lax.axis_index("gc")
    row = lax.axis_index("gr")
    rows = x_ref.shape[1]
    lines = n // line
    pos = lax.rem(me, line)
    grp = me // line
    base = grp * line

    def line_peer(k):
        return base + lax.rem(pos + k, line)

    def cross_peer(k):
        return lax.rem(grp + k, lines) * line + pos

    barrier = pltpu.get_barrier_semaphore()

    def greet_line(k, carry):
        pl.semaphore_signal(barrier, inc=1, device_id=(row, line_peer(k)), device_id_type=MESH_ID)
        return carry

    def greet_cross(k, carry):
        pl.semaphore_signal(barrier, inc=1, device_id=(row, cross_peer(k)), device_id_type=MESH_ID)
        return carry

    lax.fori_loop(1, line, greet_line, 0)
    lax.fori_loop(1, lines, greet_cross, 0)
    pl.semaphore_wait(barrier, line + lines - 2)

    own = pltpu.make_async_copy(x_ref, out_ref.at[:, pl.ds(me * rows, rows), :], local_sem)
    own.start()

    def first(k, sender_pos):
        return pltpu.make_async_remote_copy(
            src_ref=x_ref,
            dst_ref=out_ref.at[:, pl.ds((base + sender_pos) * rows, rows), :],
            send_sem=sems.at[0, k],
            recv_sem=sems.at[1, sender_pos],
            device_id=(row, line_peer(k)),
            device_id_type=MESH_ID,
        )

    def send_first(k, carry):
        first(k, pos).start()
        return carry

    lax.fori_loop(1, line, send_first, 0)

    span = line * rows

    def forward(k, block_pos, sender_grp):
        slot = pl.ds((grp * line + block_pos) * rows, rows)
        return pltpu.make_async_remote_copy(
            src_ref=out_ref.at[:, slot, :],
            dst_ref=out_ref.at[:, slot, :],
            send_sem=sems.at[2 + block_pos, k],
            recv_sem=sems.at[1, line + sender_grp],
            device_id=(row, cross_peer(k)),
            device_id_type=MESH_ID,
        )

    def whole_line(sender_grp):
        return pltpu.make_async_remote_copy(
            src_ref=out_ref.at[:, pl.ds(sender_grp * span, span), :],
            dst_ref=out_ref.at[:, pl.ds(sender_grp * span, span), :],
            send_sem=sems.at[0, 0],
            recv_sem=sems.at[1, line + sender_grp],
            device_id=(row, cross_peer(1)),
            device_id_type=MESH_ID,
        )

    own.wait()

    def send_own(k, carry):
        forward(k, pos, grp).start()
        return carry

    lax.fori_loop(1, lines, send_own, 0)

    def relay(k, carry):
        sender_pos = lax.rem(pos + line - k, line)
        first(k, sender_pos).wait_recv()

        def out(j, inner):
            forward(j, sender_pos, grp).start()
            return inner

        return lax.fori_loop(1, lines, out, carry)

    lax.fori_loop(1, line, relay, 0)

    def wait_first(k, carry):
        first(k, pos).wait_send()
        return carry

    lax.fori_loop(1, line, wait_first, 0)

    def wait_sent(k, carry):
        def done(j, inner):
            forward(j, k, grp).wait_send()
            return inner

        return lax.fori_loop(1, lines, done, carry)

    lax.fori_loop(0, line, wait_sent, 0)

    def wait_lines(k, carry):
        whole_line(lax.rem(grp + lines - k, lines)).wait_recv()
        return carry

    lax.fori_loop(1, lines, wait_lines, 0)


def gather_gc(block, n, line):
    tiles, rows, width = block.shape
    return pl.pallas_call(
        functools.partial(gather_kernel, n, line),
        out_shape=jax.ShapeDtypeStruct((tiles, rows * n, width), block.dtype),
        in_specs=[pl.BlockSpec(memory_space=pl.ANY)],
        out_specs=pl.BlockSpec(memory_space=pl.ANY),
        scratch_shapes=[
            pltpu.SemaphoreType.DMA((2 + line, line + n // line)),
            pltpu.SemaphoreType.DMA,
        ],
        compiler_params=pltpu.CompilerParams(collective_id=0, has_side_effects=True),
    )(block)


def reduce_kernel(n, part_ref, prior_ref, cross_out, prior_out, crossing_out,
                  recv_part, cross_slots, prior_slots, sems):
    me = lax.axis_index("gr")
    col = lax.axis_index("gc")
    rows = prior_ref.shape[0]
    wide = cross_out.shape[2]

    barrier = pltpu.get_barrier_semaphore()

    def greet(k, carry):
        peer = lax.rem(me + k, n)
        pl.semaphore_signal(barrier, inc=1, device_id=(peer, col), device_id_type=MESH_ID)
        return carry

    lax.fori_loop(1, n, greet, 0)
    pl.semaphore_wait(barrier, n - 1)

    def prior_copy(k, sender):
        return pltpu.make_async_remote_copy(
            src_ref=prior_ref,
            dst_ref=prior_slots.at[sender],
            send_sem=sems.at[0, k],
            recv_sem=sems.at[1, sender],
            device_id=(lax.rem(me + k, n), col),
            device_id_type=MESH_ID,
        )

    def part_copy(k, sender):
        peer = lax.rem(me + k, n)
        return pltpu.make_async_remote_copy(
            src_ref=part_ref.at[pl.ds(pl.multiple_of(peer * rows, rows), rows), :],
            dst_ref=recv_part.at[sender],
            send_sem=sems.at[2, k],
            recv_sem=sems.at[3, sender],
            device_id=(peer, col),
            device_id_type=MESH_ID,
        )

    def cross_copy(k, sender):
        return pltpu.make_async_remote_copy(
            src_ref=cross_slots.at[me],
            dst_ref=cross_slots.at[sender],
            send_sem=sems.at[4, k],
            recv_sem=sems.at[5, sender],
            device_id=(lax.rem(me + k, n), col),
            device_id_type=MESH_ID,
        )

    def send_first(k, carry):
        prior_copy(k, me).start()
        part_copy(k, me).start()
        return carry

    lax.fori_loop(1, n, send_first, 0)
    prior_slots[me] = prior_ref[...]

    acc = part_ref[pl.ds(pl.multiple_of(me * rows, rows), rows), :].astype(jnp.float32)

    def add(k, total):
        sender = lax.rem(me + n - k, n)
        part_copy(k, me).wait_send()
        part_copy(k, sender).wait_recv()
        return total + recv_part[sender].astype(jnp.float32)

    acc = lax.fori_loop(1, n, add, acc)
    crossing_out[...] = acc[:, wide:]
    cross_slots[me] = acc[:, :wide].astype(cross_slots.dtype)

    def send_second(k, carry):
        cross_copy(k, me).start()
        return carry

    lax.fori_loop(1, n, send_second, 0)

    def wait_second(k, carry):
        sender = lax.rem(me + n - k, n)
        cross_copy(k, me).wait_send()
        cross_copy(k, sender).wait_recv()
        prior_copy(k, me).wait_send()
        prior_copy(k, sender).wait_recv()
        return carry

    lax.fori_loop(1, n, wait_second, 0)
    cross_out[...] = cross_slots[...]
    prior_out[...] = prior_slots[...]


def reduce_gr(part, prior_rows, n):
    rows, cols = prior_rows.shape
    wide = part.shape[1] - cols
    vmem = pl.BlockSpec(memory_space=pltpu.VMEM)
    return pl.pallas_call(
        functools.partial(reduce_kernel, n),
        out_shape=(
            jax.ShapeDtypeStruct((n, rows, wide), part.dtype),
            jax.ShapeDtypeStruct((n, rows, cols), prior_rows.dtype),
            jax.ShapeDtypeStruct((rows, cols), jnp.float32),
        ),
        in_specs=[vmem, vmem],
        out_specs=(vmem, vmem, vmem),
        scratch_shapes=[
            pltpu.VMEM((n, rows, part.shape[1]), part.dtype),
            pltpu.VMEM((n, rows, wide), part.dtype),
            pltpu.VMEM((n, rows, cols), prior_rows.dtype),
            pltpu.SemaphoreType.DMA((6, n)),
        ],
        compiler_params=pltpu.CompilerParams(collective_id=1, has_side_effects=True),
    )(part, prior_rows)


def prior_factor_rows(prior_rows, below_shape):
    return prior_rows.reshape(-1, below_shape[3], below_shape[5])


def local(
    n_gc,
    n_gr,
    line,
    below_factor,
    panel_factor,
    prior_factor,
    diag_factor,
    diag_inverse,
    below_adjoint,
    panel_adjoint,
    prior_adjoint,
    diag_adjoint,
):
    tile_count = below_factor.shape[0]
    tile_rows = below_factor.shape[2]
    local_rows = tile_count * tile_rows
    local_cols = below_factor.shape[3] * below_factor.shape[5]
    own_rows = panel_factor.shape[2]
    width = panel_factor.shape[3]
    prior_local = prior_factor.shape[0]
    below_mat = below_factor.reshape(local_rows, local_cols)
    below_bar = below_adjoint.reshape(local_rows, local_cols)
    inverse_bf = diag_inverse.astype(jnp.bfloat16)
    own_grad = jnp.dot(
        panel_adjoint.reshape(tile_count * own_rows, width),
        inverse_bf,
        preferred_element_type=jnp.float32,
    ).astype(jnp.bfloat16)
    panel_grad = own_grad.reshape(panel_adjoint.shape)
    both = jnp.concatenate(
        [own_grad.reshape(tile_count, own_rows, width), panel_factor.reshape(tile_count, own_rows, width)],
        axis=2,
    )
    whole = gather_gc(both, n_gc, line)
    grad_rows = whole[:, :, :width].reshape(local_rows, width)
    whole_factor = whole[:, :, width:].reshape(local_rows, width)
    prior_here = prior_factor.reshape(prior_local, local_cols)
    part = jnp.concatenate(
        [row_product(grad_rows, whole_factor), row_product(grad_rows, below_mat)], axis=1
    ).astype(jnp.bfloat16)
    cross_rows, prior_rows, crossing = reduce_gr(part, prior_here, n_gr)
    summed = cross_rows.reshape(width, width).astype(jnp.float32)
    prior_whole = prior_rows.reshape(width, local_cols)
    diag_reduced = jnp.tril(diag_adjoint - summed)
    diag_gradient = diag_solve(diag_factor, diag_inverse, diag_reduced)
    below_prod = lax.dot_general(
        grad_rows.reshape(tile_count, tile_rows, width),
        prior_factor_rows(prior_rows, below_factor.shape),
        (((2,), (0,)), ((), ())),
        preferred_element_type=jnp.float32,
    ).reshape(below_adjoint.shape)
    below_new = (below_adjoint.astype(jnp.float32) - below_prod).astype(jnp.bfloat16)
    grid_row = lax.axis_index("gr")
    twice_rows = lax.dynamic_slice_in_dim(
        2.0 * diag_gradient, grid_row * prior_local, prior_local, 0
    ).astype(jnp.bfloat16)
    curvature = jnp.dot(twice_rows, prior_whole, preferred_element_type=jnp.float32)
    prior_bar = prior_adjoint.reshape(prior_local, local_cols).astype(jnp.float32)
    prior_new = (prior_bar - crossing - curvature).astype(jnp.bfloat16)
    return (
        below_new,
        panel_grad,
        prior_new.reshape(prior_adjoint.shape),
        diag_gradient,
    )


def line_length(mesh):
    column = list(mesh.devices[0])
    coords = [getattr(d, "coords", None) for d in column]
    if any(c is None for c in coords):
        return 8 if len(column) % 8 == 0 else len(column)
    first = coords[0][0]
    count = 0
    for c in coords:
        if c[0] != first:
            break
        count += 1
    return count if len(column) % count == 0 else len(column)


def solution(mesh):
    in_specs = (
        P(None, "gr", None, None, "gc", None),
        P(None, "gr", "gc", None),
        P("gr", None, "gc", None),
        P(),
        P(),
        P(None, "gr", None, None, "gc", None),
        P(None, "gr", "gc", None),
        P("gr", None, "gc", None),
        P(),
    )
    out_specs = (
        P(None, "gr", None, None, "gc", None),
        P(None, "gr", "gc", None),
        P("gr", None, "gc", None),
        P(),
    )
    return jax.shard_map(
        functools.partial(local, mesh.shape["gc"], mesh.shape["gr"], line_length(mesh)),
        mesh=mesh,
        in_specs=in_specs,
        out_specs=out_specs,
        check_vma=False,
    )
```

```python
import functools

import jax
import jax.numpy as jnp
from jax import lax
from jax.experimental import pallas as pl
from jax.experimental.pallas import tpu as pltpu
from jax.sharding import PartitionSpec as P

MESH_ID = pl.DeviceIdType.MESH


def row_product(left_rows, right_rows):
    return lax.dot_general(
        left_rows, right_rows, (((0,), (0,)), ((), ())), preferred_element_type=jnp.float32
    )


def diag_solve(diag_factor, diag_inverse, diag_reduced):
    highest = lax.Precision.HIGHEST
    chol_proj = jnp.dot(diag_factor.T, diag_reduced, precision=highest)
    index_row = lax.broadcasted_iota(jnp.int32, chol_proj.shape, 0)
    index_col = lax.broadcasted_iota(jnp.int32, chol_proj.shape, 1)
    phi_lower = jnp.where(
        index_row > index_col,
        chol_proj,
        jnp.where(index_row == index_col, chol_proj - 0.5 * chol_proj, 0.0),
    )
    symmetric = 0.5 * (phi_lower + phi_lower.T)
    left_side = jnp.dot(diag_inverse.T, symmetric, precision=highest)
    return jnp.dot(left_side, diag_inverse, precision=highest)


def gather_kernel(n, line, x_ref, out_ref, s1, fsend, lrecv, brecv, rsend, local_sem):
    me = lax.axis_index("gc")
    row = lax.axis_index("gr")
    rows = x_ref.shape[1]
    lines = n // line
    relay = lines == 4
    direct = (1, lines - 1) if relay else tuple(range(1, lines))
    pos = lax.rem(me, line)
    grp = me // line
    base = grp * line
    span = line * rows

    def line_peer(k):
        return base + lax.rem(pos + k, line)

    def cross_peer(k):
        return lax.rem(grp + k, lines) * line + pos

    barrier = pltpu.get_barrier_semaphore()

    def greet_line(k, carry):
        pl.semaphore_signal(barrier, inc=1, device_id=(row, line_peer(k)), device_id_type=MESH_ID)
        return carry

    lax.fori_loop(1, line, greet_line, 0)
    for k in direct:
        pl.semaphore_signal(barrier, inc=1, device_id=(row, cross_peer(k)), device_id_type=MESH_ID)
    pl.semaphore_wait(barrier, line - 1 + len(direct))

    own = pltpu.make_async_copy(x_ref, out_ref.at[:, pl.ds(me * rows, rows), :], local_sem)
    own.start()

    def first(k, sender_pos):
        return pltpu.make_async_remote_copy(
            src_ref=x_ref,
            dst_ref=out_ref.at[:, pl.ds((base + sender_pos) * rows, rows), :],
            send_sem=s1.at[0, k],
            recv_sem=s1.at[1, sender_pos],
            device_id=(row, line_peer(k)),
            device_id_type=MESH_ID,
        )

    def send_first(k, carry):
        first(k, pos).start()
        return carry

    lax.fori_loop(1, line, send_first, 0)

    def block(slot_line, block_pos):
        return out_ref.at[:, pl.ds((slot_line * line + block_pos) * rows, rows), :]

    def forward(k, block_pos):
        recv = brecv.at[block_pos] if (relay and k == 1) else lrecv.at[grp]
        return pltpu.make_async_remote_copy(
            src_ref=block(grp, block_pos),
            dst_ref=block(grp, block_pos),
            send_sem=fsend.at[block_pos, k],
            recv_sem=recv,
            device_id=(row, cross_peer(k)),
            device_id_type=MESH_ID,
        )

    def from_previous(block_pos):
        prev = lax.rem(grp + lines - 1, lines)
        return pltpu.make_async_remote_copy(
            src_ref=block(prev, block_pos),
            dst_ref=block(prev, block_pos),
            send_sem=rsend.at[block_pos],
            recv_sem=lrecv.at[prev],
            device_id=(row, cross_peer(1)),
            device_id_type=MESH_ID,
        )

    def arrived(block_pos):
        prev = lax.rem(grp + lines - 1, lines)
        return pltpu.make_async_remote_copy(
            src_ref=block(prev, block_pos),
            dst_ref=block(prev, block_pos),
            send_sem=rsend.at[block_pos],
            recv_sem=brecv.at[block_pos],
            device_id=(row, cross_peer(1)),
            device_id_type=MESH_ID,
        )

    def whole_line(sender_grp):
        return pltpu.make_async_remote_copy(
            src_ref=out_ref.at[:, pl.ds(sender_grp * span, span), :],
            dst_ref=out_ref.at[:, pl.ds(sender_grp * span, span), :],
            send_sem=local_sem,
            recv_sem=lrecv.at[sender_grp],
            device_id=(row, cross_peer(1)),
            device_id_type=MESH_ID,
        )

    own.wait()
    for k in direct:
        forward(k, pos).start()

    def relay_line(k, carry):
        sender_pos = lax.rem(pos + line - k, line)
        first(k, sender_pos).wait_recv()
        for j in direct:
            forward(j, sender_pos).start()
        return carry

    lax.fori_loop(1, line, relay_line, 0)

    if relay:
        def relay_ring(k, carry):
            block_pos = lax.rem(pos + line - k, line)
            arrived(block_pos).wait_recv()
            from_previous(block_pos).start()
            return carry

        lax.fori_loop(0, line, relay_ring, 0)

    def wait_first(k, carry):
        first(k, pos).wait_send()
        return carry

    lax.fori_loop(1, line, wait_first, 0)

    def wait_sent(p, carry):
        for k in direct:
            forward(k, p).wait_send()
        if relay:
            from_previous(p).wait_send()
        return carry

    lax.fori_loop(0, line, wait_sent, 0)

    if relay:
        whole_line(lax.rem(grp + 1, lines)).wait_recv()
        whole_line(lax.rem(grp + 2, lines)).wait_recv()
    else:
        def wait_lines(k, carry):
            whole_line(lax.rem(grp + lines - k, lines)).wait_recv()
            return carry

        lax.fori_loop(1, lines, wait_lines, 0)


def gather_gc(block, n, line):
    tiles, rows, width = block.shape
    lines = n // line
    return pl.pallas_call(
        functools.partial(gather_kernel, n, line),
        out_shape=jax.ShapeDtypeStruct((tiles, rows * n, width), block.dtype),
        in_specs=[pl.BlockSpec(memory_space=pl.ANY)],
        out_specs=pl.BlockSpec(memory_space=pl.ANY),
        scratch_shapes=[
            pltpu.SemaphoreType.DMA((2, line)),
            pltpu.SemaphoreType.DMA((line, lines)),
            pltpu.SemaphoreType.DMA((lines,)),
            pltpu.SemaphoreType.DMA((line,)),
            pltpu.SemaphoreType.DMA((line,)),
            pltpu.SemaphoreType.DMA,
        ],
        compiler_params=pltpu.CompilerParams(collective_id=0, has_side_effects=True),
    )(block)


def reduce_kernel(n, part_ref, prior_ref, cross_out, prior_out, crossing_out,
                  recv_part, cross_slots, prior_slots, sems):
    me = lax.axis_index("gr")
    col = lax.axis_index("gc")
    rows = prior_ref.shape[0]
    wide = cross_out.shape[2]

    barrier = pltpu.get_barrier_semaphore()

    def greet(k, carry):
        peer = lax.rem(me + k, n)
        pl.semaphore_signal(barrier, inc=1, device_id=(peer, col), device_id_type=MESH_ID)
        return carry

    lax.fori_loop(1, n, greet, 0)
    pl.semaphore_wait(barrier, n - 1)

    def prior_copy(k, sender):
        return pltpu.make_async_remote_copy(
            src_ref=prior_ref,
            dst_ref=prior_slots.at[sender],
            send_sem=sems.at[0, k],
            recv_sem=sems.at[1, sender],
            device_id=(lax.rem(me + k, n), col),
            device_id_type=MESH_ID,
        )

    def part_copy(k, sender):
        peer = lax.rem(me + k, n)
        return pltpu.make_async_remote_copy(
            src_ref=part_ref.at[pl.ds(pl.multiple_of(peer * rows, rows), rows), :],
            dst_ref=recv_part.at[sender],
            send_sem=sems.at[2, k],
            recv_sem=sems.at[3, sender],
            device_id=(peer, col),
            device_id_type=MESH_ID,
        )

    def cross_copy(k, sender):
        return pltpu.make_async_remote_copy(
            src_ref=cross_slots.at[me],
            dst_ref=cross_slots.at[sender],
            send_sem=sems.at[4, k],
            recv_sem=sems.at[5, sender],
            device_id=(lax.rem(me + k, n), col),
            device_id_type=MESH_ID,
        )

    def send_first(k, carry):
        prior_copy(k, me).start()
        part_copy(k, me).start()
        return carry

    lax.fori_loop(1, n, send_first, 0)
    prior_slots[me] = prior_ref[...]

    acc = part_ref[pl.ds(pl.multiple_of(me * rows, rows), rows), :].astype(jnp.float32)

    def add(k, total):
        sender = lax.rem(me + n - k, n)
        part_copy(k, me).wait_send()
        part_copy(k, sender).wait_recv()
        return total + recv_part[sender].astype(jnp.float32)

    acc = lax.fori_loop(1, n, add, acc)
    crossing_out[...] = acc[:, wide:]
    cross_slots[me] = acc[:, :wide].astype(cross_slots.dtype)

    def send_second(k, carry):
        cross_copy(k, me).start()
        return carry

    lax.fori_loop(1, n, send_second, 0)

    def wait_second(k, carry):
        sender = lax.rem(me + n - k, n)
        cross_copy(k, me).wait_send()
        cross_copy(k, sender).wait_recv()
        prior_copy(k, me).wait_send()
        prior_copy(k, sender).wait_recv()
        return carry

    lax.fori_loop(1, n, wait_second, 0)
    cross_out[...] = cross_slots[...]
    prior_out[...] = prior_slots[...]


def reduce_gr(part, prior_rows, n):
    rows, cols = prior_rows.shape
    wide = part.shape[1] - cols
    vmem = pl.BlockSpec(memory_space=pltpu.VMEM)
    return pl.pallas_call(
        functools.partial(reduce_kernel, n),
        out_shape=(
            jax.ShapeDtypeStruct((n, rows, wide), part.dtype),
            jax.ShapeDtypeStruct((n, rows, cols), prior_rows.dtype),
            jax.ShapeDtypeStruct((rows, cols), jnp.float32),
        ),
        in_specs=[vmem, vmem],
        out_specs=(vmem, vmem, vmem),
        scratch_shapes=[
            pltpu.VMEM((n, rows, part.shape[1]), part.dtype),
            pltpu.VMEM((n, rows, wide), part.dtype),
            pltpu.VMEM((n, rows, cols), prior_rows.dtype),
            pltpu.SemaphoreType.DMA((6, n)),
        ],
        compiler_params=pltpu.CompilerParams(collective_id=1, has_side_effects=True),
    )(part, prior_rows)


def prior_factor_rows(prior_rows, below_shape):
    return prior_rows.reshape(-1, below_shape[3], below_shape[5])


def local(
    n_gc,
    n_gr,
    line,
    below_factor,
    panel_factor,
    prior_factor,
    diag_factor,
    diag_inverse,
    below_adjoint,
    panel_adjoint,
    prior_adjoint,
    diag_adjoint,
):
    tile_count = below_factor.shape[0]
    tile_rows = below_factor.shape[2]
    local_rows = tile_count * tile_rows
    local_cols = below_factor.shape[3] * below_factor.shape[5]
    own_rows = panel_factor.shape[2]
    width = panel_factor.shape[3]
    prior_local = prior_factor.shape[0]
    below_mat = below_factor.reshape(local_rows, local_cols)
    below_bar = below_adjoint.reshape(local_rows, local_cols)
    inverse_bf = diag_inverse.astype(jnp.bfloat16)
    own_grad = jnp.dot(
        panel_adjoint.reshape(tile_count * own_rows, width),
        inverse_bf,
        preferred_element_type=jnp.float32,
    ).astype(jnp.bfloat16)
    panel_grad = own_grad.reshape(panel_adjoint.shape)
    both = jnp.concatenate(
        [own_grad.reshape(tile_count, own_rows, width), panel_factor.reshape(tile_count, own_rows, width)],
        axis=2,
    )
    whole = gather_gc(both, n_gc, line)
    grad_rows = whole[:, :, :width].reshape(local_rows, width)
    whole_factor = whole[:, :, width:].reshape(local_rows, width)
    prior_here = prior_factor.reshape(prior_local, local_cols)
    part = jnp.concatenate(
        [row_product(grad_rows, whole_factor), row_product(grad_rows, below_mat)], axis=1
    ).astype(jnp.bfloat16)
    cross_rows, prior_rows, crossing = reduce_gr(part, prior_here, n_gr)
    summed = cross_rows.reshape(width, width).astype(jnp.float32)
    prior_whole = prior_rows.reshape(width, local_cols)
    diag_reduced = jnp.tril(diag_adjoint - summed)
    diag_gradient = diag_solve(diag_factor, diag_inverse, diag_reduced)
    below_prod = lax.dot_general(
        grad_rows.reshape(tile_count, tile_rows, width),
        prior_factor_rows(prior_rows, below_factor.shape),
        (((2,), (0,)), ((), ())),
        preferred_element_type=jnp.float32,
    ).reshape(below_adjoint.shape)
    below_new = (below_adjoint.astype(jnp.float32) - below_prod).astype(jnp.bfloat16)
    grid_row = lax.axis_index("gr")
    twice_rows = lax.dynamic_slice_in_dim(
        2.0 * diag_gradient, grid_row * prior_local, prior_local, 0
    ).astype(jnp.bfloat16)
    curvature = jnp.dot(twice_rows, prior_whole, preferred_element_type=jnp.float32)
    prior_bar = prior_adjoint.reshape(prior_local, local_cols).astype(jnp.float32)
    prior_new = (prior_bar - crossing - curvature).astype(jnp.bfloat16)
    return (
        below_new,
        panel_grad,
        prior_new.reshape(prior_adjoint.shape),
        diag_gradient,
    )


def line_length(mesh):
    column = list(mesh.devices[0])
    coords = [getattr(d, "coords", None) for d in column]
    if any(c is None for c in coords):
        return 8 if len(column) % 8 == 0 else len(column)
    first = coords[0][0]
    count = 0
    for c in coords:
        if c[0] != first:
            break
        count += 1
    return count if len(column) % count == 0 else len(column)


def solution(mesh):
    in_specs = (
        P(None, "gr", None, None, "gc", None),
        P(None, "gr", "gc", None),
        P("gr", None, "gc", None),
        P(),
        P(),
        P(None, "gr", None, None, "gc", None),
        P(None, "gr", "gc", None),
        P("gr", None, "gc", None),
        P(),
    )
    out_specs = (
        P(None, "gr", None, None, "gc", None),
        P(None, "gr", "gc", None),
        P("gr", None, "gc", None),
        P(),
    )
    return jax.shard_map(
        functools.partial(local, mesh.shape["gc"], mesh.shape["gr"], line_length(mesh)),
        mesh=mesh,
        in_specs=in_specs,
        out_specs=out_specs,
        check_vma=False,
    )
```

```python
import functools

import jax
import jax.numpy as jnp
from jax import lax
from jax.experimental import pallas as pl
from jax.experimental.pallas import tpu as pltpu
from jax.sharding import PartitionSpec as P

MESH_ID = pl.DeviceIdType.MESH


def row_product(left_rows, right_rows):
    return lax.dot_general(
        left_rows, right_rows, (((0,), (0,)), ((), ())), preferred_element_type=jnp.float32
    )


def diag_solve(diag_factor, diag_inverse, diag_reduced):
    highest = lax.Precision.HIGH
    chol_proj = jnp.dot(diag_factor.T, diag_reduced, precision=highest)
    index_row = lax.broadcasted_iota(jnp.int32, chol_proj.shape, 0)
    index_col = lax.broadcasted_iota(jnp.int32, chol_proj.shape, 1)
    phi_lower = jnp.where(
        index_row > index_col,
        chol_proj,
        jnp.where(index_row == index_col, chol_proj - 0.5 * chol_proj, 0.0),
    )
    symmetric = 0.5 * (phi_lower + phi_lower.T)
    left_side = jnp.dot(diag_inverse.T, symmetric, precision=highest)
    return jnp.dot(left_side, diag_inverse, precision=highest)


def gather_kernel(n, line, x_ref, out_ref, sems, local_sem):
    me = lax.axis_index("gc")
    row = lax.axis_index("gr")
    rows = x_ref.shape[1]
    lines = n // line
    pos = lax.rem(me, line)
    grp = me // line
    base = grp * line

    def line_peer(k):
        return base + lax.rem(pos + k, line)

    def cross_peer(k):
        return lax.rem(grp + k, lines) * line + pos

    barrier = pltpu.get_barrier_semaphore()

    def greet_line(k, carry):
        pl.semaphore_signal(barrier, inc=1, device_id=(row, line_peer(k)), device_id_type=MESH_ID)
        return carry

    def greet_cross(k, carry):
        pl.semaphore_signal(barrier, inc=1, device_id=(row, cross_peer(k)), device_id_type=MESH_ID)
        return carry

    lax.fori_loop(1, line, greet_line, 0)
    lax.fori_loop(1, lines, greet_cross, 0)
    pl.semaphore_wait(barrier, line + lines - 2)

    own = pltpu.make_async_copy(x_ref, out_ref.at[:, pl.ds(me * rows, rows), :], local_sem)
    own.start()

    def first(k, sender_pos):
        return pltpu.make_async_remote_copy(
            src_ref=x_ref,
            dst_ref=out_ref.at[:, pl.ds((base + sender_pos) * rows, rows), :],
            send_sem=sems.at[0, k],
            recv_sem=sems.at[1, sender_pos],
            device_id=(row, line_peer(k)),
            device_id_type=MESH_ID,
        )

    def send_first(k, carry):
        first(k, pos).start()
        return carry

    lax.fori_loop(1, line, send_first, 0)

    span = line * rows

    def forward(k, block_pos, sender_grp):
        slot = pl.ds((grp * line + block_pos) * rows, rows)
        return pltpu.make_async_remote_copy(
            src_ref=out_ref.at[:, slot, :],
            dst_ref=out_ref.at[:, slot, :],
            send_sem=sems.at[2 + block_pos, k],
            recv_sem=sems.at[1, line + sender_grp],
            device_id=(row, cross_peer(k)),
            device_id_type=MESH_ID,
        )

    def whole_line(sender_grp):
        return pltpu.make_async_remote_copy(
            src_ref=out_ref.at[:, pl.ds(sender_grp * span, span), :],
            dst_ref=out_ref.at[:, pl.ds(sender_grp * span, span), :],
            send_sem=sems.at[0, 0],
            recv_sem=sems.at[1, line + sender_grp],
            device_id=(row, cross_peer(1)),
            device_id_type=MESH_ID,
        )

    own.wait()

    def send_own(k, carry):
        forward(k, pos, grp).start()
        return carry

    lax.fori_loop(1, lines, send_own, 0)

    def relay(k, carry):
        sender_pos = lax.rem(pos + line - k, line)
        first(k, sender_pos).wait_recv()

        def out(j, inner):
            forward(j, sender_pos, grp).start()
            return inner

        return lax.fori_loop(1, lines, out, carry)

    lax.fori_loop(1, line, relay, 0)

    def wait_first(k, carry):
        first(k, pos).wait_send()
        return carry

    lax.fori_loop(1, line, wait_first, 0)

    def wait_sent(k, carry):
        def done(j, inner):
            forward(j, k, grp).wait_send()
            return inner

        return lax.fori_loop(1, lines, done, carry)

    lax.fori_loop(0, line, wait_sent, 0)

    def wait_lines(k, carry):
        whole_line(lax.rem(grp + lines - k, lines)).wait_recv()
        return carry

    lax.fori_loop(1, lines, wait_lines, 0)


def gather_gc(block, n, line):
    tiles, rows, width = block.shape
    return pl.pallas_call(
        functools.partial(gather_kernel, n, line),
        out_shape=jax.ShapeDtypeStruct((tiles, rows * n, width), block.dtype),
        in_specs=[pl.BlockSpec(memory_space=pl.ANY)],
        out_specs=pl.BlockSpec(memory_space=pl.ANY),
        scratch_shapes=[
            pltpu.SemaphoreType.DMA((2 + line, line + n // line)),
            pltpu.SemaphoreType.DMA,
        ],
        compiler_params=pltpu.CompilerParams(collective_id=0, has_side_effects=True),
    )(block)


def reduce_kernel(n, part_ref, prior_ref, cross_out, prior_out, crossing_out,
                  recv_part, cross_slots, prior_slots, sems):
    me = lax.axis_index("gr")
    col = lax.axis_index("gc")
    rows = prior_ref.shape[0]
    wide = cross_out.shape[2]

    barrier = pltpu.get_barrier_semaphore()

    def greet(k, carry):
        peer = lax.rem(me + k, n)
        pl.semaphore_signal(barrier, inc=1, device_id=(peer, col), device_id_type=MESH_ID)
        return carry

    lax.fori_loop(1, n, greet, 0)
    pl.semaphore_wait(barrier, n - 1)

    def prior_copy(k, sender):
        return pltpu.make_async_remote_copy(
            src_ref=prior_ref,
            dst_ref=prior_slots.at[sender],
            send_sem=sems.at[0, k],
            recv_sem=sems.at[1, sender],
            device_id=(lax.rem(me + k, n), col),
            device_id_type=MESH_ID,
        )

    def part_copy(k, sender):
        peer = lax.rem(me + k, n)
        return pltpu.make_async_remote_copy(
            src_ref=part_ref.at[pl.ds(pl.multiple_of(peer * rows, rows), rows), :],
            dst_ref=recv_part.at[sender],
            send_sem=sems.at[2, k],
            recv_sem=sems.at[3, sender],
            device_id=(peer, col),
            device_id_type=MESH_ID,
        )

    def cross_copy(k, sender):
        return pltpu.make_async_remote_copy(
            src_ref=cross_slots.at[me],
            dst_ref=cross_slots.at[sender],
            send_sem=sems.at[4, k],
            recv_sem=sems.at[5, sender],
            device_id=(lax.rem(me + k, n), col),
            device_id_type=MESH_ID,
        )

    def send_first(k, carry):
        prior_copy(k, me).start()
        part_copy(k, me).start()
        return carry

    lax.fori_loop(1, n, send_first, 0)
    prior_slots[me] = prior_ref[...]

    acc = part_ref[pl.ds(pl.multiple_of(me * rows, rows), rows), :].astype(jnp.float32)

    def add(k, total):
        sender = lax.rem(me + n - k, n)
        part_copy(k, me).wait_send()
        part_copy(k, sender).wait_recv()
        return total + recv_part[sender].astype(jnp.float32)

    acc = lax.fori_loop(1, n, add, acc)
    crossing_out[...] = acc[:, wide:]
    cross_slots[me] = acc[:, :wide].astype(cross_slots.dtype)

    def send_second(k, carry):
        cross_copy(k, me).start()
        return carry

    lax.fori_loop(1, n, send_second, 0)

    def wait_second(k, carry):
        sender = lax.rem(me + n - k, n)
        cross_copy(k, me).wait_send()
        cross_copy(k, sender).wait_recv()
        prior_copy(k, me).wait_send()
        prior_copy(k, sender).wait_recv()
        return carry

    lax.fori_loop(1, n, wait_second, 0)
    cross_out[...] = cross_slots[...]
    prior_out[...] = prior_slots[...]


def reduce_gr(part, prior_rows, n):
    rows, cols = prior_rows.shape
    wide = part.shape[1] - cols
    vmem = pl.BlockSpec(memory_space=pltpu.VMEM)
    return pl.pallas_call(
        functools.partial(reduce_kernel, n),
        out_shape=(
            jax.ShapeDtypeStruct((n, rows, wide), part.dtype),
            jax.ShapeDtypeStruct((n, rows, cols), prior_rows.dtype),
            jax.ShapeDtypeStruct((rows, cols), jnp.float32),
        ),
        in_specs=[vmem, vmem],
        out_specs=(vmem, vmem, vmem),
        scratch_shapes=[
            pltpu.VMEM((n, rows, part.shape[1]), part.dtype),
            pltpu.VMEM((n, rows, wide), part.dtype),
            pltpu.VMEM((n, rows, cols), prior_rows.dtype),
            pltpu.SemaphoreType.DMA((6, n)),
        ],
        compiler_params=pltpu.CompilerParams(collective_id=1, has_side_effects=True),
    )(part, prior_rows)


def prior_factor_rows(prior_rows, below_shape):
    return prior_rows.reshape(-1, below_shape[3], below_shape[5])


def local(
    n_gc,
    n_gr,
    line,
    below_factor,
    panel_factor,
    prior_factor,
    diag_factor,
    diag_inverse,
    below_adjoint,
    panel_adjoint,
    prior_adjoint,
    diag_adjoint,
):
    tile_count = below_factor.shape[0]
    tile_rows = below_factor.shape[2]
    local_rows = tile_count * tile_rows
    local_cols = below_factor.shape[3] * below_factor.shape[5]
    own_rows = panel_factor.shape[2]
    width = panel_factor.shape[3]
    prior_local = prior_factor.shape[0]
    below_mat = below_factor.reshape(local_rows, local_cols)
    below_bar = below_adjoint.reshape(local_rows, local_cols)
    inverse_bf = diag_inverse.astype(jnp.bfloat16)
    own_grad = jnp.dot(
        panel_adjoint.reshape(tile_count * own_rows, width),
        inverse_bf,
        preferred_element_type=jnp.float32,
    ).astype(jnp.bfloat16)
    panel_grad = own_grad.reshape(panel_adjoint.shape)
    both = jnp.concatenate(
        [own_grad.reshape(tile_count, own_rows, width), panel_factor.reshape(tile_count, own_rows, width)],
        axis=2,
    )
    whole = gather_gc(both, n_gc, line)
    grad_rows = whole[:, :, :width].reshape(local_rows, width)
    whole_factor = whole[:, :, width:].reshape(local_rows, width)
    prior_here = prior_factor.reshape(prior_local, local_cols)
    part = jnp.concatenate(
        [row_product(grad_rows, whole_factor), row_product(grad_rows, below_mat)], axis=1
    ).astype(jnp.bfloat16)
    cross_rows, prior_rows, crossing = reduce_gr(part, prior_here, n_gr)
    summed = cross_rows.reshape(width, width).astype(jnp.float32)
    prior_whole = prior_rows.reshape(width, local_cols)
    diag_reduced = jnp.tril(diag_adjoint - summed)
    diag_gradient = diag_solve(diag_factor, diag_inverse, diag_reduced)
    below_prod = lax.dot_general(
        grad_rows.reshape(tile_count, tile_rows, width),
        prior_factor_rows(prior_rows, below_factor.shape),
        (((2,), (0,)), ((), ())),
        preferred_element_type=jnp.float32,
    ).reshape(below_adjoint.shape)
    below_new = (below_adjoint.astype(jnp.float32) - below_prod).astype(jnp.bfloat16)
    grid_row = lax.axis_index("gr")
    twice_rows = lax.dynamic_slice_in_dim(
        2.0 * diag_gradient, grid_row * prior_local, prior_local, 0
    ).astype(jnp.bfloat16)
    curvature = jnp.dot(twice_rows, prior_whole, preferred_element_type=jnp.float32)
    prior_bar = prior_adjoint.reshape(prior_local, local_cols).astype(jnp.float32)
    prior_new = (prior_bar - crossing - curvature).astype(jnp.bfloat16)
    return (
        below_new,
        panel_grad,
        prior_new.reshape(prior_adjoint.shape),
        diag_gradient,
    )


def line_length(mesh):
    column = list(mesh.devices[0])
    coords = [getattr(d, "coords", None) for d in column]
    if any(c is None for c in coords):
        return 8 if len(column) % 8 == 0 else len(column)
    first = coords[0][0]
    count = 0
    for c in coords:
        if c[0] != first:
            break
        count += 1
    return count if len(column) % count == 0 else len(column)


def solution(mesh):
    in_specs = (
        P(None, "gr", None, None, "gc", None),
        P(None, "gr", "gc", None),
        P("gr", None, "gc", None),
        P(),
        P(),
        P(None, "gr", None, None, "gc", None),
        P(None, "gr", "gc", None),
        P("gr", None, "gc", None),
        P(),
    )
    out_specs = (
        P(None, "gr", None, None, "gc", None),
        P(None, "gr", "gc", None),
        P("gr", None, "gc", None),
        P(),
    )
    return jax.shard_map(
        functools.partial(local, mesh.shape["gc"], mesh.shape["gr"], line_length(mesh)),
        mesh=mesh,
        in_specs=in_specs,
        out_specs=out_specs,
        check_vma=False,
    )
```

```python
import functools

import jax
import jax.numpy as jnp
from jax import lax
from jax.experimental import pallas as pl
from jax.experimental.pallas import tpu as pltpu
from jax.sharding import PartitionSpec as P

MESH_ID = pl.DeviceIdType.MESH


def row_product(left_rows, right_rows):
    return lax.dot_general(
        left_rows, right_rows, (((0,), (0,)), ((), ())), preferred_element_type=jnp.float32
    )


def diag_solve(diag_factor, diag_inverse, diag_reduced):
    highest = lax.Precision.HIGH
    chol_proj = jnp.dot(diag_factor.T, diag_reduced, precision=highest)
    index_row = lax.broadcasted_iota(jnp.int32, chol_proj.shape, 0)
    index_col = lax.broadcasted_iota(jnp.int32, chol_proj.shape, 1)
    phi_lower = jnp.where(
        index_row > index_col,
        chol_proj,
        jnp.where(index_row == index_col, chol_proj - 0.5 * chol_proj, 0.0),
    )
    symmetric = 0.5 * (phi_lower + phi_lower.T)
    left_side = jnp.dot(diag_inverse.T, symmetric, precision=highest)
    return jnp.dot(left_side, diag_inverse, precision=highest)


def gather_kernel(n, line, x_ref, out_ref, sems, local_sem):
    me = lax.axis_index("gc")
    row = lax.axis_index("gr")
    rows = x_ref.shape[2]
    lines = n // line
    pos = lax.rem(me, line)
    grp = me // line
    base = grp * line

    def line_peer(k):
        return base + lax.rem(pos + k, line)

    def cross_peer(k):
        return lax.rem(grp + k, lines) * line + pos

    barrier = pltpu.get_barrier_semaphore()

    def greet_line(k, carry):
        pl.semaphore_signal(barrier, inc=1, device_id=(row, line_peer(k)), device_id_type=MESH_ID)
        return carry

    def greet_cross(k, carry):
        pl.semaphore_signal(barrier, inc=1, device_id=(row, cross_peer(k)), device_id_type=MESH_ID)
        return carry

    lax.fori_loop(1, line, greet_line, 0)
    lax.fori_loop(1, lines, greet_cross, 0)
    pl.semaphore_wait(barrier, line + lines - 2)

    own = pltpu.make_async_copy(x_ref, out_ref.at[:, :, pl.ds(me * rows, rows), :], local_sem)
    own.start()

    def first(k, sender_pos):
        return pltpu.make_async_remote_copy(
            src_ref=x_ref,
            dst_ref=out_ref.at[:, :, pl.ds((base + sender_pos) * rows, rows), :],
            send_sem=sems.at[0, k],
            recv_sem=sems.at[1, sender_pos],
            device_id=(row, line_peer(k)),
            device_id_type=MESH_ID,
        )

    def send_first(k, carry):
        first(k, pos).start()
        return carry

    lax.fori_loop(1, line, send_first, 0)

    span = line * rows

    def forward(k, block_pos, sender_grp):
        slot = pl.ds((grp * line + block_pos) * rows, rows)
        return pltpu.make_async_remote_copy(
            src_ref=out_ref.at[:, :, slot, :],
            dst_ref=out_ref.at[:, :, slot, :],
            send_sem=sems.at[2 + block_pos, k],
            recv_sem=sems.at[1, line + sender_grp],
            device_id=(row, cross_peer(k)),
            device_id_type=MESH_ID,
        )

    def whole_line(sender_grp):
        return pltpu.make_async_remote_copy(
            src_ref=out_ref.at[:, :, pl.ds(sender_grp * span, span), :],
            dst_ref=out_ref.at[:, :, pl.ds(sender_grp * span, span), :],
            send_sem=sems.at[0, 0],
            recv_sem=sems.at[1, line + sender_grp],
            device_id=(row, cross_peer(1)),
            device_id_type=MESH_ID,
        )

    own.wait()

    def send_own(k, carry):
        forward(k, pos, grp).start()
        return carry

    lax.fori_loop(1, lines, send_own, 0)

    def relay(k, carry):
        sender_pos = lax.rem(pos + line - k, line)
        first(k, sender_pos).wait_recv()

        def out(j, inner):
            forward(j, sender_pos, grp).start()
            return inner

        return lax.fori_loop(1, lines, out, carry)

    lax.fori_loop(1, line, relay, 0)

    def wait_first(k, carry):
        first(k, pos).wait_send()
        return carry

    lax.fori_loop(1, line, wait_first, 0)

    def wait_sent(k, carry):
        def done(j, inner):
            forward(j, k, grp).wait_send()
            return inner

        return lax.fori_loop(1, lines, done, carry)

    lax.fori_loop(0, line, wait_sent, 0)

    def wait_lines(k, carry):
        whole_line(lax.rem(grp + lines - k, lines)).wait_recv()
        return carry

    lax.fori_loop(1, lines, wait_lines, 0)


def gather_gc(block, n, line):
    count, tiles, rows, width = block.shape
    return pl.pallas_call(
        functools.partial(gather_kernel, n, line),
        out_shape=jax.ShapeDtypeStruct((count, tiles, rows * n, width), block.dtype),
        in_specs=[pl.BlockSpec(memory_space=pl.ANY)],
        out_specs=pl.BlockSpec(memory_space=pl.ANY),
        scratch_shapes=[
            pltpu.SemaphoreType.DMA((2 + line, line + n // line)),
            pltpu.SemaphoreType.DMA,
        ],
        compiler_params=pltpu.CompilerParams(collective_id=0, has_side_effects=True),
    )(block)


def reduce_kernel(n, part_ref, prior_ref, cross_out, prior_out, crossing_out,
                  recv_part, cross_slots, prior_slots, sems):
    me = lax.axis_index("gr")
    col = lax.axis_index("gc")
    rows = prior_ref.shape[0]
    wide = cross_out.shape[2]

    barrier = pltpu.get_barrier_semaphore()

    def greet(k, carry):
        peer = lax.rem(me + k, n)
        pl.semaphore_signal(barrier, inc=1, device_id=(peer, col), device_id_type=MESH_ID)
        return carry

    lax.fori_loop(1, n, greet, 0)
    pl.semaphore_wait(barrier, n - 1)

    def prior_copy(k, sender):
        return pltpu.make_async_remote_copy(
            src_ref=prior_ref,
            dst_ref=prior_slots.at[sender],
            send_sem=sems.at[0, k],
            recv_sem=sems.at[1, sender],
            device_id=(lax.rem(me + k, n), col),
            device_id_type=MESH_ID,
        )

    def part_copy(k, sender):
        peer = lax.rem(me + k, n)
        return pltpu.make_async_remote_copy(
            src_ref=part_ref.at[pl.ds(pl.multiple_of(peer * rows, rows), rows), :],
            dst_ref=recv_part.at[sender],
            send_sem=sems.at[2, k],
            recv_sem=sems.at[3, sender],
            device_id=(peer, col),
            device_id_type=MESH_ID,
        )

    def cross_copy(k, sender):
        return pltpu.make_async_remote_copy(
            src_ref=cross_slots.at[me],
            dst_ref=cross_slots.at[sender],
            send_sem=sems.at[4, k],
            recv_sem=sems.at[5, sender],
            device_id=(lax.rem(me + k, n), col),
            device_id_type=MESH_ID,
        )

    def send_first(k, carry):
        prior_copy(k, me).start()
        part_copy(k, me).start()
        return carry

    lax.fori_loop(1, n, send_first, 0)
    prior_slots[me] = prior_ref[...]

    acc = part_ref[pl.ds(pl.multiple_of(me * rows, rows), rows), :].astype(jnp.float32)

    def add(k, total):
        sender = lax.rem(me + n - k, n)
        part_copy(k, me).wait_send()
        part_copy(k, sender).wait_recv()
        return total + recv_part[sender].astype(jnp.float32)

    acc = lax.fori_loop(1, n, add, acc)
    crossing_out[...] = acc[:, wide:]
    cross_slots[me] = acc[:, :wide].astype(cross_slots.dtype)

    def send_second(k, carry):
        cross_copy(k, me).start()
        return carry

    lax.fori_loop(1, n, send_second, 0)

    def wait_second(k, carry):
        sender = lax.rem(me + n - k, n)
        cross_copy(k, me).wait_send()
        cross_copy(k, sender).wait_recv()
        prior_copy(k, me).wait_send()
        prior_copy(k, sender).wait_recv()
        return carry

    lax.fori_loop(1, n, wait_second, 0)
    cross_out[...] = cross_slots[...]
    prior_out[...] = prior_slots[...]


def reduce_gr(part, prior_rows, n):
    rows, cols = prior_rows.shape
    wide = part.shape[1] - cols
    vmem = pl.BlockSpec(memory_space=pltpu.VMEM)
    return pl.pallas_call(
        functools.partial(reduce_kernel, n),
        out_shape=(
            jax.ShapeDtypeStruct((n, rows, wide), part.dtype),
            jax.ShapeDtypeStruct((n, rows, cols), prior_rows.dtype),
            jax.ShapeDtypeStruct((rows, cols), jnp.float32),
        ),
        in_specs=[vmem, vmem],
        out_specs=(vmem, vmem, vmem),
        scratch_shapes=[
            pltpu.VMEM((n, rows, part.shape[1]), part.dtype),
            pltpu.VMEM((n, rows, wide), part.dtype),
            pltpu.VMEM((n, rows, cols), prior_rows.dtype),
            pltpu.SemaphoreType.DMA((6, n)),
        ],
        compiler_params=pltpu.CompilerParams(collective_id=1, has_side_effects=True),
    )(part, prior_rows)


def prior_factor_rows(prior_rows, below_shape):
    return prior_rows.reshape(-1, below_shape[3], below_shape[5])


def local(
    n_gc,
    n_gr,
    line,
    below_factor,
    panel_factor,
    prior_factor,
    diag_factor,
    diag_inverse,
    below_adjoint,
    panel_adjoint,
    prior_adjoint,
    diag_adjoint,
):
    tile_count = below_factor.shape[0]
    tile_rows = below_factor.shape[2]
    local_rows = tile_count * tile_rows
    local_cols = below_factor.shape[3] * below_factor.shape[5]
    own_rows = panel_factor.shape[2]
    width = panel_factor.shape[3]
    prior_local = prior_factor.shape[0]
    below_mat = below_factor.reshape(local_rows, local_cols)
    below_bar = below_adjoint.reshape(local_rows, local_cols)
    inverse_bf = diag_inverse.astype(jnp.bfloat16)
    own_grad = jnp.dot(
        panel_adjoint.reshape(tile_count * own_rows, width),
        inverse_bf,
        preferred_element_type=jnp.float32,
    ).astype(jnp.bfloat16)
    panel_grad = own_grad.reshape(panel_adjoint.shape)
    both = jnp.stack(
        [own_grad.reshape(tile_count, own_rows, width), panel_factor.reshape(tile_count, own_rows, width)]
    )
    whole = gather_gc(both, n_gc, line)
    grad_rows = whole[0].reshape(local_rows, width)
    whole_factor = whole[1].reshape(local_rows, width)
    prior_here = prior_factor.reshape(prior_local, local_cols)
    part = jnp.concatenate(
        [row_product(grad_rows, whole_factor), row_product(grad_rows, below_mat)], axis=1
    ).astype(jnp.bfloat16)
    cross_rows, prior_rows, crossing = reduce_gr(part, prior_here, n_gr)
    summed = cross_rows.reshape(width, width).astype(jnp.float32)
    prior_whole = prior_rows.reshape(width, local_cols)
    diag_reduced = jnp.tril(diag_adjoint - summed)
    diag_gradient = diag_solve(diag_factor, diag_inverse, diag_reduced)
    below_prod = lax.dot_general(
        grad_rows.reshape(tile_count, tile_rows, width),
        prior_factor_rows(prior_rows, below_factor.shape),
        (((2,), (0,)), ((), ())),
        preferred_element_type=jnp.float32,
    ).reshape(below_adjoint.shape)
    below_new = (below_adjoint.astype(jnp.float32) - below_prod).astype(jnp.bfloat16)
    grid_row = lax.axis_index("gr")
    twice_rows = lax.dynamic_slice_in_dim(
        2.0 * diag_gradient, grid_row * prior_local, prior_local, 0
    ).astype(jnp.bfloat16)
    curvature = jnp.dot(twice_rows, prior_whole, preferred_element_type=jnp.float32)
    prior_bar = prior_adjoint.reshape(prior_local, local_cols).astype(jnp.float32)
    prior_new = (prior_bar - crossing - curvature).astype(jnp.bfloat16)
    return (
        below_new,
        panel_grad,
        prior_new.reshape(prior_adjoint.shape),
        diag_gradient,
    )


def line_length(mesh):
    column = list(mesh.devices[0])
    coords = [getattr(d, "coords", None) for d in column]
    if any(c is None for c in coords):
        return 8 if len(column) % 8 == 0 else len(column)
    first = coords[0][0]
    count = 0
    for c in coords:
        if c[0] != first:
            break
        count += 1
    return count if len(column) % count == 0 else len(column)


def solution(mesh):
    in_specs = (
        P(None, "gr", None, None, "gc", None),
        P(None, "gr", "gc", None),
        P("gr", None, "gc", None),
        P(),
        P(),
        P(None, "gr", None, None, "gc", None),
        P(None, "gr", "gc", None),
        P("gr", None, "gc", None),
        P(),
    )
    out_specs = (
        P(None, "gr", None, None, "gc", None),
        P(None, "gr", "gc", None),
        P("gr", None, "gc", None),
        P(),
    )
    return jax.shard_map(
        functools.partial(local, mesh.shape["gc"], mesh.shape["gr"], line_length(mesh)),
        mesh=mesh,
        in_specs=in_specs,
        out_specs=out_specs,
        check_vma=False,
    )
```

```python
import functools

import jax
import jax.numpy as jnp
from jax import lax
from jax.experimental import pallas as pl
from jax.experimental.pallas import tpu as pltpu
from jax.sharding import PartitionSpec as P

MESH_ID = pl.DeviceIdType.MESH


def row_product(left_rows, right_rows):
    return lax.dot_general(
        left_rows, right_rows, (((0,), (0,)), ((), ())), preferred_element_type=jnp.float32
    )


def diag_solve(diag_factor, diag_inverse, diag_reduced):
    highest = lax.Precision.HIGH
    chol_proj = jnp.dot(diag_factor.T, diag_reduced, precision=highest)
    index_row = lax.broadcasted_iota(jnp.int32, chol_proj.shape, 0)
    index_col = lax.broadcasted_iota(jnp.int32, chol_proj.shape, 1)
    phi_lower = jnp.where(
        index_row > index_col,
        chol_proj,
        jnp.where(index_row == index_col, chol_proj - 0.5 * chol_proj, 0.0),
    )
    symmetric = 0.5 * (phi_lower + phi_lower.T)
    left_side = jnp.dot(diag_inverse.T, symmetric, precision=highest)
    return jnp.dot(left_side, diag_inverse, precision=highest)


def gather_kernel(n, line, x_ref, p_ref, out_ref, psum_ref, precv, psems, sems, local_sem):
    me = lax.axis_index("gc")
    row = lax.axis_index("gr")
    rows = x_ref.shape[2]
    lines = n // line
    pos = lax.rem(me, line)
    grp = me // line
    base = grp * line

    def line_peer(k):
        return base + lax.rem(pos + k, line)

    def cross_peer(k):
        return lax.rem(grp + k, lines) * line + pos

    barrier = pltpu.get_barrier_semaphore()

    def greet(k, carry):
        pl.semaphore_signal(barrier, inc=1, device_id=(row, lax.rem(me + k, n)), device_id_type=MESH_ID)
        return carry

    lax.fori_loop(1, n, greet, 0)
    pl.semaphore_wait(barrier, n - 1)

    def part_copy(k, sender):
        peer = lax.rem(me + k, n)
        return pltpu.make_async_remote_copy(
            src_ref=p_ref.at[peer],
            dst_ref=precv.at[sender],
            send_sem=psems.at[0, k],
            recv_sem=psems.at[1, sender],
            device_id=(row, peer),
            device_id_type=MESH_ID,
        )

    own = pltpu.make_async_copy(x_ref, out_ref.at[:, :, pl.ds(me * rows, rows), :], local_sem)
    own.start()

    def first(k, sender_pos):
        return pltpu.make_async_remote_copy(
            src_ref=x_ref,
            dst_ref=out_ref.at[:, :, pl.ds((base + sender_pos) * rows, rows), :],
            send_sem=sems.at[0, k],
            recv_sem=sems.at[1, sender_pos],
            device_id=(row, line_peer(k)),
            device_id_type=MESH_ID,
        )

    def send_first(k, carry):
        first(k, pos).start()
        return carry

    lax.fori_loop(1, line, send_first, 0)

    def send_parts(k, carry):
        part_copy(k, me).start()
        return carry

    lax.fori_loop(1, n, send_parts, 0)

    span = line * rows

    def forward(k, block_pos, sender_grp):
        slot = pl.ds((grp * line + block_pos) * rows, rows)
        return pltpu.make_async_remote_copy(
            src_ref=out_ref.at[:, :, slot, :],
            dst_ref=out_ref.at[:, :, slot, :],
            send_sem=sems.at[2 + block_pos, k],
            recv_sem=sems.at[1, line + sender_grp],
            device_id=(row, cross_peer(k)),
            device_id_type=MESH_ID,
        )

    def whole_line(sender_grp):
        return pltpu.make_async_remote_copy(
            src_ref=out_ref.at[:, :, pl.ds(sender_grp * span, span), :],
            dst_ref=out_ref.at[:, :, pl.ds(sender_grp * span, span), :],
            send_sem=sems.at[0, 0],
            recv_sem=sems.at[1, line + sender_grp],
            device_id=(row, cross_peer(1)),
            device_id_type=MESH_ID,
        )

    own.wait()

    def send_own(k, carry):
        forward(k, pos, grp).start()
        return carry

    lax.fori_loop(1, lines, send_own, 0)

    def relay(k, carry):
        sender_pos = lax.rem(pos + line - k, line)
        first(k, sender_pos).wait_recv()

        def out(j, inner):
            forward(j, sender_pos, grp).start()
            return inner

        return lax.fori_loop(1, lines, out, carry)

    lax.fori_loop(1, line, relay, 0)

    def wait_first(k, carry):
        first(k, pos).wait_send()
        return carry

    lax.fori_loop(1, line, wait_first, 0)

    def wait_sent(k, carry):
        def done(j, inner):
            forward(j, k, grp).wait_send()
            return inner

        return lax.fori_loop(1, lines, done, carry)

    lax.fori_loop(0, line, wait_sent, 0)

    def wait_lines(k, carry):
        whole_line(lax.rem(grp + lines - k, lines)).wait_recv()
        return carry

    lax.fori_loop(1, lines, wait_lines, 0)

    precv[me] = p_ref[me]

    def wait_parts(k, carry):
        part_copy(k, me).wait_send()
        part_copy(k, lax.rem(me + n - k, n)).wait_recv()
        return carry

    lax.fori_loop(1, n, wait_parts, 0)

    def add_part(j, total):
        return total + precv[j].astype(jnp.float32)

    psum_ref[...] = lax.fori_loop(0, n, add_part, jnp.zeros(psum_ref.shape, jnp.float32))


def gather_gc(block, part, n, line):
    count, tiles, rows, width = block.shape
    vmem = pl.BlockSpec(memory_space=pltpu.VMEM)
    return pl.pallas_call(
        functools.partial(gather_kernel, n, line),
        out_shape=(
            jax.ShapeDtypeStruct((count, tiles, rows * n, width), block.dtype),
            jax.ShapeDtypeStruct(part.shape[1:], jnp.float32),
        ),
        in_specs=[pl.BlockSpec(memory_space=pl.ANY), vmem],
        out_specs=(pl.BlockSpec(memory_space=pl.ANY), vmem),
        scratch_shapes=[
            pltpu.VMEM(part.shape, part.dtype),
            pltpu.SemaphoreType.DMA((2, n)),
            pltpu.SemaphoreType.DMA((2 + line, line + n // line)),
            pltpu.SemaphoreType.DMA,
        ],
        compiler_params=pltpu.CompilerParams(collective_id=0, has_side_effects=True),
    )(block, part)


def reduce_kernel(n, n_gc, crossing_ref, piece_ref, prior_ref, cross_out, prior_out, crossing_out,
                  recv_crossing, recv_piece, prior_slots, cross_slots, sems):
    me = lax.axis_index("gr")
    col = lax.axis_index("gc")
    rows = prior_ref.shape[0]

    barrier = pltpu.get_barrier_semaphore()

    def greet_gr(k, carry):
        pl.semaphore_signal(barrier, inc=1, device_id=(lax.rem(me + k, n), col), device_id_type=MESH_ID)
        return carry

    def greet_gc(k, carry):
        pl.semaphore_signal(barrier, inc=1, device_id=(me, lax.rem(col + k, n_gc)), device_id_type=MESH_ID)
        return carry

    lax.fori_loop(1, n, greet_gr, 0)
    lax.fori_loop(1, n_gc, greet_gc, 0)
    pl.semaphore_wait(barrier, n + n_gc - 2)

    def gr_copy(k, sender, src, dst, index):
        return pltpu.make_async_remote_copy(
            src_ref=src,
            dst_ref=dst.at[sender],
            send_sem=sems.at[index, k],
            recv_sem=sems.at[index + 1, sender],
            device_id=(lax.rem(me + k, n), col),
            device_id_type=MESH_ID,
        )

    def crossing_copy(k, sender):
        peer = lax.rem(me + k, n)
        src = crossing_ref.at[pl.ds(pl.multiple_of(peer * rows, rows), rows), :]
        return gr_copy(k, sender, src, recv_crossing, 0)

    def piece_copy(k, sender):
        return gr_copy(k, sender, piece_ref, recv_piece, 2)

    def prior_copy(k, sender):
        return gr_copy(k, sender, prior_ref, prior_slots, 4)

    def cross_copy(k, sender):
        return pltpu.make_async_remote_copy(
            src_ref=cross_slots.at[col],
            dst_ref=cross_slots.at[sender],
            send_sem=sems.at[6, k],
            recv_sem=sems.at[7, sender],
            device_id=(me, lax.rem(col + k, n_gc)),
            device_id_type=MESH_ID,
        )

    def send_first(k, carry):
        piece_copy(k, me).start()
        crossing_copy(k, me).start()
        prior_copy(k, me).start()
        return carry

    lax.fori_loop(1, n, send_first, 0)
    prior_slots[me] = prior_ref[...]
    recv_piece[me] = piece_ref[...]
    recv_crossing[me] = crossing_ref[pl.ds(pl.multiple_of(me * rows, rows), rows), :]

    def wait_first(k, carry):
        sender = lax.rem(me + n - k, n)
        piece_copy(k, me).wait_send()
        piece_copy(k, sender).wait_recv()
        crossing_copy(k, me).wait_send()
        crossing_copy(k, sender).wait_recv()
        return carry

    lax.fori_loop(1, n, wait_first, 0)

    def add_piece(j, total):
        return total + recv_piece[j]

    piece = lax.fori_loop(0, n, add_piece, jnp.zeros(piece_ref.shape, jnp.float32))
    cross_slots[col] = piece.astype(cross_slots.dtype)

    def send_second(k, carry):
        cross_copy(k, col).start()
        return carry

    lax.fori_loop(1, n_gc, send_second, 0)

    def add_crossing(j, total):
        return total + recv_crossing[j].astype(jnp.float32)

    crossing_out[...] = lax.fori_loop(0, n, add_crossing, jnp.zeros(crossing_out.shape, jnp.float32))

    def wait_second(k, carry):
        cross_copy(k, col).wait_send()
        cross_copy(k, lax.rem(col + n_gc - k, n_gc)).wait_recv()
        return carry

    lax.fori_loop(1, n_gc, wait_second, 0)

    def wait_prior(k, carry):
        prior_copy(k, me).wait_send()
        prior_copy(k, lax.rem(me + n - k, n)).wait_recv()
        return carry

    lax.fori_loop(1, n, wait_prior, 0)
    cross_out[...] = cross_slots[...]
    prior_out[...] = prior_slots[...]


def reduce_gr(crossing_part, piece, prior_rows, n, n_gc):
    rows, cols = prior_rows.shape
    vmem = pl.BlockSpec(memory_space=pltpu.VMEM)
    return pl.pallas_call(
        functools.partial(reduce_kernel, n, n_gc),
        out_shape=(
            jax.ShapeDtypeStruct((n_gc,) + piece.shape, jnp.bfloat16),
            jax.ShapeDtypeStruct((n, rows, cols), prior_rows.dtype),
            jax.ShapeDtypeStruct((rows, cols), jnp.float32),
        ),
        in_specs=[vmem, vmem, vmem],
        out_specs=(vmem, vmem, vmem),
        scratch_shapes=[
            pltpu.VMEM((n, rows, cols), crossing_part.dtype),
            pltpu.VMEM((n,) + piece.shape, jnp.float32),
            pltpu.VMEM((n, rows, cols), prior_rows.dtype),
            pltpu.VMEM((n_gc,) + piece.shape, jnp.bfloat16),
            pltpu.SemaphoreType.DMA((8, max(n, n_gc))),
        ],
        compiler_params=pltpu.CompilerParams(collective_id=1, has_side_effects=True),
    )(crossing_part, piece, prior_rows)


def prior_factor_rows(prior_rows, below_shape):
    return prior_rows.reshape(-1, below_shape[3], below_shape[5])


def local(
    n_gc,
    n_gr,
    line,
    below_factor,
    panel_factor,
    prior_factor,
    diag_factor,
    diag_inverse,
    below_adjoint,
    panel_adjoint,
    prior_adjoint,
    diag_adjoint,
):
    tile_count = below_factor.shape[0]
    tile_rows = below_factor.shape[2]
    local_rows = tile_count * tile_rows
    local_cols = below_factor.shape[3] * below_factor.shape[5]
    own_rows = panel_factor.shape[2]
    width = panel_factor.shape[3]
    prior_local = prior_factor.shape[0]
    below_mat = below_factor.reshape(local_rows, local_cols)
    below_bar = below_adjoint.reshape(local_rows, local_cols)
    inverse_bf = diag_inverse.astype(jnp.bfloat16)
    own_grad = jnp.dot(
        panel_adjoint.reshape(tile_count * own_rows, width),
        inverse_bf,
        preferred_element_type=jnp.float32,
    ).astype(jnp.bfloat16)
    panel_grad = own_grad.reshape(panel_adjoint.shape)
    own_factor = panel_factor.reshape(tile_count * own_rows, width)
    own_part = row_product(own_grad, own_factor).astype(jnp.bfloat16)
    whole, piece = gather_gc(
        own_grad.reshape(1, tile_count, own_rows, width),
        own_part.reshape(n_gc, width // n_gc, width),
        n_gc,
        line,
    )
    grad_rows = whole[0].reshape(local_rows, width)
    prior_here = prior_factor.reshape(prior_local, local_cols)
    crossing_part = row_product(grad_rows, below_mat).astype(jnp.bfloat16)
    cross_rows, prior_rows, crossing = reduce_gr(crossing_part, piece, prior_here, n_gr, n_gc)
    summed = cross_rows.reshape(width, width).astype(jnp.float32)
    prior_whole = prior_rows.reshape(width, local_cols)
    diag_reduced = jnp.tril(diag_adjoint - summed)
    diag_gradient = diag_solve(diag_factor, diag_inverse, diag_reduced)
    below_prod = lax.dot_general(
        grad_rows.reshape(tile_count, tile_rows, width),
        prior_factor_rows(prior_rows, below_factor.shape),
        (((2,), (0,)), ((), ())),
        preferred_element_type=jnp.float32,
    ).reshape(below_adjoint.shape)
    below_new = (below_adjoint.astype(jnp.float32) - below_prod).astype(jnp.bfloat16)
    grid_row = lax.axis_index("gr")
    twice_rows = lax.dynamic_slice_in_dim(
        2.0 * diag_gradient, grid_row * prior_local, prior_local, 0
    ).astype(jnp.bfloat16)
    curvature = jnp.dot(twice_rows, prior_whole, preferred_element_type=jnp.float32)
    prior_bar = prior_adjoint.reshape(prior_local, local_cols).astype(jnp.float32)
    prior_new = (prior_bar - crossing - curvature).astype(jnp.bfloat16)
    return (
        below_new,
        panel_grad,
        prior_new.reshape(prior_adjoint.shape),
        diag_gradient,
    )


def line_length(mesh):
    column = list(mesh.devices[0])
    coords = [getattr(d, "coords", None) for d in column]
    if any(c is None for c in coords):
        return 8 if len(column) % 8 == 0 else len(column)
    first = coords[0][0]
    count = 0
    for c in coords:
        if c[0] != first:
            break
        count += 1
    return count if len(column) % count == 0 else len(column)


def solution(mesh):
    in_specs = (
        P(None, "gr", None, None, "gc", None),
        P(None, "gr", "gc", None),
        P("gr", None, "gc", None),
        P(),
        P(),
        P(None, "gr", None, None, "gc", None),
        P(None, "gr", "gc", None),
        P("gr", None, "gc", None),
        P(),
    )
    out_specs = (
        P(None, "gr", None, None, "gc", None),
        P(None, "gr", "gc", None),
        P("gr", None, "gc", None),
        P(),
    )
    return jax.shard_map(
        functools.partial(local, mesh.shape["gc"], mesh.shape["gr"], line_length(mesh)),
        mesh=mesh,
        in_specs=in_specs,
        out_specs=out_specs,
        check_vma=False,
    )
```

```python
import functools

import jax
import jax.numpy as jnp
from jax import lax
from jax.experimental import pallas as pl
from jax.experimental.pallas import tpu as pltpu
from jax.sharding import PartitionSpec as P

MESH_ID = pl.DeviceIdType.MESH


def row_product(left_rows, right_rows):
    return lax.dot_general(
        left_rows, right_rows, (((0,), (0,)), ((), ())), preferred_element_type=jnp.float32
    )


def diag_solve(diag_factor, diag_inverse, diag_reduced):
    highest = lax.Precision.HIGH
    chol_proj = jnp.dot(diag_factor.T, diag_reduced, precision=highest)
    index_row = lax.broadcasted_iota(jnp.int32, chol_proj.shape, 0)
    index_col = lax.broadcasted_iota(jnp.int32, chol_proj.shape, 1)
    phi_lower = jnp.where(
        index_row > index_col,
        chol_proj,
        jnp.where(index_row == index_col, chol_proj - 0.5 * chol_proj, 0.0),
    )
    symmetric = 0.5 * (phi_lower + phi_lower.T)
    left_side = jnp.dot(diag_inverse.T, symmetric, precision=highest)
    return jnp.dot(left_side, diag_inverse, precision=highest)


def gather_kernel(n, line, x_ref, p_ref, out_ref, psum_ref, precv, psems, sems, local_sem):
    me = lax.axis_index("gc")
    row = lax.axis_index("gr")
    rows = x_ref.shape[2]
    lines = n // line
    pos = lax.rem(me, line)
    grp = me // line
    base = grp * line

    def line_peer(k):
        return base + lax.rem(pos + k, line)

    def cross_peer(k):
        return lax.rem(grp + k, lines) * line + pos

    barrier = pltpu.get_barrier_semaphore()

    def greet(k, carry):
        pl.semaphore_signal(barrier, inc=1, device_id=(row, lax.rem(me + k, n)), device_id_type=MESH_ID)
        return carry

    lax.fori_loop(1, n, greet, 0)
    pl.semaphore_wait(barrier, n - 1)

    def part_copy(k, sender):
        peer = lax.rem(me + k, n)
        return pltpu.make_async_remote_copy(
            src_ref=p_ref.at[peer],
            dst_ref=precv.at[sender],
            send_sem=psems.at[0, k],
            recv_sem=psems.at[1, sender],
            device_id=(row, peer),
            device_id_type=MESH_ID,
        )

    own = pltpu.make_async_copy(x_ref, out_ref.at[:, :, pl.ds(me * rows, rows), :], local_sem)
    own.start()

    def first(k, sender_pos):
        return pltpu.make_async_remote_copy(
            src_ref=x_ref,
            dst_ref=out_ref.at[:, :, pl.ds((base + sender_pos) * rows, rows), :],
            send_sem=sems.at[0, k],
            recv_sem=sems.at[1, sender_pos],
            device_id=(row, line_peer(k)),
            device_id_type=MESH_ID,
        )

    def send_first(k, carry):
        first(k, pos).start()
        return carry

    lax.fori_loop(1, line, send_first, 0)

    def send_parts(k, carry):
        part_copy(k, me).start()
        return carry

    lax.fori_loop(1, n, send_parts, 0)

    span = line * rows

    def forward(k, block_pos, sender_grp):
        slot = pl.ds((grp * line + block_pos) * rows, rows)
        return pltpu.make_async_remote_copy(
            src_ref=out_ref.at[:, :, slot, :],
            dst_ref=out_ref.at[:, :, slot, :],
            send_sem=sems.at[2 + block_pos, k],
            recv_sem=sems.at[1, line + sender_grp],
            device_id=(row, cross_peer(k)),
            device_id_type=MESH_ID,
        )

    def whole_line(sender_grp):
        return pltpu.make_async_remote_copy(
            src_ref=out_ref.at[:, :, pl.ds(sender_grp * span, span), :],
            dst_ref=out_ref.at[:, :, pl.ds(sender_grp * span, span), :],
            send_sem=sems.at[0, 0],
            recv_sem=sems.at[1, line + sender_grp],
            device_id=(row, cross_peer(1)),
            device_id_type=MESH_ID,
        )

    own.wait()

    def send_own(k, carry):
        forward(k, pos, grp).start()
        return carry

    lax.fori_loop(1, lines, send_own, 0)

    def relay(k, carry):
        sender_pos = lax.rem(pos + line - k, line)
        first(k, sender_pos).wait_recv()

        def out(j, inner):
            forward(j, sender_pos, grp).start()
            return inner

        return lax.fori_loop(1, lines, out, carry)

    lax.fori_loop(1, line, relay, 0)

    def wait_first(k, carry):
        first(k, pos).wait_send()
        return carry

    lax.fori_loop(1, line, wait_first, 0)

    def wait_sent(k, carry):
        def done(j, inner):
            forward(j, k, grp).wait_send()
            return inner

        return lax.fori_loop(1, lines, done, carry)

    lax.fori_loop(0, line, wait_sent, 0)

    def wait_lines(k, carry):
        whole_line(lax.rem(grp + lines - k, lines)).wait_recv()
        return carry

    lax.fori_loop(1, lines, wait_lines, 0)

    precv[me] = p_ref[me]

    def wait_parts(k, carry):
        part_copy(k, me).wait_send()
        part_copy(k, lax.rem(me + n - k, n)).wait_recv()
        return carry

    lax.fori_loop(1, n, wait_parts, 0)

    def add_part(j, total):
        return total + precv[j].astype(jnp.float32)

    psum_ref[...] = lax.fori_loop(0, n, add_part, jnp.zeros(psum_ref.shape, jnp.float32))


def gather_gc(block, part, n, line):
    count, tiles, rows, width = block.shape
    vmem = pl.BlockSpec(memory_space=pltpu.VMEM)
    return pl.pallas_call(
        functools.partial(gather_kernel, n, line),
        out_shape=(
            jax.ShapeDtypeStruct((count, tiles, rows * n, width), block.dtype),
            jax.ShapeDtypeStruct(part.shape[1:], jnp.float32),
        ),
        in_specs=[pl.BlockSpec(memory_space=pl.ANY), vmem],
        out_specs=(pl.BlockSpec(memory_space=pl.ANY), vmem),
        scratch_shapes=[
            pltpu.VMEM(part.shape, part.dtype),
            pltpu.SemaphoreType.DMA((2, n)),
            pltpu.SemaphoreType.DMA((2 + line, line + n // line)),
            pltpu.SemaphoreType.DMA,
        ],
        compiler_params=pltpu.CompilerParams(collective_id=0, has_side_effects=True),
    )(block, part)


def reduce_kernel(n, n_gc, crossing_ref, piece_ref, prior_ref, cross_out, prior_out, crossing_out,
                  recv_crossing, recv_piece, prior_slots, cross_slots, sems):
    me = lax.axis_index("gr")
    col = lax.axis_index("gc")
    rows = prior_ref.shape[0]

    barrier = pltpu.get_barrier_semaphore()

    def greet_gr(k, carry):
        pl.semaphore_signal(barrier, inc=1, device_id=(lax.rem(me + k, n), col), device_id_type=MESH_ID)
        return carry

    def greet_gc(k, carry):
        pl.semaphore_signal(barrier, inc=1, device_id=(me, lax.rem(col + k, n_gc)), device_id_type=MESH_ID)
        return carry

    lax.fori_loop(1, n, greet_gr, 0)
    lax.fori_loop(1, n_gc, greet_gc, 0)
    pl.semaphore_wait(barrier, n + n_gc - 2)

    def gr_copy(k, sender, src, dst, index):
        return pltpu.make_async_remote_copy(
            src_ref=src,
            dst_ref=dst.at[sender],
            send_sem=sems.at[index, k],
            recv_sem=sems.at[index + 1, sender],
            device_id=(lax.rem(me + k, n), col),
            device_id_type=MESH_ID,
        )

    def crossing_copy(k, sender):
        peer = lax.rem(me + k, n)
        src = crossing_ref.at[pl.ds(pl.multiple_of(peer * rows, rows), rows), :]
        return gr_copy(k, sender, src, recv_crossing, 0)

    def piece_copy(k, sender):
        return gr_copy(k, sender, piece_ref, recv_piece, 2)

    def prior_copy(k, sender):
        return gr_copy(k, sender, prior_ref, prior_slots, 4)

    def cross_copy(k, sender):
        return pltpu.make_async_remote_copy(
            src_ref=cross_slots.at[col],
            dst_ref=cross_slots.at[sender],
            send_sem=sems.at[6, k],
            recv_sem=sems.at[7, sender],
            device_id=(me, lax.rem(col + k, n_gc)),
            device_id_type=MESH_ID,
        )

    def send_first(k, carry):
        piece_copy(k, me).start()
        crossing_copy(k, me).start()
        prior_copy(k, me).start()
        return carry

    lax.fori_loop(1, n, send_first, 0)
    prior_slots[me] = prior_ref[...]
    recv_piece[me] = piece_ref[...]
    recv_crossing[me] = crossing_ref[pl.ds(pl.multiple_of(me * rows, rows), rows), :]

    def wait_first(k, carry):
        piece_copy(k, me).wait_send()
        piece_copy(k, lax.rem(me + n - k, n)).wait_recv()
        return carry

    lax.fori_loop(1, n, wait_first, 0)

    def add_piece(j, total):
        return total + recv_piece[j]

    piece = lax.fori_loop(0, n, add_piece, jnp.zeros(piece_ref.shape, jnp.float32))
    cross_slots[col] = piece.astype(cross_slots.dtype)

    def send_second(k, carry):
        cross_copy(k, col).start()
        return carry

    lax.fori_loop(1, n_gc, send_second, 0)

    def wait_crossing(k, carry):
        crossing_copy(k, me).wait_send()
        crossing_copy(k, lax.rem(me + n - k, n)).wait_recv()
        return carry

    lax.fori_loop(1, n, wait_crossing, 0)

    def add_crossing(j, total):
        return total + recv_crossing[j].astype(jnp.float32)

    crossing_out[...] = lax.fori_loop(0, n, add_crossing, jnp.zeros(crossing_out.shape, jnp.float32))

    def wait_second(k, carry):
        cross_copy(k, col).wait_send()
        cross_copy(k, lax.rem(col + n_gc - k, n_gc)).wait_recv()
        return carry

    lax.fori_loop(1, n_gc, wait_second, 0)

    def wait_prior(k, carry):
        prior_copy(k, me).wait_send()
        prior_copy(k, lax.rem(me + n - k, n)).wait_recv()
        return carry

    lax.fori_loop(1, n, wait_prior, 0)
    cross_out[...] = cross_slots[...]
    prior_out[...] = prior_slots[...]


def reduce_gr(crossing_part, piece, prior_rows, n, n_gc):
    rows, cols = prior_rows.shape
    vmem = pl.BlockSpec(memory_space=pltpu.VMEM)
    return pl.pallas_call(
        functools.partial(reduce_kernel, n, n_gc),
        out_shape=(
            jax.ShapeDtypeStruct((n_gc,) + piece.shape, jnp.bfloat16),
            jax.ShapeDtypeStruct((n, rows, cols), prior_rows.dtype),
            jax.ShapeDtypeStruct((rows, cols), jnp.float32),
        ),
        in_specs=[vmem, vmem, vmem],
        out_specs=(vmem, vmem, vmem),
        scratch_shapes=[
            pltpu.VMEM((n, rows, cols), crossing_part.dtype),
            pltpu.VMEM((n,) + piece.shape, jnp.float32),
            pltpu.VMEM((n, rows, cols), prior_rows.dtype),
            pltpu.VMEM((n_gc,) + piece.shape, jnp.bfloat16),
            pltpu.SemaphoreType.DMA((8, max(n, n_gc))),
        ],
        compiler_params=pltpu.CompilerParams(collective_id=1, has_side_effects=True),
    )(crossing_part, piece, prior_rows)


def prior_factor_rows(prior_rows, below_shape):
    return prior_rows.reshape(-1, below_shape[3], below_shape[5])


def local(
    n_gc,
    n_gr,
    line,
    below_factor,
    panel_factor,
    prior_factor,
    diag_factor,
    diag_inverse,
    below_adjoint,
    panel_adjoint,
    prior_adjoint,
    diag_adjoint,
):
    tile_count = below_factor.shape[0]
    tile_rows = below_factor.shape[2]
    local_rows = tile_count * tile_rows
    local_cols = below_factor.shape[3] * below_factor.shape[5]
    own_rows = panel_factor.shape[2]
    width = panel_factor.shape[3]
    prior_local = prior_factor.shape[0]
    below_mat = below_factor.reshape(local_rows, local_cols)
    below_bar = below_adjoint.reshape(local_rows, local_cols)
    inverse_bf = diag_inverse.astype(jnp.bfloat16)
    own_grad = jnp.dot(
        panel_adjoint.reshape(tile_count * own_rows, width),
        inverse_bf,
        preferred_element_type=jnp.float32,
    ).astype(jnp.bfloat16)
    panel_grad = own_grad.reshape(panel_adjoint.shape)
    own_factor = panel_factor.reshape(tile_count * own_rows, width)
    own_part = row_product(own_grad, own_factor).astype(jnp.bfloat16)
    whole, piece = gather_gc(
        own_grad.reshape(1, tile_count, own_rows, width),
        own_part.reshape(n_gc, width // n_gc, width),
        n_gc,
        line,
    )
    grad_rows = whole[0].reshape(local_rows, width)
    prior_here = prior_factor.reshape(prior_local, local_cols)
    crossing_part = row_product(grad_rows, below_mat).astype(jnp.bfloat16)
    cross_rows, prior_rows, crossing = reduce_gr(crossing_part, piece, prior_here, n_gr, n_gc)
    summed = cross_rows.reshape(width, width).astype(jnp.float32)
    prior_whole = prior_rows.reshape(width, local_cols)
    diag_reduced = jnp.tril(diag_adjoint - summed)
    diag_gradient = diag_solve(diag_factor, diag_inverse, diag_reduced)
    below_prod = lax.dot_general(
        grad_rows.reshape(tile_count, tile_rows, width),
        prior_factor_rows(prior_rows, below_factor.shape),
        (((2,), (0,)), ((), ())),
        preferred_element_type=jnp.float32,
    ).reshape(below_adjoint.shape)
    below_new = (below_adjoint.astype(jnp.float32) - below_prod).astype(jnp.bfloat16)
    grid_row = lax.axis_index("gr")
    twice_rows = lax.dynamic_slice_in_dim(
        2.0 * diag_gradient, grid_row * prior_local, prior_local, 0
    ).astype(jnp.bfloat16)
    curvature = jnp.dot(twice_rows, prior_whole, preferred_element_type=jnp.float32)
    prior_bar = prior_adjoint.reshape(prior_local, local_cols).astype(jnp.float32)
    prior_new = (prior_bar - crossing - curvature).astype(jnp.bfloat16)
    return (
        below_new,
        panel_grad,
        prior_new.reshape(prior_adjoint.shape),
        diag_gradient,
    )


def line_length(mesh):
    column = list(mesh.devices[0])
    coords = [getattr(d, "coords", None) for d in column]
    if any(c is None for c in coords):
        return 8 if len(column) % 8 == 0 else len(column)
    first = coords[0][0]
    count = 0
    for c in coords:
        if c[0] != first:
            break
        count += 1
    return count if len(column) % count == 0 else len(column)


def solution(mesh):
    in_specs = (
        P(None, "gr", None, None, "gc", None),
        P(None, "gr", "gc", None),
        P("gr", None, "gc", None),
        P(),
        P(),
        P(None, "gr", None, None, "gc", None),
        P(None, "gr", "gc", None),
        P("gr", None, "gc", None),
        P(),
    )
    out_specs = (
        P(None, "gr", None, None, "gc", None),
        P(None, "gr", "gc", None),
        P("gr", None, "gc", None),
        P(),
    )
    return jax.shard_map(
        functools.partial(local, mesh.shape["gc"], mesh.shape["gr"], line_length(mesh)),
        mesh=mesh,
        in_specs=in_specs,
        out_specs=out_specs,
        check_vma=False,
    )
```

```python
import functools

import jax
import jax.numpy as jnp
from jax import lax
from jax.experimental import pallas as pl
from jax.experimental.pallas import tpu as pltpu
from jax.sharding import PartitionSpec as P

MESH_ID = pl.DeviceIdType.MESH


def row_product(left_rows, right_rows):
    return lax.dot_general(
        left_rows, right_rows, (((0,), (0,)), ((), ())), preferred_element_type=jnp.float32
    )


def diag_solve(diag_factor, diag_inverse, diag_reduced):
    highest = lax.Precision.HIGH
    chol_proj = jnp.dot(diag_factor.T, diag_reduced, precision=highest)
    index_row = lax.broadcasted_iota(jnp.int32, chol_proj.shape, 0)
    index_col = lax.broadcasted_iota(jnp.int32, chol_proj.shape, 1)
    phi_lower = jnp.where(
        index_row > index_col,
        chol_proj,
        jnp.where(index_row == index_col, chol_proj - 0.5 * chol_proj, 0.0),
    )
    symmetric = 0.5 * (phi_lower + phi_lower.T)
    left_side = jnp.dot(diag_inverse.T, symmetric, precision=highest)
    return jnp.dot(left_side, diag_inverse, precision=highest)


def by_width(index, rows, width, action):
    group = (rows * (index + 1) - 1) // 128
    for j in range(width // 128):
        @pl.when(group == j)
        def _():
            action(128 * (j + 1))


def gather_kernel(n, line, x_ref, p_ref, out_ref, psum_ref, precv, psems, sems, local_sem):
    me = lax.axis_index("gc")
    row = lax.axis_index("gr")
    rows = x_ref.shape[2]
    lines = n // line
    pos = lax.rem(me, line)
    grp = me // line
    base = grp * line

    def line_peer(k):
        return base + lax.rem(pos + k, line)

    def cross_peer(k):
        return lax.rem(grp + k, lines) * line + pos

    part_rows, part_width = p_ref.shape[1], p_ref.shape[2]
    precv[...] = jnp.zeros(precv.shape, precv.dtype)
    barrier = pltpu.get_barrier_semaphore()

    def greet(k, carry):
        pl.semaphore_signal(barrier, inc=1, device_id=(row, lax.rem(me + k, n)), device_id_type=MESH_ID)
        return carry

    lax.fori_loop(1, n, greet, 0)
    pl.semaphore_wait(barrier, n - 1)

    def part_copy(k, sender, cols):
        peer = lax.rem(me + k, n)
        return pltpu.make_async_remote_copy(
            src_ref=p_ref.at[peer, :, pl.ds(0, cols)],
            dst_ref=precv.at[sender, :, pl.ds(0, cols)],
            send_sem=psems.at[0, k],
            recv_sem=psems.at[1, sender],
            device_id=(row, peer),
            device_id_type=MESH_ID,
        )

    own = pltpu.make_async_copy(x_ref, out_ref.at[:, :, pl.ds(me * rows, rows), :], local_sem)
    own.start()

    def first(k, sender_pos):
        return pltpu.make_async_remote_copy(
            src_ref=x_ref,
            dst_ref=out_ref.at[:, :, pl.ds((base + sender_pos) * rows, rows), :],
            send_sem=sems.at[0, k],
            recv_sem=sems.at[1, sender_pos],
            device_id=(row, line_peer(k)),
            device_id_type=MESH_ID,
        )

    def send_first(k, carry):
        first(k, pos).start()
        return carry

    lax.fori_loop(1, line, send_first, 0)

    def send_parts(k, carry):
        by_width(lax.rem(me + k, n), part_rows, part_width, lambda cols: part_copy(k, me, cols).start())
        return carry

    lax.fori_loop(1, n, send_parts, 0)

    span = line * rows

    def forward(k, block_pos, sender_grp):
        slot = pl.ds((grp * line + block_pos) * rows, rows)
        return pltpu.make_async_remote_copy(
            src_ref=out_ref.at[:, :, slot, :],
            dst_ref=out_ref.at[:, :, slot, :],
            send_sem=sems.at[2 + block_pos, k],
            recv_sem=sems.at[1, line + sender_grp],
            device_id=(row, cross_peer(k)),
            device_id_type=MESH_ID,
        )

    def whole_line(sender_grp):
        return pltpu.make_async_remote_copy(
            src_ref=out_ref.at[:, :, pl.ds(sender_grp * span, span), :],
            dst_ref=out_ref.at[:, :, pl.ds(sender_grp * span, span), :],
            send_sem=sems.at[0, 0],
            recv_sem=sems.at[1, line + sender_grp],
            device_id=(row, cross_peer(1)),
            device_id_type=MESH_ID,
        )

    own.wait()

    def send_own(k, carry):
        forward(k, pos, grp).start()
        return carry

    lax.fori_loop(1, lines, send_own, 0)

    def relay(k, carry):
        sender_pos = lax.rem(pos + line - k, line)
        first(k, sender_pos).wait_recv()

        def out(j, inner):
            forward(j, sender_pos, grp).start()
            return inner

        return lax.fori_loop(1, lines, out, carry)

    lax.fori_loop(1, line, relay, 0)

    def wait_first(k, carry):
        first(k, pos).wait_send()
        return carry

    lax.fori_loop(1, line, wait_first, 0)

    def wait_sent(k, carry):
        def done(j, inner):
            forward(j, k, grp).wait_send()
            return inner

        return lax.fori_loop(1, lines, done, carry)

    lax.fori_loop(0, line, wait_sent, 0)

    def wait_lines(k, carry):
        whole_line(lax.rem(grp + lines - k, lines)).wait_recv()
        return carry

    lax.fori_loop(1, lines, wait_lines, 0)

    precv[me] = p_ref[me]

    def wait_parts(k, carry):
        sender = lax.rem(me + n - k, n)
        by_width(lax.rem(me + k, n), part_rows, part_width, lambda cols: part_copy(k, me, cols).wait_send())
        by_width(me, part_rows, part_width, lambda cols: part_copy(k, sender, cols).wait_recv())
        return carry

    lax.fori_loop(1, n, wait_parts, 0)

    def add_part(j, total):
        return total + precv[j].astype(jnp.float32)

    psum_ref[...] = lax.fori_loop(0, n, add_part, jnp.zeros(psum_ref.shape, jnp.float32))


def gather_gc(block, part, n, line):
    count, tiles, rows, width = block.shape
    vmem = pl.BlockSpec(memory_space=pltpu.VMEM)
    return pl.pallas_call(
        functools.partial(gather_kernel, n, line),
        out_shape=(
            jax.ShapeDtypeStruct((count, tiles, rows * n, width), block.dtype),
            jax.ShapeDtypeStruct(part.shape[1:], jnp.float32),
        ),
        in_specs=[pl.BlockSpec(memory_space=pl.ANY), vmem],
        out_specs=(pl.BlockSpec(memory_space=pl.ANY), vmem),
        scratch_shapes=[
            pltpu.VMEM(part.shape, part.dtype),
            pltpu.SemaphoreType.DMA((2, n)),
            pltpu.SemaphoreType.DMA((2 + line, line + n // line)),
            pltpu.SemaphoreType.DMA,
        ],
        compiler_params=pltpu.CompilerParams(collective_id=0, has_side_effects=True),
    )(block, part)


def reduce_kernel(n, n_gc, crossing_ref, piece_ref, prior_ref, cross_out, prior_out, crossing_out,
                  recv_crossing, recv_piece, prior_slots, cross_slots, sems):
    me = lax.axis_index("gr")
    col = lax.axis_index("gc")
    rows = prior_ref.shape[0]
    piece_rows, piece_width = piece_ref.shape
    cross_slots[...] = jnp.zeros(cross_slots.shape, cross_slots.dtype)

    barrier = pltpu.get_barrier_semaphore()

    def greet_gr(k, carry):
        pl.semaphore_signal(barrier, inc=1, device_id=(lax.rem(me + k, n), col), device_id_type=MESH_ID)
        return carry

    def greet_gc(k, carry):
        pl.semaphore_signal(barrier, inc=1, device_id=(me, lax.rem(col + k, n_gc)), device_id_type=MESH_ID)
        return carry

    lax.fori_loop(1, n, greet_gr, 0)
    lax.fori_loop(1, n_gc, greet_gc, 0)
    pl.semaphore_wait(barrier, n + n_gc - 2)

    def gr_copy(k, sender, src, dst, index):
        return pltpu.make_async_remote_copy(
            src_ref=src,
            dst_ref=dst.at[sender],
            send_sem=sems.at[index, k],
            recv_sem=sems.at[index + 1, sender],
            device_id=(lax.rem(me + k, n), col),
            device_id_type=MESH_ID,
        )

    def crossing_copy(k, sender):
        peer = lax.rem(me + k, n)
        src = crossing_ref.at[pl.ds(pl.multiple_of(peer * rows, rows), rows), :]
        return gr_copy(k, sender, src, recv_crossing, 0)

    def piece_copy(k, sender):
        return gr_copy(k, sender, piece_ref, recv_piece, 2)

    def prior_copy(k, sender):
        return gr_copy(k, sender, prior_ref, prior_slots, 4)

    def cross_copy(k, sender, cols):
        return pltpu.make_async_remote_copy(
            src_ref=cross_slots.at[col, :, pl.ds(0, cols)],
            dst_ref=cross_slots.at[sender, :, pl.ds(0, cols)],
            send_sem=sems.at[6, k],
            recv_sem=sems.at[7, sender],
            device_id=(me, lax.rem(col + k, n_gc)),
            device_id_type=MESH_ID,
        )

    def send_first(k, carry):
        piece_copy(k, me).start()
        crossing_copy(k, me).start()
        prior_copy(k, me).start()
        return carry

    lax.fori_loop(1, n, send_first, 0)
    prior_slots[me] = prior_ref[...]
    recv_piece[me] = piece_ref[...]
    recv_crossing[me] = crossing_ref[pl.ds(pl.multiple_of(me * rows, rows), rows), :]

    def wait_first(k, carry):
        piece_copy(k, me).wait_send()
        piece_copy(k, lax.rem(me + n - k, n)).wait_recv()
        return carry

    lax.fori_loop(1, n, wait_first, 0)

    def add_piece(j, total):
        return total + recv_piece[j]

    piece = lax.fori_loop(0, n, add_piece, jnp.zeros(piece_ref.shape, jnp.float32))
    cross_slots[col] = piece.astype(cross_slots.dtype)

    def send_second(k, carry):
        by_width(col, piece_rows, piece_width, lambda cols: cross_copy(k, col, cols).start())
        return carry

    lax.fori_loop(1, n_gc, send_second, 0)

    def wait_crossing(k, carry):
        crossing_copy(k, me).wait_send()
        crossing_copy(k, lax.rem(me + n - k, n)).wait_recv()
        return carry

    lax.fori_loop(1, n, wait_crossing, 0)

    def add_crossing(j, total):
        return total + recv_crossing[j].astype(jnp.float32)

    crossing_out[...] = lax.fori_loop(0, n, add_crossing, jnp.zeros(crossing_out.shape, jnp.float32))

    def wait_second(k, carry):
        sender = lax.rem(col + n_gc - k, n_gc)
        by_width(col, piece_rows, piece_width, lambda cols: cross_copy(k, col, cols).wait_send())
        by_width(sender, piece_rows, piece_width, lambda cols: cross_copy(k, sender, cols).wait_recv())
        return carry

    lax.fori_loop(1, n_gc, wait_second, 0)

    def wait_prior(k, carry):
        prior_copy(k, me).wait_send()
        prior_copy(k, lax.rem(me + n - k, n)).wait_recv()
        return carry

    lax.fori_loop(1, n, wait_prior, 0)
    cross_out[...] = cross_slots[...]
    prior_out[...] = prior_slots[...]


def reduce_gr(crossing_part, piece, prior_rows, n, n_gc):
    rows, cols = prior_rows.shape
    vmem = pl.BlockSpec(memory_space=pltpu.VMEM)
    return pl.pallas_call(
        functools.partial(reduce_kernel, n, n_gc),
        out_shape=(
            jax.ShapeDtypeStruct((n_gc,) + piece.shape, jnp.bfloat16),
            jax.ShapeDtypeStruct((n, rows, cols), prior_rows.dtype),
            jax.ShapeDtypeStruct((rows, cols), jnp.float32),
        ),
        in_specs=[vmem, vmem, vmem],
        out_specs=(vmem, vmem, vmem),
        scratch_shapes=[
            pltpu.VMEM((n, rows, cols), crossing_part.dtype),
            pltpu.VMEM((n,) + piece.shape, jnp.float32),
            pltpu.VMEM((n, rows, cols), prior_rows.dtype),
            pltpu.VMEM((n_gc,) + piece.shape, jnp.bfloat16),
            pltpu.SemaphoreType.DMA((8, max(n, n_gc))),
        ],
        compiler_params=pltpu.CompilerParams(collective_id=1, has_side_effects=True),
    )(crossing_part, piece, prior_rows)


def prior_factor_rows(prior_rows, below_shape):
    return prior_rows.reshape(-1, below_shape[3], below_shape[5])


def local(
    n_gc,
    n_gr,
    line,
    below_factor,
    panel_factor,
    prior_factor,
    diag_factor,
    diag_inverse,
    below_adjoint,
    panel_adjoint,
    prior_adjoint,
    diag_adjoint,
):
    tile_count = below_factor.shape[0]
    tile_rows = below_factor.shape[2]
    local_rows = tile_count * tile_rows
    local_cols = below_factor.shape[3] * below_factor.shape[5]
    own_rows = panel_factor.shape[2]
    width = panel_factor.shape[3]
    prior_local = prior_factor.shape[0]
    below_mat = below_factor.reshape(local_rows, local_cols)
    below_bar = below_adjoint.reshape(local_rows, local_cols)
    inverse_bf = diag_inverse.astype(jnp.bfloat16)
    own_grad = jnp.dot(
        panel_adjoint.reshape(tile_count * own_rows, width),
        inverse_bf,
        preferred_element_type=jnp.float32,
    ).astype(jnp.bfloat16)
    panel_grad = own_grad.reshape(panel_adjoint.shape)
    own_factor = panel_factor.reshape(tile_count * own_rows, width)
    own_part = row_product(own_grad, own_factor).astype(jnp.bfloat16)
    whole, piece = gather_gc(
        own_grad.reshape(1, tile_count, own_rows, width),
        own_part.reshape(n_gc, width // n_gc, width),
        n_gc,
        line,
    )
    grad_rows = whole[0].reshape(local_rows, width)
    prior_here = prior_factor.reshape(prior_local, local_cols)
    crossing_part = row_product(grad_rows, below_mat).astype(jnp.bfloat16)
    cross_rows, prior_rows, crossing = reduce_gr(crossing_part, piece, prior_here, n_gr, n_gc)
    summed = cross_rows.reshape(width, width).astype(jnp.float32)
    prior_whole = prior_rows.reshape(width, local_cols)
    diag_reduced = jnp.tril(diag_adjoint - summed)
    diag_gradient = diag_solve(diag_factor, diag_inverse, diag_reduced)
    below_prod = lax.dot_general(
        grad_rows.reshape(tile_count, tile_rows, width),
        prior_factor_rows(prior_rows, below_factor.shape),
        (((2,), (0,)), ((), ())),
        preferred_element_type=jnp.float32,
    ).reshape(below_adjoint.shape)
    below_new = (below_adjoint.astype(jnp.float32) - below_prod).astype(jnp.bfloat16)
    grid_row = lax.axis_index("gr")
    twice_rows = lax.dynamic_slice_in_dim(
        2.0 * diag_gradient, grid_row * prior_local, prior_local, 0
    ).astype(jnp.bfloat16)
    curvature = jnp.dot(twice_rows, prior_whole, preferred_element_type=jnp.float32)
    prior_bar = prior_adjoint.reshape(prior_local, local_cols).astype(jnp.float32)
    prior_new = (prior_bar - crossing - curvature).astype(jnp.bfloat16)
    return (
        below_new,
        panel_grad,
        prior_new.reshape(prior_adjoint.shape),
        diag_gradient,
    )


def line_length(mesh):
    column = list(mesh.devices[0])
    coords = [getattr(d, "coords", None) for d in column]
    if any(c is None for c in coords):
        return 8 if len(column) % 8 == 0 else len(column)
    first = coords[0][0]
    count = 0
    for c in coords:
        if c[0] != first:
            break
        count += 1
    return count if len(column) % count == 0 else len(column)


def solution(mesh):
    in_specs = (
        P(None, "gr", None, None, "gc", None),
        P(None, "gr", "gc", None),
        P("gr", None, "gc", None),
        P(),
        P(),
        P(None, "gr", None, None, "gc", None),
        P(None, "gr", "gc", None),
        P("gr", None, "gc", None),
        P(),
    )
    out_specs = (
        P(None, "gr", None, None, "gc", None),
        P(None, "gr", "gc", None),
        P("gr", None, "gc", None),
        P(),
    )
    return jax.shard_map(
        functools.partial(local, mesh.shape["gc"], mesh.shape["gr"], line_length(mesh)),
        mesh=mesh,
        in_specs=in_specs,
        out_specs=out_specs,
        check_vma=False,
    )
```

```python
import functools

import jax
import jax.numpy as jnp
from jax import lax
from jax.experimental import pallas as pl
from jax.experimental.pallas import tpu as pltpu
from jax.sharding import PartitionSpec as P

MESH_ID = pl.DeviceIdType.MESH


def row_product(left_rows, right_rows):
    return lax.dot_general(
        left_rows, right_rows, (((0,), (0,)), ((), ())), preferred_element_type=jnp.float32
    )


def diag_solve(diag_factor, diag_inverse, diag_reduced):
    highest = lax.Precision.HIGH
    chol_proj = jnp.dot(diag_factor.T, diag_reduced, precision=highest)
    index_row = lax.broadcasted_iota(jnp.int32, chol_proj.shape, 0)
    index_col = lax.broadcasted_iota(jnp.int32, chol_proj.shape, 1)
    phi_lower = jnp.where(
        index_row > index_col,
        chol_proj,
        jnp.where(index_row == index_col, chol_proj - 0.5 * chol_proj, 0.0),
    )
    symmetric = 0.5 * (phi_lower + phi_lower.T)
    left_side = jnp.dot(diag_inverse.T, symmetric, precision=highest)
    return jnp.dot(left_side, diag_inverse, precision=highest)


def by_width(index, rows, width, action):
    group = (rows * (index + 1) - 1) // 128
    for j in range(width // 128):
        @pl.when(group == j)
        def _():
            action(128 * (j + 1))


def gather_kernel(n, line, x_ref, p_ref, out_ref, psum_ref, precv, psems, sems, local_sem):
    me = lax.axis_index("gc")
    row = lax.axis_index("gr")
    rows = x_ref.shape[2]
    lines = n // line
    pos = lax.rem(me, line)
    grp = me // line
    base = grp * line

    def line_peer(k):
        return base + lax.rem(pos + k, line)

    def cross_peer(k):
        return lax.rem(grp + k, lines) * line + pos

    part_rows, part_width = p_ref.shape[1], p_ref.shape[2]
    precv[...] = jnp.zeros(precv.shape, precv.dtype)
    barrier = pltpu.get_barrier_semaphore()

    def greet(k, carry):
        pl.semaphore_signal(barrier, inc=1, device_id=(row, lax.rem(me + k, n)), device_id_type=MESH_ID)
        return carry

    lax.fori_loop(1, n, greet, 0)
    pl.semaphore_wait(barrier, n - 1)

    def part_copy(k, sender, cols):
        peer = lax.rem(me + k, n)
        return pltpu.make_async_remote_copy(
            src_ref=p_ref.at[peer, :, pl.ds(0, cols)],
            dst_ref=precv.at[sender, :, pl.ds(0, cols)],
            send_sem=psems.at[0, k],
            recv_sem=psems.at[1, sender],
            device_id=(row, peer),
            device_id_type=MESH_ID,
        )

    own = pltpu.make_async_copy(x_ref, out_ref.at[:, :, pl.ds(me * rows, rows), :], local_sem)
    own.start()

    def first(k, sender_pos):
        return pltpu.make_async_remote_copy(
            src_ref=x_ref,
            dst_ref=out_ref.at[:, :, pl.ds((base + sender_pos) * rows, rows), :],
            send_sem=sems.at[0, k],
            recv_sem=sems.at[1, sender_pos],
            device_id=(row, line_peer(k)),
            device_id_type=MESH_ID,
        )

    def send_first(k, carry):
        first(k, pos).start()
        return carry

    lax.fori_loop(1, line, send_first, 0)

    def send_parts(k, carry):
        by_width(lax.rem(me + k, n), part_rows, part_width, lambda cols: part_copy(k, me, cols).start())
        return carry

    lax.fori_loop(1, n, send_parts, 0)

    span = line * rows

    def forward(k, block_pos, sender_grp):
        slot = pl.ds((grp * line + block_pos) * rows, rows)
        return pltpu.make_async_remote_copy(
            src_ref=out_ref.at[:, :, slot, :],
            dst_ref=out_ref.at[:, :, slot, :],
            send_sem=sems.at[2 + block_pos, k],
            recv_sem=sems.at[1, line + sender_grp],
            device_id=(row, cross_peer(k)),
            device_id_type=MESH_ID,
        )

    def whole_line(sender_grp):
        return pltpu.make_async_remote_copy(
            src_ref=out_ref.at[:, :, pl.ds(sender_grp * span, span), :],
            dst_ref=out_ref.at[:, :, pl.ds(sender_grp * span, span), :],
            send_sem=sems.at[0, 0],
            recv_sem=sems.at[1, line + sender_grp],
            device_id=(row, cross_peer(1)),
            device_id_type=MESH_ID,
        )

    own.wait()

    def send_own(k, carry):
        forward(k, pos, grp).start()
        return carry

    lax.fori_loop(1, lines, send_own, 0)

    def relay(k, carry):
        sender_pos = lax.rem(pos + line - k, line)
        first(k, sender_pos).wait_recv()

        def out(j, inner):
            forward(j, sender_pos, grp).start()
            return inner

        return lax.fori_loop(1, lines, out, carry)

    lax.fori_loop(1, line, relay, 0)

    def wait_first(k, carry):
        first(k, pos).wait_send()
        return carry

    lax.fori_loop(1, line, wait_first, 0)

    def wait_sent(k, carry):
        def done(j, inner):
            forward(j, k, grp).wait_send()
            return inner

        return lax.fori_loop(1, lines, done, carry)

    lax.fori_loop(0, line, wait_sent, 0)

    def wait_lines(k, carry):
        whole_line(lax.rem(grp + lines - k, lines)).wait_recv()
        return carry

    lax.fori_loop(1, lines, wait_lines, 0)

    precv[me] = p_ref[me]

    def wait_parts(k, carry):
        sender = lax.rem(me + n - k, n)
        by_width(lax.rem(me + k, n), part_rows, part_width, lambda cols: part_copy(k, me, cols).wait_send())
        by_width(me, part_rows, part_width, lambda cols: part_copy(k, sender, cols).wait_recv())
        return carry

    lax.fori_loop(1, n, wait_parts, 0)

    def add_part(j, total):
        return total + precv[j].astype(jnp.float32)

    psum_ref[...] = lax.fori_loop(0, n, add_part, jnp.zeros(psum_ref.shape, jnp.float32))


def gather_gc(block, part, n, line):
    count, tiles, rows, width = block.shape
    vmem = pl.BlockSpec(memory_space=pltpu.VMEM)
    return pl.pallas_call(
        functools.partial(gather_kernel, n, line),
        out_shape=(
            jax.ShapeDtypeStruct((count, tiles, rows * n, width), block.dtype),
            jax.ShapeDtypeStruct(part.shape[1:], jnp.float32),
        ),
        in_specs=[pl.BlockSpec(memory_space=pl.ANY), vmem],
        out_specs=(pl.BlockSpec(memory_space=pl.ANY), vmem),
        scratch_shapes=[
            pltpu.VMEM(part.shape, part.dtype),
            pltpu.SemaphoreType.DMA((2, n)),
            pltpu.SemaphoreType.DMA((2 + line, line + n // line)),
            pltpu.SemaphoreType.DMA,
        ],
        compiler_params=pltpu.CompilerParams(collective_id=0, has_side_effects=True),
    )(block, part)


def reduce_kernel(n, n_gc, crossing_ref, piece_ref, prior_ref, cross_out, prior_out, crossing_out,
                  recv_crossing, recv_piece, prior_slots, cross_slots, sems):
    me = lax.axis_index("gr")
    col = lax.axis_index("gc")
    rows = prior_ref.shape[0]
    piece_rows, piece_width = piece_ref.shape
    cross_slots[...] = jnp.zeros(cross_slots.shape, cross_slots.dtype)
    recv_piece[...] = jnp.zeros(recv_piece.shape, recv_piece.dtype)

    barrier = pltpu.get_barrier_semaphore()

    def greet_gr(k, carry):
        pl.semaphore_signal(barrier, inc=1, device_id=(lax.rem(me + k, n), col), device_id_type=MESH_ID)
        return carry

    def greet_gc(k, carry):
        pl.semaphore_signal(barrier, inc=1, device_id=(me, lax.rem(col + k, n_gc)), device_id_type=MESH_ID)
        return carry

    lax.fori_loop(1, n, greet_gr, 0)
    lax.fori_loop(1, n_gc, greet_gc, 0)
    pl.semaphore_wait(barrier, n + n_gc - 2)

    def gr_copy(k, sender, src, dst, index):
        return pltpu.make_async_remote_copy(
            src_ref=src,
            dst_ref=dst.at[sender],
            send_sem=sems.at[index, k],
            recv_sem=sems.at[index + 1, sender],
            device_id=(lax.rem(me + k, n), col),
            device_id_type=MESH_ID,
        )

    def crossing_copy(k, sender):
        peer = lax.rem(me + k, n)
        src = crossing_ref.at[pl.ds(pl.multiple_of(peer * rows, rows), rows), :]
        return gr_copy(k, sender, src, recv_crossing, 0)

    def piece_copy(k, sender, cols):
        return pltpu.make_async_remote_copy(
            src_ref=piece_ref.at[:, pl.ds(0, cols)],
            dst_ref=recv_piece.at[sender, :, pl.ds(0, cols)],
            send_sem=sems.at[2, k],
            recv_sem=sems.at[3, sender],
            device_id=(lax.rem(me + k, n), col),
            device_id_type=MESH_ID,
        )

    def prior_copy(k, sender):
        return gr_copy(k, sender, prior_ref, prior_slots, 4)

    def cross_copy(k, sender, cols):
        return pltpu.make_async_remote_copy(
            src_ref=cross_slots.at[col, :, pl.ds(0, cols)],
            dst_ref=cross_slots.at[sender, :, pl.ds(0, cols)],
            send_sem=sems.at[6, k],
            recv_sem=sems.at[7, sender],
            device_id=(me, lax.rem(col + k, n_gc)),
            device_id_type=MESH_ID,
        )

    def send_first(k, carry):
        by_width(col, piece_rows, piece_width, lambda cols: piece_copy(k, me, cols).start())
        return carry

    def send_rest(k, carry):
        crossing_copy(k, me).start()
        prior_copy(k, me).start()
        return carry

    lax.fori_loop(1, n, send_first, 0)
    prior_slots[me] = prior_ref[...]
    recv_piece[me] = piece_ref[...]
    recv_crossing[me] = crossing_ref[pl.ds(pl.multiple_of(me * rows, rows), rows), :]

    def wait_first(k, carry):
        sender = lax.rem(me + n - k, n)
        by_width(col, piece_rows, piece_width, lambda cols: piece_copy(k, me, cols).wait_send())
        by_width(col, piece_rows, piece_width, lambda cols: piece_copy(k, sender, cols).wait_recv())
        return carry

    lax.fori_loop(1, n, wait_first, 0)

    def add_piece(j, total):
        return total + recv_piece[j]

    piece = lax.fori_loop(0, n, add_piece, jnp.zeros(piece_ref.shape, jnp.float32))
    cross_slots[col] = piece.astype(cross_slots.dtype)

    def send_second(k, carry):
        by_width(col, piece_rows, piece_width, lambda cols: cross_copy(k, col, cols).start())
        return carry

    lax.fori_loop(1, n_gc, send_second, 0)
    lax.fori_loop(1, n, send_rest, 0)

    def wait_crossing(k, carry):
        crossing_copy(k, me).wait_send()
        crossing_copy(k, lax.rem(me + n - k, n)).wait_recv()
        return carry

    lax.fori_loop(1, n, wait_crossing, 0)

    def add_crossing(j, total):
        return total + recv_crossing[j].astype(jnp.float32)

    crossing_out[...] = lax.fori_loop(0, n, add_crossing, jnp.zeros(crossing_out.shape, jnp.float32))

    def wait_second(k, carry):
        sender = lax.rem(col + n_gc - k, n_gc)
        by_width(col, piece_rows, piece_width, lambda cols: cross_copy(k, col, cols).wait_send())
        by_width(sender, piece_rows, piece_width, lambda cols: cross_copy(k, sender, cols).wait_recv())
        return carry

    lax.fori_loop(1, n_gc, wait_second, 0)

    def wait_prior(k, carry):
        prior_copy(k, me).wait_send()
        prior_copy(k, lax.rem(me + n - k, n)).wait_recv()
        return carry

    lax.fori_loop(1, n, wait_prior, 0)
    cross_out[...] = cross_slots[...]
    prior_out[...] = prior_slots[...]


def reduce_gr(crossing_part, piece, prior_rows, n, n_gc):
    rows, cols = prior_rows.shape
    vmem = pl.BlockSpec(memory_space=pltpu.VMEM)
    return pl.pallas_call(
        functools.partial(reduce_kernel, n, n_gc),
        out_shape=(
            jax.ShapeDtypeStruct((n_gc,) + piece.shape, jnp.bfloat16),
            jax.ShapeDtypeStruct((n, rows, cols), prior_rows.dtype),
            jax.ShapeDtypeStruct((rows, cols), jnp.float32),
        ),
        in_specs=[vmem, vmem, vmem],
        out_specs=(vmem, vmem, vmem),
        scratch_shapes=[
            pltpu.VMEM((n, rows, cols), crossing_part.dtype),
            pltpu.VMEM((n,) + piece.shape, jnp.float32),
            pltpu.VMEM((n, rows, cols), prior_rows.dtype),
            pltpu.VMEM((n_gc,) + piece.shape, jnp.bfloat16),
            pltpu.SemaphoreType.DMA((8, max(n, n_gc))),
        ],
        compiler_params=pltpu.CompilerParams(collective_id=1, has_side_effects=True),
    )(crossing_part, piece, prior_rows)


def prior_factor_rows(prior_rows, below_shape):
    return prior_rows.reshape(-1, below_shape[3], below_shape[5])


def local(
    n_gc,
    n_gr,
    line,
    below_factor,
    panel_factor,
    prior_factor,
    diag_factor,
    diag_inverse,
    below_adjoint,
    panel_adjoint,
    prior_adjoint,
    diag_adjoint,
):
    tile_count = below_factor.shape[0]
    tile_rows = below_factor.shape[2]
    local_rows = tile_count * tile_rows
    local_cols = below_factor.shape[3] * below_factor.shape[5]
    own_rows = panel_factor.shape[2]
    width = panel_factor.shape[3]
    prior_local = prior_factor.shape[0]
    below_mat = below_factor.reshape(local_rows, local_cols)
    below_bar = below_adjoint.reshape(local_rows, local_cols)
    inverse_bf = diag_inverse.astype(jnp.bfloat16)
    own_grad = jnp.dot(
        panel_adjoint.reshape(tile_count * own_rows, width),
        inverse_bf,
        preferred_element_type=jnp.float32,
    ).astype(jnp.bfloat16)
    panel_grad = own_grad.reshape(panel_adjoint.shape)
    own_factor = panel_factor.reshape(tile_count * own_rows, width)
    own_part = row_product(own_grad, own_factor).astype(jnp.bfloat16)
    whole, piece = gather_gc(
        own_grad.reshape(1, tile_count, own_rows, width),
        own_part.reshape(n_gc, width // n_gc, width),
        n_gc,
        line,
    )
    grad_rows = whole[0].reshape(local_rows, width)
    prior_here = prior_factor.reshape(prior_local, local_cols)
    crossing_part = row_product(grad_rows, below_mat).astype(jnp.bfloat16)
    cross_rows, prior_rows, crossing = reduce_gr(crossing_part, piece, prior_here, n_gr, n_gc)
    summed = cross_rows.reshape(width, width).astype(jnp.float32)
    prior_whole = prior_rows.reshape(width, local_cols)
    diag_reduced = jnp.tril(diag_adjoint - summed)
    diag_gradient = diag_solve(diag_factor, diag_inverse, diag_reduced)
    below_prod = lax.dot_general(
        grad_rows.reshape(tile_count, tile_rows, width),
        prior_factor_rows(prior_rows, below_factor.shape),
        (((2,), (0,)), ((), ())),
        preferred_element_type=jnp.float32,
    ).reshape(below_adjoint.shape)
    below_new = (below_adjoint.astype(jnp.float32) - below_prod).astype(jnp.bfloat16)
    grid_row = lax.axis_index("gr")
    twice_rows = lax.dynamic_slice_in_dim(
        2.0 * diag_gradient, grid_row * prior_local, prior_local, 0
    ).astype(jnp.bfloat16)
    curvature = jnp.dot(twice_rows, prior_whole, preferred_element_type=jnp.float32)
    prior_bar = prior_adjoint.reshape(prior_local, local_cols).astype(jnp.float32)
    prior_new = (prior_bar - crossing - curvature).astype(jnp.bfloat16)
    return (
        below_new,
        panel_grad,
        prior_new.reshape(prior_adjoint.shape),
        diag_gradient,
    )


def line_length(mesh):
    column = list(mesh.devices[0])
    coords = [getattr(d, "coords", None) for d in column]
    if any(c is None for c in coords):
        return 8 if len(column) % 8 == 0 else len(column)
    first = coords[0][0]
    count = 0
    for c in coords:
        if c[0] != first:
            break
        count += 1
    return count if len(column) % count == 0 else len(column)


def solution(mesh):
    in_specs = (
        P(None, "gr", None, None, "gc", None),
        P(None, "gr", "gc", None),
        P("gr", None, "gc", None),
        P(),
        P(),
        P(None, "gr", None, None, "gc", None),
        P(None, "gr", "gc", None),
        P("gr", None, "gc", None),
        P(),
    )
    out_specs = (
        P(None, "gr", None, None, "gc", None),
        P(None, "gr", "gc", None),
        P("gr", None, "gc", None),
        P(),
    )
    return jax.shard_map(
        functools.partial(local, mesh.shape["gc"], mesh.shape["gr"], line_length(mesh)),
        mesh=mesh,
        in_specs=in_specs,
        out_specs=out_specs,
        check_vma=False,
    )
```

```python
import functools

import jax
import jax.numpy as jnp
from jax import lax
from jax.experimental import pallas as pl
from jax.experimental.pallas import tpu as pltpu
from jax.sharding import PartitionSpec as P

MESH_ID = pl.DeviceIdType.MESH


def row_product(left_rows, right_rows):
    return lax.dot_general(
        left_rows, right_rows, (((0,), (0,)), ((), ())), preferred_element_type=jnp.float32
    )


def diag_solve(diag_factor, diag_inverse, diag_reduced):
    highest = lax.Precision.HIGH
    chol_proj = jnp.dot(diag_factor.T, diag_reduced, precision=highest)
    index_row = lax.broadcasted_iota(jnp.int32, chol_proj.shape, 0)
    index_col = lax.broadcasted_iota(jnp.int32, chol_proj.shape, 1)
    phi_lower = jnp.where(
        index_row > index_col,
        chol_proj,
        jnp.where(index_row == index_col, chol_proj - 0.5 * chol_proj, 0.0),
    )
    symmetric = 0.5 * (phi_lower + phi_lower.T)
    left_side = jnp.dot(diag_inverse.T, symmetric, precision=highest)
    return jnp.dot(left_side, diag_inverse, precision=highest)


def by_width(index, rows, width, action):
    group = (rows * (index + 1) - 1) // 128
    for j in range(width // 128):
        @pl.when(group == j)
        def _():
            action(128 * (j + 1))


def gather_kernel(n, line, x_ref, p_ref, out_ref, psum_ref, precv, psems, sems, local_sem):
    me = lax.axis_index("gc")
    row = lax.axis_index("gr")
    rows = x_ref.shape[2]
    lines = n // line
    pos = lax.rem(me, line)
    grp = me // line
    base = grp * line

    def line_peer(k):
        return base + lax.rem(pos + k, line)

    def cross_peer(k):
        return lax.rem(grp + k, lines) * line + pos

    part_rows, part_width = p_ref.shape[1], p_ref.shape[2]
    precv[...] = jnp.zeros(precv.shape, precv.dtype)
    barrier = pltpu.get_barrier_semaphore()

    def greet(k, carry):
        pl.semaphore_signal(barrier, inc=1, device_id=(row, lax.rem(me + k, n)), device_id_type=MESH_ID)
        return carry

    lax.fori_loop(1, n, greet, 0)
    pl.semaphore_wait(barrier, n - 1)

    def part_copy(k, sender, cols):
        peer = lax.rem(me + k, n)
        return pltpu.make_async_remote_copy(
            src_ref=p_ref.at[peer, :, pl.ds(0, cols)],
            dst_ref=precv.at[sender, :, pl.ds(0, cols)],
            send_sem=psems.at[0, k],
            recv_sem=psems.at[1, sender],
            device_id=(row, peer),
            device_id_type=MESH_ID,
        )

    own = pltpu.make_async_copy(x_ref, out_ref.at[:, :, pl.ds(me * rows, rows), :], local_sem)
    own.start()

    def first(k, sender_pos):
        return pltpu.make_async_remote_copy(
            src_ref=x_ref,
            dst_ref=out_ref.at[:, :, pl.ds((base + sender_pos) * rows, rows), :],
            send_sem=sems.at[0, k],
            recv_sem=sems.at[1, sender_pos],
            device_id=(row, line_peer(k)),
            device_id_type=MESH_ID,
        )

    def send_first(k, carry):
        first(k, pos).start()
        return carry

    lax.fori_loop(1, line, send_first, 0)

    def send_parts(k, carry):
        by_width(lax.rem(me + k, n), part_rows, part_width, lambda cols: part_copy(k, me, cols).start())
        return carry

    lax.fori_loop(1, n, send_parts, 0)

    span = line * rows

    def forward(k, block_pos, sender_grp):
        slot = pl.ds((grp * line + block_pos) * rows, rows)
        return pltpu.make_async_remote_copy(
            src_ref=out_ref.at[:, :, slot, :],
            dst_ref=out_ref.at[:, :, slot, :],
            send_sem=sems.at[2 + block_pos, k],
            recv_sem=sems.at[1, line + sender_grp],
            device_id=(row, cross_peer(k)),
            device_id_type=MESH_ID,
        )

    def whole_line(sender_grp):
        return pltpu.make_async_remote_copy(
            src_ref=out_ref.at[:, :, pl.ds(sender_grp * span, span), :],
            dst_ref=out_ref.at[:, :, pl.ds(sender_grp * span, span), :],
            send_sem=sems.at[0, 0],
            recv_sem=sems.at[1, line + sender_grp],
            device_id=(row, cross_peer(1)),
            device_id_type=MESH_ID,
        )

    own.wait()

    def send_own(k, carry):
        forward(k, pos, grp).start()
        return carry

    lax.fori_loop(1, lines, send_own, 0)

    def relay(k, carry):
        sender_pos = lax.rem(pos + line - k, line)
        first(k, sender_pos).wait_recv()

        def out(j, inner):
            forward(j, sender_pos, grp).start()
            return inner

        return lax.fori_loop(1, lines, out, carry)

    lax.fori_loop(1, line, relay, 0)

    def wait_first(k, carry):
        first(k, pos).wait_send()
        return carry

    lax.fori_loop(1, line, wait_first, 0)

    def wait_sent(k, carry):
        def done(j, inner):
            forward(j, k, grp).wait_send()
            return inner

        return lax.fori_loop(1, lines, done, carry)

    lax.fori_loop(0, line, wait_sent, 0)

    def wait_lines(k, carry):
        whole_line(lax.rem(grp + lines - k, lines)).wait_recv()
        return carry

    lax.fori_loop(1, lines, wait_lines, 0)

    precv[me] = p_ref[me]

    def wait_parts(k, carry):
        sender = lax.rem(me + n - k, n)
        by_width(lax.rem(me + k, n), part_rows, part_width, lambda cols: part_copy(k, me, cols).wait_send())
        by_width(me, part_rows, part_width, lambda cols: part_copy(k, sender, cols).wait_recv())
        return carry

    lax.fori_loop(1, n, wait_parts, 0)

    def add_part(j, total):
        return total + precv[j].astype(jnp.float32)

    psum_ref[...] = lax.fori_loop(0, n, add_part, jnp.zeros(psum_ref.shape, jnp.float32))


def gather_gc(block, part, n, line):
    count, tiles, rows, width = block.shape
    vmem = pl.BlockSpec(memory_space=pltpu.VMEM)
    return pl.pallas_call(
        functools.partial(gather_kernel, n, line),
        out_shape=(
            jax.ShapeDtypeStruct((count, tiles, rows * n, width), block.dtype),
            jax.ShapeDtypeStruct(part.shape[1:], jnp.float32),
        ),
        in_specs=[pl.BlockSpec(memory_space=pl.ANY), vmem],
        out_specs=(pl.BlockSpec(memory_space=pl.ANY), vmem),
        scratch_shapes=[
            pltpu.VMEM(part.shape, part.dtype),
            pltpu.SemaphoreType.DMA((2, n)),
            pltpu.SemaphoreType.DMA((2 + line, line + n // line)),
            pltpu.SemaphoreType.DMA,
        ],
        compiler_params=pltpu.CompilerParams(collective_id=0, has_side_effects=True),
    )(block, part)


def reduce_kernel(n, n_gc, crossing_ref, piece_ref, prior_ref, cross_out, prior_out, crossing_out,
                  recv_crossing, recv_piece, prior_slots, cross_slots, sems):
    me = lax.axis_index("gr")
    col = lax.axis_index("gc")
    rows = prior_ref.shape[0]
    piece_rows, piece_width = piece_ref.shape
    cross_slots[...] = jnp.zeros(cross_slots.shape, cross_slots.dtype)
    recv_piece[...] = jnp.zeros(recv_piece.shape, recv_piece.dtype)

    barrier = pltpu.get_barrier_semaphore()

    def greet_gr(k, carry):
        pl.semaphore_signal(barrier, inc=1, device_id=(lax.rem(me + k, n), col), device_id_type=MESH_ID)
        return carry

    def greet_gc(k, carry):
        pl.semaphore_signal(barrier, inc=1, device_id=(me, lax.rem(col + k, n_gc)), device_id_type=MESH_ID)
        return carry

    lax.fori_loop(1, n, greet_gr, 0)
    lax.fori_loop(1, n_gc, greet_gc, 0)
    pl.semaphore_wait(barrier, n + n_gc - 2)

    def gr_copy(k, sender, src, dst, index):
        return pltpu.make_async_remote_copy(
            src_ref=src,
            dst_ref=dst.at[sender],
            send_sem=sems.at[index, k],
            recv_sem=sems.at[index + 1, sender],
            device_id=(lax.rem(me + k, n), col),
            device_id_type=MESH_ID,
        )

    def crossing_copy(k, sender):
        peer = lax.rem(me + k, n)
        src = crossing_ref.at[pl.ds(pl.multiple_of(peer * rows, rows), rows), :]
        return gr_copy(k, sender, src, recv_crossing, 0)

    def piece_copy(k, sender, cols):
        return pltpu.make_async_remote_copy(
            src_ref=piece_ref.at[:, pl.ds(0, cols)],
            dst_ref=recv_piece.at[sender, :, pl.ds(0, cols)],
            send_sem=sems.at[2, k],
            recv_sem=sems.at[3, sender],
            device_id=(lax.rem(me + k, n), col),
            device_id_type=MESH_ID,
        )

    def prior_copy(k, sender):
        return gr_copy(k, sender, prior_ref, prior_slots, 4)

    def cross_copy(k, sender, cols):
        return pltpu.make_async_remote_copy(
            src_ref=cross_slots.at[col, :, pl.ds(0, cols)],
            dst_ref=cross_slots.at[sender, :, pl.ds(0, cols)],
            send_sem=sems.at[6, k],
            recv_sem=sems.at[7, sender],
            device_id=(me, lax.rem(col + k, n_gc)),
            device_id_type=MESH_ID,
        )

    def send_first(k, carry):
        by_width(col, piece_rows, piece_width, lambda cols: piece_copy(k, me, cols).start())
        return carry

    def send_rest(k, carry):
        crossing_copy(k, me).start()
        prior_copy(k, me).start()
        return carry

    lax.fori_loop(1, n, send_first, 0)
    prior_slots[me] = prior_ref[...]
    recv_piece[me] = piece_ref[...]
    recv_crossing[me] = crossing_ref[pl.ds(pl.multiple_of(me * rows, rows), rows), :]

    def wait_first(k, carry):
        sender = lax.rem(me + n - k, n)
        by_width(col, piece_rows, piece_width, lambda cols: piece_copy(k, me, cols).wait_send())
        by_width(col, piece_rows, piece_width, lambda cols: piece_copy(k, sender, cols).wait_recv())
        return carry

    lax.fori_loop(1, n, wait_first, 0)

    def add_piece(j, total):
        return total + recv_piece[j]

    piece = lax.fori_loop(0, n, add_piece, jnp.zeros(piece_ref.shape, jnp.float32))
    cross_slots[col] = piece.astype(cross_slots.dtype)

    def send_second(k, carry):
        by_width(col, piece_rows, piece_width, lambda cols: cross_copy(k, col, cols).start())
        return carry

    lax.fori_loop(1, n_gc, send_second, 0)
    lax.fori_loop(1, n, send_rest, 0)

    def wait_crossing(k, carry):
        crossing_copy(k, me).wait_send()
        crossing_copy(k, lax.rem(me + n - k, n)).wait_recv()
        return carry

    lax.fori_loop(1, n, wait_crossing, 0)

    def add_crossing(j, total):
        return total + recv_crossing[j].astype(jnp.float32)

    crossing_out[...] = lax.fori_loop(0, n, add_crossing, jnp.zeros(crossing_out.shape, jnp.float32))

    def wait_second(k, carry):
        sender = lax.rem(col + n_gc - k, n_gc)
        by_width(col, piece_rows, piece_width, lambda cols: cross_copy(k, col, cols).wait_send())
        by_width(sender, piece_rows, piece_width, lambda cols: cross_copy(k, sender, cols).wait_recv())
        return carry

    lax.fori_loop(1, n_gc, wait_second, 0)

    def wait_prior(k, carry):
        prior_copy(k, me).wait_send()
        prior_copy(k, lax.rem(me + n - k, n)).wait_recv()
        return carry

    lax.fori_loop(1, n, wait_prior, 0)
    cross_out[...] = cross_slots[...]
    prior_out[...] = prior_slots[...]


def reduce_gr(crossing_part, piece, prior_rows, n, n_gc):
    rows, cols = prior_rows.shape
    vmem = pl.BlockSpec(memory_space=pltpu.VMEM)
    return pl.pallas_call(
        functools.partial(reduce_kernel, n, n_gc),
        out_shape=(
            jax.ShapeDtypeStruct((n_gc,) + piece.shape, jnp.bfloat16),
            jax.ShapeDtypeStruct((n, rows, cols), prior_rows.dtype),
            jax.ShapeDtypeStruct((rows, cols), jnp.float32),
        ),
        in_specs=[vmem, vmem, vmem],
        out_specs=(vmem, vmem, vmem),
        scratch_shapes=[
            pltpu.VMEM((n, rows, cols), crossing_part.dtype),
            pltpu.VMEM((n,) + piece.shape, jnp.float32),
            pltpu.VMEM((n, rows, cols), prior_rows.dtype),
            pltpu.VMEM((n_gc,) + piece.shape, jnp.bfloat16),
            pltpu.SemaphoreType.DMA((8, max(n, n_gc))),
        ],
        compiler_params=pltpu.CompilerParams(collective_id=1, has_side_effects=True),
    )(crossing_part, piece, prior_rows)


def prior_factor_rows(prior_rows, below_shape):
    return prior_rows.reshape(-1, below_shape[3], below_shape[5])


def local(
    n_gc,
    n_gr,
    line,
    below_factor,
    panel_factor,
    prior_factor,
    diag_factor,
    diag_inverse,
    below_adjoint,
    panel_adjoint,
    prior_adjoint,
    diag_adjoint,
):
    tile_count = below_factor.shape[0]
    tile_rows = below_factor.shape[2]
    local_rows = tile_count * tile_rows
    local_cols = below_factor.shape[3] * below_factor.shape[5]
    own_rows = panel_factor.shape[2]
    width = panel_factor.shape[3]
    prior_local = prior_factor.shape[0]
    below_mat = below_factor.reshape(local_rows, local_cols)
    below_bar = below_adjoint.reshape(local_rows, local_cols)
    inverse_bf = diag_inverse.astype(jnp.bfloat16)
    own_grad = lax.dot_general(
        panel_adjoint.reshape(tile_count, own_rows, width),
        inverse_bf,
        (((2,), (0,)), ((), ())),
        preferred_element_type=jnp.float32,
    ).astype(jnp.bfloat16)
    panel_grad = own_grad.reshape(panel_adjoint.shape)
    own_part = lax.dot_general(
        own_grad,
        panel_factor.reshape(tile_count, own_rows, width),
        (((0, 1), (0, 1)), ((), ())),
        preferred_element_type=jnp.float32,
    ).astype(jnp.bfloat16)
    whole, piece = gather_gc(
        own_grad.reshape(1, tile_count, own_rows, width),
        own_part.reshape(n_gc, width // n_gc, width),
        n_gc,
        line,
    )
    grad_rows = whole[0].reshape(local_rows, width)
    prior_here = prior_factor.reshape(prior_local, local_cols)
    crossing_part = row_product(grad_rows, below_mat).astype(jnp.bfloat16)
    cross_rows, prior_rows, crossing = reduce_gr(crossing_part, piece, prior_here, n_gr, n_gc)
    summed = cross_rows.reshape(width, width).astype(jnp.float32)
    prior_whole = prior_rows.reshape(width, local_cols)
    diag_reduced = jnp.tril(diag_adjoint - summed)
    diag_gradient = diag_solve(diag_factor, diag_inverse, diag_reduced)
    below_prod = lax.dot_general(
        grad_rows.reshape(tile_count, tile_rows, width),
        prior_factor_rows(prior_rows, below_factor.shape),
        (((2,), (0,)), ((), ())),
        preferred_element_type=jnp.float32,
    ).reshape(below_adjoint.shape)
    below_new = (below_adjoint.astype(jnp.float32) - below_prod).astype(jnp.bfloat16)
    grid_row = lax.axis_index("gr")
    twice_rows = lax.dynamic_slice_in_dim(
        2.0 * diag_gradient, grid_row * prior_local, prior_local, 0
    ).astype(jnp.bfloat16)
    curvature = jnp.dot(twice_rows, prior_whole, preferred_element_type=jnp.float32)
    prior_bar = prior_adjoint.reshape(prior_local, local_cols).astype(jnp.float32)
    prior_new = (prior_bar - crossing - curvature).astype(jnp.bfloat16)
    return (
        below_new,
        panel_grad,
        prior_new.reshape(prior_adjoint.shape),
        diag_gradient,
    )


def line_length(mesh):
    column = list(mesh.devices[0])
    coords = [getattr(d, "coords", None) for d in column]
    if any(c is None for c in coords):
        return 8 if len(column) % 8 == 0 else len(column)
    first = coords[0][0]
    count = 0
    for c in coords:
        if c[0] != first:
            break
        count += 1
    return count if len(column) % count == 0 else len(column)


def solution(mesh):
    in_specs = (
        P(None, "gr", None, None, "gc", None),
        P(None, "gr", "gc", None),
        P("gr", None, "gc", None),
        P(),
        P(),
        P(None, "gr", None, None, "gc", None),
        P(None, "gr", "gc", None),
        P("gr", None, "gc", None),
        P(),
    )
    out_specs = (
        P(None, "gr", None, None, "gc", None),
        P(None, "gr", "gc", None),
        P("gr", None, "gc", None),
        P(),
    )
    return jax.shard_map(
        functools.partial(local, mesh.shape["gc"], mesh.shape["gr"], line_length(mesh)),
        mesh=mesh,
        in_specs=in_specs,
        out_specs=out_specs,
        check_vma=False,
    )
```

```python
import functools

import jax
import jax.numpy as jnp
from jax import lax
from jax.experimental import pallas as pl
from jax.experimental.pallas import tpu as pltpu
from jax.sharding import PartitionSpec as P

MESH_ID = pl.DeviceIdType.MESH


def row_product(left_rows, right_rows):
    return lax.dot_general(
        left_rows, right_rows, (((0,), (0,)), ((), ())), preferred_element_type=jnp.float32
    )


def diag_solve(diag_factor, diag_inverse, diag_reduced):
    highest = lax.Precision.HIGH
    chol_proj = jnp.dot(diag_factor.T, diag_reduced, precision=highest)
    index_row = lax.broadcasted_iota(jnp.int32, chol_proj.shape, 0)
    index_col = lax.broadcasted_iota(jnp.int32, chol_proj.shape, 1)
    phi_lower = jnp.where(
        index_row > index_col,
        chol_proj,
        jnp.where(index_row == index_col, chol_proj - 0.5 * chol_proj, 0.0),
    )
    symmetric = 0.5 * (phi_lower + phi_lower.T)
    left_side = jnp.dot(diag_inverse.T, symmetric, precision=highest)
    return jnp.dot(left_side, diag_inverse, precision=highest)


def by_width(index, rows, width, action):
    group = (rows * (index + 1) - 1) // 128
    for j in range(width // 128):
        @pl.when(group == j)
        def _():
            action(128 * (j + 1))


def gather_kernel(n, line, n_gr, x_ref, p_ref, out_ref, cross_out, precv, recv_piece, cross_slots,
                  psems, sems, local_sem):
    me = lax.axis_index("gc")
    row = lax.axis_index("gr")
    rows = x_ref.shape[2]
    lines = n // line
    pos = lax.rem(me, line)
    grp = me // line
    base = grp * line

    def line_peer(k):
        return base + lax.rem(pos + k, line)

    def cross_peer(k):
        return lax.rem(grp + k, lines) * line + pos

    part_rows, part_width = p_ref.shape[1], p_ref.shape[2]
    precv[...] = jnp.zeros(precv.shape, precv.dtype)
    recv_piece[...] = jnp.zeros(recv_piece.shape, recv_piece.dtype)
    cross_slots[...] = jnp.zeros(cross_slots.shape, cross_slots.dtype)
    barrier = pltpu.get_barrier_semaphore()

    def greet(k, carry):
        pl.semaphore_signal(barrier, inc=1, device_id=(row, lax.rem(me + k, n)), device_id_type=MESH_ID)
        return carry

    def greet_gr(k, carry):
        pl.semaphore_signal(barrier, inc=1, device_id=(lax.rem(row + k, n_gr), me), device_id_type=MESH_ID)
        return carry

    lax.fori_loop(1, n, greet, 0)
    lax.fori_loop(1, n_gr, greet_gr, 0)
    pl.semaphore_wait(barrier, n + n_gr - 2)

    def part_copy(k, sender, cols):
        peer = lax.rem(me + k, n)
        return pltpu.make_async_remote_copy(
            src_ref=p_ref.at[peer, :, pl.ds(0, cols)],
            dst_ref=precv.at[sender, :, pl.ds(0, cols)],
            send_sem=psems.at[0, k],
            recv_sem=psems.at[1, sender],
            device_id=(row, peer),
            device_id_type=MESH_ID,
        )

    own = pltpu.make_async_copy(x_ref, out_ref.at[:, :, pl.ds(me * rows, rows), :], local_sem)
    own.start()

    def first(k, sender_pos):
        return pltpu.make_async_remote_copy(
            src_ref=x_ref,
            dst_ref=out_ref.at[:, :, pl.ds((base + sender_pos) * rows, rows), :],
            send_sem=sems.at[0, k],
            recv_sem=sems.at[1, sender_pos],
            device_id=(row, line_peer(k)),
            device_id_type=MESH_ID,
        )

    def send_first(k, carry):
        first(k, pos).start()
        return carry

    lax.fori_loop(1, line, send_first, 0)

    def send_parts(k, carry):
        by_width(lax.rem(me + k, n), part_rows, part_width, lambda cols: part_copy(k, me, cols).start())
        return carry

    lax.fori_loop(1, n, send_parts, 0)

    span = line * rows

    def forward(k, block_pos, sender_grp):
        slot = pl.ds((grp * line + block_pos) * rows, rows)
        return pltpu.make_async_remote_copy(
            src_ref=out_ref.at[:, :, slot, :],
            dst_ref=out_ref.at[:, :, slot, :],
            send_sem=sems.at[2 + block_pos, k],
            recv_sem=sems.at[1, line + sender_grp],
            device_id=(row, cross_peer(k)),
            device_id_type=MESH_ID,
        )

    def whole_line(sender_grp):
        return pltpu.make_async_remote_copy(
            src_ref=out_ref.at[:, :, pl.ds(sender_grp * span, span), :],
            dst_ref=out_ref.at[:, :, pl.ds(sender_grp * span, span), :],
            send_sem=sems.at[0, 0],
            recv_sem=sems.at[1, line + sender_grp],
            device_id=(row, cross_peer(1)),
            device_id_type=MESH_ID,
        )

    own.wait()

    def send_own(k, carry):
        forward(k, pos, grp).start()
        return carry

    lax.fori_loop(1, lines, send_own, 0)

    def relay(k, carry):
        sender_pos = lax.rem(pos + line - k, line)
        first(k, sender_pos).wait_recv()

        def out(j, inner):
            forward(j, sender_pos, grp).start()
            return inner

        return lax.fori_loop(1, lines, out, carry)

    lax.fori_loop(1, line, relay, 0)

    precv[me] = p_ref[me]

    def wait_parts(k, carry):
        sender = lax.rem(me + n - k, n)
        by_width(lax.rem(me + k, n), part_rows, part_width, lambda cols: part_copy(k, me, cols).wait_send())
        by_width(me, part_rows, part_width, lambda cols: part_copy(k, sender, cols).wait_recv())
        return carry

    lax.fori_loop(1, n, wait_parts, 0)

    def add_part(j, total):
        return total + precv[j].astype(jnp.float32)

    piece = lax.fori_loop(0, n, add_part, jnp.zeros(recv_piece.shape[1:], jnp.float32))
    recv_piece[row] = piece

    def piece_copy(k, sender, cols):
        return pltpu.make_async_remote_copy(
            src_ref=recv_piece.at[row, :, pl.ds(0, cols)],
            dst_ref=recv_piece.at[sender, :, pl.ds(0, cols)],
            send_sem=psems.at[2, k],
            recv_sem=psems.at[3, sender],
            device_id=(lax.rem(row + k, n_gr), me),
            device_id_type=MESH_ID,
        )

    def send_piece(k, carry):
        by_width(me, part_rows, part_width, lambda cols: piece_copy(k, row, cols).start())
        return carry

    lax.fori_loop(1, n_gr, send_piece, 0)

    def wait_piece(k, carry):
        sender = lax.rem(row + n_gr - k, n_gr)
        by_width(me, part_rows, part_width, lambda cols: piece_copy(k, row, cols).wait_send())
        by_width(me, part_rows, part_width, lambda cols: piece_copy(k, sender, cols).wait_recv())
        return carry

    lax.fori_loop(1, n_gr, wait_piece, 0)

    def add_piece(j, total):
        return total + recv_piece[j]

    summed = lax.fori_loop(0, n_gr, add_piece, jnp.zeros(recv_piece.shape[1:], jnp.float32))
    cross_slots[me] = summed.astype(cross_slots.dtype)

    def cross_copy(k, sender, cols):
        return pltpu.make_async_remote_copy(
            src_ref=cross_slots.at[me, :, pl.ds(0, cols)],
            dst_ref=cross_slots.at[sender, :, pl.ds(0, cols)],
            send_sem=psems.at[4, k],
            recv_sem=psems.at[5, sender],
            device_id=(row, lax.rem(me + k, n)),
            device_id_type=MESH_ID,
        )

    def send_cross(k, carry):
        by_width(me, part_rows, part_width, lambda cols: cross_copy(k, me, cols).start())
        return carry

    lax.fori_loop(1, n, send_cross, 0)

    def wait_first(k, carry):
        first(k, pos).wait_send()
        return carry

    lax.fori_loop(1, line, wait_first, 0)

    def wait_sent(k, carry):
        def done(j, inner):
            forward(j, k, grp).wait_send()
            return inner

        return lax.fori_loop(1, lines, done, carry)

    lax.fori_loop(0, line, wait_sent, 0)

    def wait_lines(k, carry):
        whole_line(lax.rem(grp + lines - k, lines)).wait_recv()
        return carry

    lax.fori_loop(1, lines, wait_lines, 0)

    def wait_cross(k, carry):
        sender = lax.rem(me + n - k, n)
        by_width(me, part_rows, part_width, lambda cols: cross_copy(k, me, cols).wait_send())
        by_width(sender, part_rows, part_width, lambda cols: cross_copy(k, sender, cols).wait_recv())
        return carry

    lax.fori_loop(1, n, wait_cross, 0)
    cross_out[...] = cross_slots[...]


def gather_gc(block, part, n, line, n_gr):
    count, tiles, rows, width = block.shape
    vmem = pl.BlockSpec(memory_space=pltpu.VMEM)
    return pl.pallas_call(
        functools.partial(gather_kernel, n, line, n_gr),
        out_shape=(
            jax.ShapeDtypeStruct((count, tiles, rows * n, width), block.dtype),
            jax.ShapeDtypeStruct(part.shape, jnp.bfloat16),
        ),
        in_specs=[pl.BlockSpec(memory_space=pl.ANY), vmem],
        out_specs=(pl.BlockSpec(memory_space=pl.ANY), vmem),
        scratch_shapes=[
            pltpu.VMEM(part.shape, part.dtype),
            pltpu.VMEM((n_gr,) + part.shape[1:], jnp.float32),
            pltpu.VMEM(part.shape, jnp.bfloat16),
            pltpu.SemaphoreType.DMA((6, max(n, n_gr))),
            pltpu.SemaphoreType.DMA((2 + line, line + n // line)),
            pltpu.SemaphoreType.DMA,
        ],
        compiler_params=pltpu.CompilerParams(collective_id=0, has_side_effects=True),
    )(block, part)


def reduce_kernel(n, crossing_ref, prior_ref, prior_out, crossing_out, recv_crossing, prior_slots, sems):
    me = lax.axis_index("gr")
    col = lax.axis_index("gc")
    rows = prior_ref.shape[0]

    barrier = pltpu.get_barrier_semaphore()

    def greet_gr(k, carry):
        pl.semaphore_signal(barrier, inc=1, device_id=(lax.rem(me + k, n), col), device_id_type=MESH_ID)
        return carry

    lax.fori_loop(1, n, greet_gr, 0)
    pl.semaphore_wait(barrier, n - 1)

    def gr_copy(k, sender, src, dst, index):
        return pltpu.make_async_remote_copy(
            src_ref=src,
            dst_ref=dst.at[sender],
            send_sem=sems.at[index, k],
            recv_sem=sems.at[index + 1, sender],
            device_id=(lax.rem(me + k, n), col),
            device_id_type=MESH_ID,
        )

    def crossing_copy(k, sender):
        peer = lax.rem(me + k, n)
        src = crossing_ref.at[pl.ds(pl.multiple_of(peer * rows, rows), rows), :]
        return gr_copy(k, sender, src, recv_crossing, 0)

    def prior_copy(k, sender):
        return gr_copy(k, sender, prior_ref, prior_slots, 2)

    def send(k, carry):
        crossing_copy(k, me).start()
        prior_copy(k, me).start()
        return carry

    lax.fori_loop(1, n, send, 0)
    prior_slots[me] = prior_ref[...]
    recv_crossing[me] = crossing_ref[pl.ds(pl.multiple_of(me * rows, rows), rows), :]

    def wait(k, carry):
        sender = lax.rem(me + n - k, n)
        crossing_copy(k, me).wait_send()
        crossing_copy(k, sender).wait_recv()
        prior_copy(k, me).wait_send()
        prior_copy(k, sender).wait_recv()
        return carry

    lax.fori_loop(1, n, wait, 0)

    def add_crossing(j, total):
        return total + recv_crossing[j].astype(jnp.float32)

    crossing_out[...] = lax.fori_loop(0, n, add_crossing, jnp.zeros(crossing_out.shape, jnp.float32))
    prior_out[...] = prior_slots[...]


def reduce_gr(crossing_part, prior_rows, n):
    rows, cols = prior_rows.shape
    vmem = pl.BlockSpec(memory_space=pltpu.VMEM)
    return pl.pallas_call(
        functools.partial(reduce_kernel, n),
        out_shape=(
            jax.ShapeDtypeStruct((n, rows, cols), prior_rows.dtype),
            jax.ShapeDtypeStruct((rows, cols), jnp.float32),
        ),
        in_specs=[vmem, vmem],
        out_specs=(vmem, vmem),
        scratch_shapes=[
            pltpu.VMEM((n, rows, cols), crossing_part.dtype),
            pltpu.VMEM((n, rows, cols), prior_rows.dtype),
            pltpu.SemaphoreType.DMA((4, n)),
        ],
        compiler_params=pltpu.CompilerParams(collective_id=1, has_side_effects=True),
    )(crossing_part, prior_rows)


def prior_factor_rows(prior_rows, below_shape):
    return prior_rows.reshape(-1, below_shape[3], below_shape[5])


def local(
    n_gc,
    n_gr,
    line,
    below_factor,
    panel_factor,
    prior_factor,
    diag_factor,
    diag_inverse,
    below_adjoint,
    panel_adjoint,
    prior_adjoint,
    diag_adjoint,
):
    tile_count = below_factor.shape[0]
    tile_rows = below_factor.shape[2]
    local_rows = tile_count * tile_rows
    local_cols = below_factor.shape[3] * below_factor.shape[5]
    own_rows = panel_factor.shape[2]
    width = panel_factor.shape[3]
    prior_local = prior_factor.shape[0]
    below_mat = below_factor.reshape(local_rows, local_cols)
    below_bar = below_adjoint.reshape(local_rows, local_cols)
    inverse_bf = diag_inverse.astype(jnp.bfloat16)
    own_grad = lax.dot_general(
        panel_adjoint.reshape(tile_count, own_rows, width),
        inverse_bf,
        (((2,), (0,)), ((), ())),
        preferred_element_type=jnp.float32,
    ).astype(jnp.bfloat16)
    panel_grad = own_grad.reshape(panel_adjoint.shape)
    own_part = lax.dot_general(
        own_grad,
        panel_factor.reshape(tile_count, own_rows, width),
        (((0, 1), (0, 1)), ((), ())),
        preferred_element_type=jnp.float32,
    ).astype(jnp.bfloat16)
    whole, cross_rows = gather_gc(
        own_grad.reshape(1, tile_count, own_rows, width),
        own_part.reshape(n_gc, width // n_gc, width),
        n_gc,
        line,
        n_gr,
    )
    grad_rows = whole[0].reshape(local_rows, width)
    prior_here = prior_factor.reshape(prior_local, local_cols)
    crossing_part = row_product(grad_rows, below_mat).astype(jnp.bfloat16)
    prior_rows, crossing = reduce_gr(crossing_part, prior_here, n_gr)
    summed = cross_rows.reshape(width, width).astype(jnp.float32)
    prior_whole = prior_rows.reshape(width, local_cols)
    diag_reduced = jnp.tril(diag_adjoint - summed)
    diag_gradient = diag_solve(diag_factor, diag_inverse, diag_reduced)
    below_prod = lax.dot_general(
        grad_rows.reshape(tile_count, tile_rows, width),
        prior_factor_rows(prior_rows, below_factor.shape),
        (((2,), (0,)), ((), ())),
        preferred_element_type=jnp.float32,
    ).reshape(below_adjoint.shape)
    below_new = (below_adjoint.astype(jnp.float32) - below_prod).astype(jnp.bfloat16)
    grid_row = lax.axis_index("gr")
    twice_rows = lax.dynamic_slice_in_dim(
        2.0 * diag_gradient, grid_row * prior_local, prior_local, 0
    ).astype(jnp.bfloat16)
    curvature = jnp.dot(twice_rows, prior_whole, preferred_element_type=jnp.float32)
    prior_bar = prior_adjoint.reshape(prior_local, local_cols).astype(jnp.float32)
    prior_new = (prior_bar - crossing - curvature).astype(jnp.bfloat16)
    return (
        below_new,
        panel_grad,
        prior_new.reshape(prior_adjoint.shape),
        diag_gradient,
    )


def line_length(mesh):
    column = list(mesh.devices[0])
    coords = [getattr(d, "coords", None) for d in column]
    if any(c is None for c in coords):
        return 8 if len(column) % 8 == 0 else len(column)
    first = coords[0][0]
    count = 0
    for c in coords:
        if c[0] != first:
            break
        count += 1
    return count if len(column) % count == 0 else len(column)


def solution(mesh):
    in_specs = (
        P(None, "gr", None, None, "gc", None),
        P(None, "gr", "gc", None),
        P("gr", None, "gc", None),
        P(),
        P(),
        P(None, "gr", None, None, "gc", None),
        P(None, "gr", "gc", None),
        P("gr", None, "gc", None),
        P(),
    )
    out_specs = (
        P(None, "gr", None, None, "gc", None),
        P(None, "gr", "gc", None),
        P("gr", None, "gc", None),
        P(),
    )
    return jax.shard_map(
        functools.partial(local, mesh.shape["gc"], mesh.shape["gr"], line_length(mesh)),
        mesh=mesh,
        in_specs=in_specs,
        out_specs=out_specs,
        check_vma=False,
    )
```

```python
import functools

import jax
import jax.numpy as jnp
from jax import lax
from jax.experimental import pallas as pl
from jax.experimental.pallas import tpu as pltpu
from jax.sharding import PartitionSpec as P

MESH_ID = pl.DeviceIdType.MESH


def row_product(left_rows, right_rows):
    return lax.dot_general(
        left_rows, right_rows, (((0,), (0,)), ((), ())), preferred_element_type=jnp.float32
    )


def diag_solve(diag_factor, diag_inverse, diag_reduced):
    highest = lax.Precision.HIGH
    chol_proj = jnp.dot(diag_factor.T, diag_reduced, precision=highest)
    index_row = lax.broadcasted_iota(jnp.int32, chol_proj.shape, 0)
    index_col = lax.broadcasted_iota(jnp.int32, chol_proj.shape, 1)
    phi_lower = jnp.where(
        index_row > index_col,
        chol_proj,
        jnp.where(index_row == index_col, chol_proj - 0.5 * chol_proj, 0.0),
    )
    symmetric = 0.5 * (phi_lower + phi_lower.T)
    left_side = jnp.dot(diag_inverse.T, symmetric, precision=highest)
    return jnp.dot(left_side, diag_inverse, precision=highest)


def by_width(index, rows, width, action):
    group = (rows * (index + 1) - 1) // 128
    for j in range(width // 128):
        @pl.when(group == j)
        def _():
            action(128 * (j + 1))


def gather_kernel(n, line, n_gr, x_ref, p_ref, out_ref, cross_out, precv, recv_piece, cross_slots,
                  psems, sems, local_sem):
    me = lax.axis_index("gc")
    row = lax.axis_index("gr")
    rows = x_ref.shape[2]
    lines = n // line
    pos = lax.rem(me, line)
    grp = me // line
    base = grp * line

    def line_peer(k):
        return base + lax.rem(pos + k, line)

    def cross_peer(k):
        return lax.rem(grp + k, lines) * line + pos

    part_rows, part_width = p_ref.shape[1], p_ref.shape[2]
    precv[...] = jnp.zeros(precv.shape, precv.dtype)
    recv_piece[...] = jnp.zeros(recv_piece.shape, recv_piece.dtype)
    cross_slots[...] = jnp.zeros(cross_slots.shape, cross_slots.dtype)
    barrier = pltpu.get_barrier_semaphore()

    def greet(k, carry):
        pl.semaphore_signal(barrier, inc=1, device_id=(row, lax.rem(me + k, n)), device_id_type=MESH_ID)
        return carry

    def greet_gr(k, carry):
        pl.semaphore_signal(barrier, inc=1, device_id=(lax.rem(row + k, n_gr), me), device_id_type=MESH_ID)
        return carry

    lax.fori_loop(1, n, greet, 0)
    lax.fori_loop(1, n_gr, greet_gr, 0)
    pl.semaphore_wait(barrier, n + n_gr - 2)

    def part_copy(k, sender, cols):
        peer = lax.rem(me + k, n)
        return pltpu.make_async_remote_copy(
            src_ref=p_ref.at[peer, :, pl.ds(0, cols)],
            dst_ref=precv.at[sender, :, pl.ds(0, cols)],
            send_sem=psems.at[0, k],
            recv_sem=psems.at[1, sender],
            device_id=(row, peer),
            device_id_type=MESH_ID,
        )

    def send_parts(k, carry):
        by_width(lax.rem(me + k, n), part_rows, part_width, lambda cols: part_copy(k, me, cols).start())
        return carry

    lax.fori_loop(1, n, send_parts, 0)

    own = pltpu.make_async_copy(x_ref, out_ref.at[:, :, pl.ds(me * rows, rows), :], local_sem)
    own.start()

    def first(k, sender_pos):
        return pltpu.make_async_remote_copy(
            src_ref=x_ref,
            dst_ref=out_ref.at[:, :, pl.ds((base + sender_pos) * rows, rows), :],
            send_sem=sems.at[0, k],
            recv_sem=sems.at[1, sender_pos],
            device_id=(row, line_peer(k)),
            device_id_type=MESH_ID,
        )

    def send_first(k, carry):
        first(k, pos).start()
        return carry

    lax.fori_loop(1, line, send_first, 0)


    span = line * rows

    def forward(k, block_pos, sender_grp):
        slot = pl.ds((grp * line + block_pos) * rows, rows)
        return pltpu.make_async_remote_copy(
            src_ref=out_ref.at[:, :, slot, :],
            dst_ref=out_ref.at[:, :, slot, :],
            send_sem=sems.at[2 + block_pos, k],
            recv_sem=sems.at[1, line + sender_grp],
            device_id=(row, cross_peer(k)),
            device_id_type=MESH_ID,
        )

    def whole_line(sender_grp):
        return pltpu.make_async_remote_copy(
            src_ref=out_ref.at[:, :, pl.ds(sender_grp * span, span), :],
            dst_ref=out_ref.at[:, :, pl.ds(sender_grp * span, span), :],
            send_sem=sems.at[0, 0],
            recv_sem=sems.at[1, line + sender_grp],
            device_id=(row, cross_peer(1)),
            device_id_type=MESH_ID,
        )

    own.wait()

    def send_own(k, carry):
        forward(k, pos, grp).start()
        return carry

    lax.fori_loop(1, lines, send_own, 0)


    precv[me] = p_ref[me]

    def wait_parts(k, carry):
        sender = lax.rem(me + n - k, n)
        by_width(lax.rem(me + k, n), part_rows, part_width, lambda cols: part_copy(k, me, cols).wait_send())
        by_width(me, part_rows, part_width, lambda cols: part_copy(k, sender, cols).wait_recv())
        return carry

    lax.fori_loop(1, n, wait_parts, 0)

    def add_part(j, total):
        return total + precv[j].astype(jnp.float32)

    piece = lax.fori_loop(0, n, add_part, jnp.zeros(recv_piece.shape[1:], jnp.float32))
    recv_piece[row] = piece

    def piece_copy(k, sender, cols):
        return pltpu.make_async_remote_copy(
            src_ref=recv_piece.at[row, :, pl.ds(0, cols)],
            dst_ref=recv_piece.at[sender, :, pl.ds(0, cols)],
            send_sem=psems.at[2, k],
            recv_sem=psems.at[3, sender],
            device_id=(lax.rem(row + k, n_gr), me),
            device_id_type=MESH_ID,
        )

    def send_piece(k, carry):
        by_width(me, part_rows, part_width, lambda cols: piece_copy(k, row, cols).start())
        return carry

    lax.fori_loop(1, n_gr, send_piece, 0)

    def relay(k, carry):
        sender_pos = lax.rem(pos + line - k, line)
        first(k, sender_pos).wait_recv()

        def out(j, inner):
            forward(j, sender_pos, grp).start()
            return inner

        return lax.fori_loop(1, lines, out, carry)

    lax.fori_loop(1, line, relay, 0)

    def wait_piece(k, carry):
        sender = lax.rem(row + n_gr - k, n_gr)
        by_width(me, part_rows, part_width, lambda cols: piece_copy(k, row, cols).wait_send())
        by_width(me, part_rows, part_width, lambda cols: piece_copy(k, sender, cols).wait_recv())
        return carry

    lax.fori_loop(1, n_gr, wait_piece, 0)

    def add_piece(j, total):
        return total + recv_piece[j]

    summed = lax.fori_loop(0, n_gr, add_piece, jnp.zeros(recv_piece.shape[1:], jnp.float32))
    cross_slots[me] = summed.astype(cross_slots.dtype)

    def cross_copy(k, sender, cols):
        return pltpu.make_async_remote_copy(
            src_ref=cross_slots.at[me, :, pl.ds(0, cols)],
            dst_ref=cross_slots.at[sender, :, pl.ds(0, cols)],
            send_sem=psems.at[4, k],
            recv_sem=psems.at[5, sender],
            device_id=(row, lax.rem(me + k, n)),
            device_id_type=MESH_ID,
        )

    def send_cross(k, carry):
        by_width(me, part_rows, part_width, lambda cols: cross_copy(k, me, cols).start())
        return carry

    lax.fori_loop(1, n, send_cross, 0)

    def wait_first(k, carry):
        first(k, pos).wait_send()
        return carry

    lax.fori_loop(1, line, wait_first, 0)

    def wait_sent(k, carry):
        def done(j, inner):
            forward(j, k, grp).wait_send()
            return inner

        return lax.fori_loop(1, lines, done, carry)

    lax.fori_loop(0, line, wait_sent, 0)

    def wait_lines(k, carry):
        whole_line(lax.rem(grp + lines - k, lines)).wait_recv()
        return carry

    lax.fori_loop(1, lines, wait_lines, 0)

    def wait_cross(k, carry):
        sender = lax.rem(me + n - k, n)
        by_width(me, part_rows, part_width, lambda cols: cross_copy(k, me, cols).wait_send())
        by_width(sender, part_rows, part_width, lambda cols: cross_copy(k, sender, cols).wait_recv())
        return carry

    lax.fori_loop(1, n, wait_cross, 0)
    cross_out[...] = cross_slots[...]


def gather_gc(block, part, n, line, n_gr):
    count, tiles, rows, width = block.shape
    vmem = pl.BlockSpec(memory_space=pltpu.VMEM)
    return pl.pallas_call(
        functools.partial(gather_kernel, n, line, n_gr),
        out_shape=(
            jax.ShapeDtypeStruct((count, tiles, rows * n, width), block.dtype),
            jax.ShapeDtypeStruct(part.shape, jnp.bfloat16),
        ),
        in_specs=[pl.BlockSpec(memory_space=pl.ANY), vmem],
        out_specs=(pl.BlockSpec(memory_space=pl.ANY), vmem),
        scratch_shapes=[
            pltpu.VMEM(part.shape, part.dtype),
            pltpu.VMEM((n_gr,) + part.shape[1:], jnp.float32),
            pltpu.VMEM(part.shape, jnp.bfloat16),
            pltpu.SemaphoreType.DMA((6, max(n, n_gr))),
            pltpu.SemaphoreType.DMA((2 + line, line + n // line)),
            pltpu.SemaphoreType.DMA,
        ],
        compiler_params=pltpu.CompilerParams(collective_id=0, has_side_effects=True),
    )(block, part)


def reduce_kernel(n, crossing_ref, prior_ref, prior_out, crossing_out, recv_crossing, prior_slots, sems):
    me = lax.axis_index("gr")
    col = lax.axis_index("gc")
    rows = prior_ref.shape[0]

    barrier = pltpu.get_barrier_semaphore()

    def greet_gr(k, carry):
        pl.semaphore_signal(barrier, inc=1, device_id=(lax.rem(me + k, n), col), device_id_type=MESH_ID)
        return carry

    lax.fori_loop(1, n, greet_gr, 0)
    pl.semaphore_wait(barrier, n - 1)

    def gr_copy(k, sender, src, dst, index):
        return pltpu.make_async_remote_copy(
            src_ref=src,
            dst_ref=dst.at[sender],
            send_sem=sems.at[index, k],
            recv_sem=sems.at[index + 1, sender],
            device_id=(lax.rem(me + k, n), col),
            device_id_type=MESH_ID,
        )

    def crossing_copy(k, sender):
        peer = lax.rem(me + k, n)
        src = crossing_ref.at[pl.ds(pl.multiple_of(peer * rows, rows), rows), :]
        return gr_copy(k, sender, src, recv_crossing, 0)

    def prior_copy(k, sender):
        return gr_copy(k, sender, prior_ref, prior_slots, 2)

    def send(k, carry):
        crossing_copy(k, me).start()
        prior_copy(k, me).start()
        return carry

    lax.fori_loop(1, n, send, 0)
    prior_slots[me] = prior_ref[...]
    recv_crossing[me] = crossing_ref[pl.ds(pl.multiple_of(me * rows, rows), rows), :]

    def wait(k, carry):
        sender = lax.rem(me + n - k, n)
        crossing_copy(k, me).wait_send()
        crossing_copy(k, sender).wait_recv()
        prior_copy(k, me).wait_send()
        prior_copy(k, sender).wait_recv()
        return carry

    lax.fori_loop(1, n, wait, 0)

    def add_crossing(j, total):
        return total + recv_crossing[j].astype(jnp.float32)

    crossing_out[...] = lax.fori_loop(0, n, add_crossing, jnp.zeros(crossing_out.shape, jnp.float32))
    prior_out[...] = prior_slots[...]


def reduce_gr(crossing_part, prior_rows, n):
    rows, cols = prior_rows.shape
    vmem = pl.BlockSpec(memory_space=pltpu.VMEM)
    return pl.pallas_call(
        functools.partial(reduce_kernel, n),
        out_shape=(
            jax.ShapeDtypeStruct((n, rows, cols), prior_rows.dtype),
            jax.ShapeDtypeStruct((rows, cols), jnp.float32),
        ),
        in_specs=[vmem, vmem],
        out_specs=(vmem, vmem),
        scratch_shapes=[
            pltpu.VMEM((n, rows, cols), crossing_part.dtype),
            pltpu.VMEM((n, rows, cols), prior_rows.dtype),
            pltpu.SemaphoreType.DMA((4, n)),
        ],
        compiler_params=pltpu.CompilerParams(collective_id=1, has_side_effects=True),
    )(crossing_part, prior_rows)


def prior_factor_rows(prior_rows, below_shape):
    return prior_rows.reshape(-1, below_shape[3], below_shape[5])


def local(
    n_gc,
    n_gr,
    line,
    below_factor,
    panel_factor,
    prior_factor,
    diag_factor,
    diag_inverse,
    below_adjoint,
    panel_adjoint,
    prior_adjoint,
    diag_adjoint,
):
    tile_count = below_factor.shape[0]
    tile_rows = below_factor.shape[2]
    local_rows = tile_count * tile_rows
    local_cols = below_factor.shape[3] * below_factor.shape[5]
    own_rows = panel_factor.shape[2]
    width = panel_factor.shape[3]
    prior_local = prior_factor.shape[0]
    below_mat = below_factor.reshape(local_rows, local_cols)
    below_bar = below_adjoint.reshape(local_rows, local_cols)
    inverse_bf = diag_inverse.astype(jnp.bfloat16)
    own_grad = lax.dot_general(
        panel_adjoint.reshape(tile_count, own_rows, width),
        inverse_bf,
        (((2,), (0,)), ((), ())),
        preferred_element_type=jnp.float32,
    ).astype(jnp.bfloat16)
    panel_grad = own_grad.reshape(panel_adjoint.shape)
    own_part = lax.dot_general(
        own_grad,
        panel_factor.reshape(tile_count, own_rows, width),
        (((0, 1), (0, 1)), ((), ())),
        preferred_element_type=jnp.float32,
    ).astype(jnp.bfloat16)
    whole, cross_rows = gather_gc(
        own_grad.reshape(1, tile_count, own_rows, width),
        own_part.reshape(n_gc, width // n_gc, width),
        n_gc,
        line,
        n_gr,
    )
    grad_rows = whole[0].reshape(local_rows, width)
    prior_here = prior_factor.reshape(prior_local, local_cols)
    crossing_part = row_product(grad_rows, below_mat).astype(jnp.bfloat16)
    prior_rows, crossing = reduce_gr(crossing_part, prior_here, n_gr)
    summed = cross_rows.reshape(width, width).astype(jnp.float32)
    prior_whole = prior_rows.reshape(width, local_cols)
    diag_reduced = jnp.tril(diag_adjoint - summed)
    diag_gradient = diag_solve(diag_factor, diag_inverse, diag_reduced)
    below_prod = lax.dot_general(
        grad_rows.reshape(tile_count, tile_rows, width),
        prior_factor_rows(prior_rows, below_factor.shape),
        (((2,), (0,)), ((), ())),
        preferred_element_type=jnp.float32,
    ).reshape(below_adjoint.shape)
    below_new = (below_adjoint.astype(jnp.float32) - below_prod).astype(jnp.bfloat16)
    grid_row = lax.axis_index("gr")
    twice_rows = lax.dynamic_slice_in_dim(
        2.0 * diag_gradient, grid_row * prior_local, prior_local, 0
    ).astype(jnp.bfloat16)
    curvature = jnp.dot(twice_rows, prior_whole, preferred_element_type=jnp.float32)
    prior_bar = prior_adjoint.reshape(prior_local, local_cols).astype(jnp.float32)
    prior_new = (prior_bar - crossing - curvature).astype(jnp.bfloat16)
    return (
        below_new,
        panel_grad,
        prior_new.reshape(prior_adjoint.shape),
        diag_gradient,
    )


def line_length(mesh):
    column = list(mesh.devices[0])
    coords = [getattr(d, "coords", None) for d in column]
    if any(c is None for c in coords):
        return 8 if len(column) % 8 == 0 else len(column)
    first = coords[0][0]
    count = 0
    for c in coords:
        if c[0] != first:
            break
        count += 1
    return count if len(column) % count == 0 else len(column)


def solution(mesh):
    in_specs = (
        P(None, "gr", None, None, "gc", None),
        P(None, "gr", "gc", None),
        P("gr", None, "gc", None),
        P(),
        P(),
        P(None, "gr", None, None, "gc", None),
        P(None, "gr", "gc", None),
        P("gr", None, "gc", None),
        P(),
    )
    out_specs = (
        P(None, "gr", None, None, "gc", None),
        P(None, "gr", "gc", None),
        P("gr", None, "gc", None),
        P(),
    )
    return jax.shard_map(
        functools.partial(local, mesh.shape["gc"], mesh.shape["gr"], line_length(mesh)),
        mesh=mesh,
        in_specs=in_specs,
        out_specs=out_specs,
        check_vma=False,
    )
```

```python
import functools

import jax
import jax.numpy as jnp
from jax import lax
from jax.experimental import pallas as pl
from jax.experimental.pallas import tpu as pltpu
from jax.sharding import PartitionSpec as P

MESH_ID = pl.DeviceIdType.MESH


def row_product(left_rows, right_rows):
    return lax.dot_general(
        left_rows, right_rows, (((0,), (0,)), ((), ())), preferred_element_type=jnp.float32
    )


def diag_solve(diag_factor, diag_inverse, diag_reduced):
    highest = lax.Precision.HIGH
    chol_proj = jnp.dot(diag_factor.T, diag_reduced, precision=highest)
    index_row = lax.broadcasted_iota(jnp.int32, chol_proj.shape, 0)
    index_col = lax.broadcasted_iota(jnp.int32, chol_proj.shape, 1)
    phi_lower = jnp.where(
        index_row > index_col,
        chol_proj,
        jnp.where(index_row == index_col, chol_proj - 0.5 * chol_proj, 0.0),
    )
    symmetric = 0.5 * (phi_lower + phi_lower.T)
    left_side = jnp.dot(diag_inverse.T, symmetric, precision=highest)
    return jnp.dot(left_side, diag_inverse, precision=highest)


def by_width(index, rows, width, action):
    group = (rows * (index + 1) - 1) // 128
    for j in range(width // 128):
        @pl.when(group == j)
        def _():
            action(128 * (j + 1))


def gather_kernel(n, line, n_gr, x_ref, p_ref, prior_ref, out_ref, cross_out, prior_out, precv, recv_piece,
                  cross_slots, prior_slots, psems, sems, local_sem):
    me = lax.axis_index("gc")
    row = lax.axis_index("gr")
    rows = x_ref.shape[2]
    lines = n // line
    pos = lax.rem(me, line)
    grp = me // line
    base = grp * line

    def line_peer(k):
        return base + lax.rem(pos + k, line)

    def cross_peer(k):
        return lax.rem(grp + k, lines) * line + pos

    part_rows, part_width = p_ref.shape[1], p_ref.shape[2]
    precv[...] = jnp.zeros(precv.shape, precv.dtype)
    recv_piece[...] = jnp.zeros(recv_piece.shape, recv_piece.dtype)
    cross_slots[...] = jnp.zeros(cross_slots.shape, cross_slots.dtype)
    barrier = pltpu.get_barrier_semaphore()

    def greet(k, carry):
        pl.semaphore_signal(barrier, inc=1, device_id=(row, lax.rem(me + k, n)), device_id_type=MESH_ID)
        return carry

    def greet_gr(k, carry):
        pl.semaphore_signal(barrier, inc=1, device_id=(lax.rem(row + k, n_gr), me), device_id_type=MESH_ID)
        return carry

    lax.fori_loop(1, n, greet, 0)
    lax.fori_loop(1, n_gr, greet_gr, 0)
    pl.semaphore_wait(barrier, n + n_gr - 2)

    def part_copy(k, sender, cols):
        peer = lax.rem(me + k, n)
        return pltpu.make_async_remote_copy(
            src_ref=p_ref.at[peer, :, pl.ds(0, cols)],
            dst_ref=precv.at[sender, :, pl.ds(0, cols)],
            send_sem=psems.at[0, k],
            recv_sem=psems.at[1, sender],
            device_id=(row, peer),
            device_id_type=MESH_ID,
        )

    def send_parts(k, carry):
        by_width(lax.rem(me + k, n), part_rows, part_width, lambda cols: part_copy(k, me, cols).start())
        return carry

    lax.fori_loop(1, n, send_parts, 0)

    own = pltpu.make_async_copy(x_ref, out_ref.at[:, :, pl.ds(me * rows, rows), :], local_sem)
    own.start()

    def first(k, sender_pos):
        return pltpu.make_async_remote_copy(
            src_ref=x_ref,
            dst_ref=out_ref.at[:, :, pl.ds((base + sender_pos) * rows, rows), :],
            send_sem=sems.at[0, k],
            recv_sem=sems.at[1, sender_pos],
            device_id=(row, line_peer(k)),
            device_id_type=MESH_ID,
        )

    def send_first(k, carry):
        first(k, pos).start()
        return carry

    lax.fori_loop(1, line, send_first, 0)


    span = line * rows

    def forward(k, block_pos, sender_grp):
        slot = pl.ds((grp * line + block_pos) * rows, rows)
        return pltpu.make_async_remote_copy(
            src_ref=out_ref.at[:, :, slot, :],
            dst_ref=out_ref.at[:, :, slot, :],
            send_sem=sems.at[2 + block_pos, k],
            recv_sem=sems.at[1, line + sender_grp],
            device_id=(row, cross_peer(k)),
            device_id_type=MESH_ID,
        )

    def whole_line(sender_grp):
        return pltpu.make_async_remote_copy(
            src_ref=out_ref.at[:, :, pl.ds(sender_grp * span, span), :],
            dst_ref=out_ref.at[:, :, pl.ds(sender_grp * span, span), :],
            send_sem=sems.at[0, 0],
            recv_sem=sems.at[1, line + sender_grp],
            device_id=(row, cross_peer(1)),
            device_id_type=MESH_ID,
        )

    own.wait()

    def send_own(k, carry):
        forward(k, pos, grp).start()
        return carry

    lax.fori_loop(1, lines, send_own, 0)


    precv[me] = p_ref[me]

    def wait_parts(k, carry):
        sender = lax.rem(me + n - k, n)
        by_width(lax.rem(me + k, n), part_rows, part_width, lambda cols: part_copy(k, me, cols).wait_send())
        by_width(me, part_rows, part_width, lambda cols: part_copy(k, sender, cols).wait_recv())
        return carry

    lax.fori_loop(1, n, wait_parts, 0)

    def add_part(j, total):
        return total + precv[j].astype(jnp.float32)

    piece = lax.fori_loop(0, n, add_part, jnp.zeros(recv_piece.shape[1:], jnp.float32))
    recv_piece[row] = piece

    def piece_copy(k, sender, cols):
        return pltpu.make_async_remote_copy(
            src_ref=recv_piece.at[row, :, pl.ds(0, cols)],
            dst_ref=recv_piece.at[sender, :, pl.ds(0, cols)],
            send_sem=psems.at[2, k],
            recv_sem=psems.at[3, sender],
            device_id=(lax.rem(row + k, n_gr), me),
            device_id_type=MESH_ID,
        )

    def send_piece(k, carry):
        by_width(me, part_rows, part_width, lambda cols: piece_copy(k, row, cols).start())
        return carry

    lax.fori_loop(1, n_gr, send_piece, 0)

    def relay(k, carry):
        sender_pos = lax.rem(pos + line - k, line)
        first(k, sender_pos).wait_recv()

        def out(j, inner):
            forward(j, sender_pos, grp).start()
            return inner

        return lax.fori_loop(1, lines, out, carry)

    lax.fori_loop(1, line, relay, 0)

    def wait_piece(k, carry):
        sender = lax.rem(row + n_gr - k, n_gr)
        by_width(me, part_rows, part_width, lambda cols: piece_copy(k, row, cols).wait_send())
        by_width(me, part_rows, part_width, lambda cols: piece_copy(k, sender, cols).wait_recv())
        return carry

    lax.fori_loop(1, n_gr, wait_piece, 0)

    def add_piece(j, total):
        return total + recv_piece[j]

    summed = lax.fori_loop(0, n_gr, add_piece, jnp.zeros(recv_piece.shape[1:], jnp.float32))
    cross_slots[me] = summed.astype(cross_slots.dtype)

    def cross_copy(k, sender, cols):
        return pltpu.make_async_remote_copy(
            src_ref=cross_slots.at[me, :, pl.ds(0, cols)],
            dst_ref=cross_slots.at[sender, :, pl.ds(0, cols)],
            send_sem=psems.at[4, k],
            recv_sem=psems.at[5, sender],
            device_id=(row, lax.rem(me + k, n)),
            device_id_type=MESH_ID,
        )

    def send_cross(k, carry):
        by_width(me, part_rows, part_width, lambda cols: cross_copy(k, me, cols).start())
        return carry

    lax.fori_loop(1, n, send_cross, 0)

    def prior_copy(k, sender):
        return pltpu.make_async_remote_copy(
            src_ref=prior_ref,
            dst_ref=prior_slots.at[sender],
            send_sem=psems.at[6, k],
            recv_sem=psems.at[7, sender],
            device_id=(lax.rem(row + k, n_gr), me),
            device_id_type=MESH_ID,
        )

    def send_prior(k, carry):
        prior_copy(k, row).start()
        return carry

    lax.fori_loop(1, n_gr, send_prior, 0)
    prior_slots[row] = prior_ref[...]

    def wait_first(k, carry):
        first(k, pos).wait_send()
        return carry

    lax.fori_loop(1, line, wait_first, 0)

    def wait_sent(k, carry):
        def done(j, inner):
            forward(j, k, grp).wait_send()
            return inner

        return lax.fori_loop(1, lines, done, carry)

    lax.fori_loop(0, line, wait_sent, 0)

    def wait_lines(k, carry):
        whole_line(lax.rem(grp + lines - k, lines)).wait_recv()
        return carry

    lax.fori_loop(1, lines, wait_lines, 0)

    def wait_cross(k, carry):
        sender = lax.rem(me + n - k, n)
        by_width(me, part_rows, part_width, lambda cols: cross_copy(k, me, cols).wait_send())
        by_width(sender, part_rows, part_width, lambda cols: cross_copy(k, sender, cols).wait_recv())
        return carry

    lax.fori_loop(1, n, wait_cross, 0)
    cross_out[...] = cross_slots[...]

    def wait_prior(k, carry):
        prior_copy(k, row).wait_send()
        prior_copy(k, lax.rem(row + n_gr - k, n_gr)).wait_recv()
        return carry

    lax.fori_loop(1, n_gr, wait_prior, 0)
    prior_out[...] = prior_slots[...]


def gather_gc(block, part, prior_rows, n, line, n_gr):
    count, tiles, rows, width = block.shape
    vmem = pl.BlockSpec(memory_space=pltpu.VMEM)
    return pl.pallas_call(
        functools.partial(gather_kernel, n, line, n_gr),
        out_shape=(
            jax.ShapeDtypeStruct((count, tiles, rows * n, width), block.dtype),
            jax.ShapeDtypeStruct(part.shape, jnp.bfloat16),
            jax.ShapeDtypeStruct((n_gr,) + prior_rows.shape, prior_rows.dtype),
        ),
        in_specs=[pl.BlockSpec(memory_space=pl.ANY), vmem, vmem],
        out_specs=(pl.BlockSpec(memory_space=pl.ANY), vmem, vmem),
        scratch_shapes=[
            pltpu.VMEM(part.shape, part.dtype),
            pltpu.VMEM((n_gr,) + part.shape[1:], jnp.float32),
            pltpu.VMEM(part.shape, jnp.bfloat16),
            pltpu.VMEM((n_gr,) + prior_rows.shape, prior_rows.dtype),
            pltpu.SemaphoreType.DMA((8, max(n, n_gr))),
            pltpu.SemaphoreType.DMA((2 + line, line + n // line)),
            pltpu.SemaphoreType.DMA,
        ],
        compiler_params=pltpu.CompilerParams(collective_id=0, has_side_effects=True),
    )(block, part, prior_rows)


def reduce_kernel(n, crossing_ref, crossing_out, recv_crossing, sems):
    me = lax.axis_index("gr")
    col = lax.axis_index("gc")
    rows = crossing_out.shape[0]

    barrier = pltpu.get_barrier_semaphore()

    def greet_gr(k, carry):
        pl.semaphore_signal(barrier, inc=1, device_id=(lax.rem(me + k, n), col), device_id_type=MESH_ID)
        return carry

    lax.fori_loop(1, n, greet_gr, 0)
    pl.semaphore_wait(barrier, n - 1)

    def gr_copy(k, sender, src, dst, index):
        return pltpu.make_async_remote_copy(
            src_ref=src,
            dst_ref=dst.at[sender],
            send_sem=sems.at[index, k],
            recv_sem=sems.at[index + 1, sender],
            device_id=(lax.rem(me + k, n), col),
            device_id_type=MESH_ID,
        )

    def crossing_copy(k, sender):
        peer = lax.rem(me + k, n)
        src = crossing_ref.at[pl.ds(pl.multiple_of(peer * rows, rows), rows), :]
        return gr_copy(k, sender, src, recv_crossing, 0)

    def send(k, carry):
        crossing_copy(k, me).start()
        return carry

    lax.fori_loop(1, n, send, 0)
    recv_crossing[me] = crossing_ref[pl.ds(pl.multiple_of(me * rows, rows), rows), :]

    def wait(k, carry):
        sender = lax.rem(me + n - k, n)
        crossing_copy(k, me).wait_send()
        crossing_copy(k, sender).wait_recv()
        return carry

    lax.fori_loop(1, n, wait, 0)

    def add_crossing(j, total):
        return total + recv_crossing[j].astype(jnp.float32)

    crossing_out[...] = lax.fori_loop(0, n, add_crossing, jnp.zeros(crossing_out.shape, jnp.float32))


def reduce_gr(crossing_part, n):
    rows = crossing_part.shape[0] // n
    cols = crossing_part.shape[1]
    vmem = pl.BlockSpec(memory_space=pltpu.VMEM)
    return pl.pallas_call(
        functools.partial(reduce_kernel, n),
        out_shape=jax.ShapeDtypeStruct((rows, cols), jnp.float32),
        in_specs=[vmem],
        out_specs=vmem,
        scratch_shapes=[
            pltpu.VMEM((n, rows, cols), crossing_part.dtype),
            pltpu.SemaphoreType.DMA((2, n)),
        ],
        compiler_params=pltpu.CompilerParams(collective_id=1, has_side_effects=True),
    )(crossing_part)


def prior_factor_rows(prior_rows, below_shape):
    return prior_rows.reshape(-1, below_shape[3], below_shape[5])


def local(
    n_gc,
    n_gr,
    line,
    below_factor,
    panel_factor,
    prior_factor,
    diag_factor,
    diag_inverse,
    below_adjoint,
    panel_adjoint,
    prior_adjoint,
    diag_adjoint,
):
    tile_count = below_factor.shape[0]
    tile_rows = below_factor.shape[2]
    local_rows = tile_count * tile_rows
    local_cols = below_factor.shape[3] * below_factor.shape[5]
    own_rows = panel_factor.shape[2]
    width = panel_factor.shape[3]
    prior_local = prior_factor.shape[0]
    below_mat = below_factor.reshape(local_rows, local_cols)
    below_bar = below_adjoint.reshape(local_rows, local_cols)
    inverse_bf = diag_inverse.astype(jnp.bfloat16)
    own_grad = lax.dot_general(
        panel_adjoint.reshape(tile_count, own_rows, width),
        inverse_bf,
        (((2,), (0,)), ((), ())),
        preferred_element_type=jnp.float32,
    ).astype(jnp.bfloat16)
    panel_grad = own_grad.reshape(panel_adjoint.shape)
    own_part = lax.dot_general(
        own_grad,
        panel_factor.reshape(tile_count, own_rows, width),
        (((0, 1), (0, 1)), ((), ())),
        preferred_element_type=jnp.float32,
    ).astype(jnp.bfloat16)
    prior_here = prior_factor.reshape(prior_local, local_cols)
    whole, cross_rows, prior_rows = gather_gc(
        own_grad.reshape(1, tile_count, own_rows, width),
        own_part.reshape(n_gc, width // n_gc, width),
        prior_here,
        n_gc,
        line,
        n_gr,
    )
    grad_rows = whole[0].reshape(local_rows, width)
    crossing_part = row_product(grad_rows, below_mat).astype(jnp.bfloat16)
    crossing = reduce_gr(crossing_part, n_gr)
    summed = cross_rows.reshape(width, width).astype(jnp.float32)
    prior_whole = prior_rows.reshape(width, local_cols)
    diag_reduced = jnp.tril(diag_adjoint - summed)
    diag_gradient = diag_solve(diag_factor, diag_inverse, diag_reduced)
    below_prod = lax.dot_general(
        grad_rows.reshape(tile_count, tile_rows, width),
        prior_factor_rows(prior_rows, below_factor.shape),
        (((2,), (0,)), ((), ())),
        preferred_element_type=jnp.float32,
    ).reshape(below_adjoint.shape)
    below_new = (below_adjoint.astype(jnp.float32) - below_prod).astype(jnp.bfloat16)
    grid_row = lax.axis_index("gr")
    twice_rows = lax.dynamic_slice_in_dim(
        2.0 * diag_gradient, grid_row * prior_local, prior_local, 0
    ).astype(jnp.bfloat16)
    curvature = jnp.dot(twice_rows, prior_whole, preferred_element_type=jnp.float32)
    prior_bar = prior_adjoint.reshape(prior_local, local_cols).astype(jnp.float32)
    prior_new = (prior_bar - crossing - curvature).astype(jnp.bfloat16)
    return (
        below_new,
        panel_grad,
        prior_new.reshape(prior_adjoint.shape),
        diag_gradient,
    )


def line_length(mesh):
    column = list(mesh.devices[0])
    coords = [getattr(d, "coords", None) for d in column]
    if any(c is None for c in coords):
        return 8 if len(column) % 8 == 0 else len(column)
    first = coords[0][0]
    count = 0
    for c in coords:
        if c[0] != first:
            break
        count += 1
    return count if len(column) % count == 0 else len(column)


def solution(mesh):
    in_specs = (
        P(None, "gr", None, None, "gc", None),
        P(None, "gr", "gc", None),
        P("gr", None, "gc", None),
        P(),
        P(),
        P(None, "gr", None, None, "gc", None),
        P(None, "gr", "gc", None),
        P("gr", None, "gc", None),
        P(),
    )
    out_specs = (
        P(None, "gr", None, None, "gc", None),
        P(None, "gr", "gc", None),
        P("gr", None, "gc", None),
        P(),
    )
    return jax.shard_map(
        functools.partial(local, mesh.shape["gc"], mesh.shape["gr"], line_length(mesh)),
        mesh=mesh,
        in_specs=in_specs,
        out_specs=out_specs,
        check_vma=False,
    )
```

```python
import functools

import jax
import jax.numpy as jnp
from jax import lax
from jax.experimental import pallas as pl
from jax.experimental.pallas import tpu as pltpu
from jax.sharding import PartitionSpec as P

MESH_ID = pl.DeviceIdType.MESH


def row_product(left_rows, right_rows):
    return lax.dot_general(
        left_rows, right_rows, (((0,), (0,)), ((), ())), preferred_element_type=jnp.float32
    )


def diag_solve(diag_factor, diag_inverse, diag_reduced):
    highest = lax.Precision.HIGH
    chol_proj = jnp.dot(diag_factor.T, diag_reduced, precision=highest)
    index_row = lax.broadcasted_iota(jnp.int32, chol_proj.shape, 0)
    index_col = lax.broadcasted_iota(jnp.int32, chol_proj.shape, 1)
    phi_lower = jnp.where(
        index_row > index_col,
        chol_proj,
        jnp.where(index_row == index_col, chol_proj - 0.5 * chol_proj, 0.0),
    )
    symmetric = 0.5 * (phi_lower + phi_lower.T)
    left_side = jnp.dot(diag_inverse.T, symmetric, precision=highest)
    return jnp.dot(left_side, diag_inverse, precision=highest)


def by_width(index, rows, width, action):
    group = (rows * (index + 1) - 1) // 128
    for j in range(width // 128):
        @pl.when(group == j)
        def _():
            action(128 * (j + 1))


def gather_kernel(n, line, n_gr, x_ref, p_ref, prior_ref, out_ref, cross_out, prior_out, precv, recv_piece,
                  cross_slots, prior_slots, psems, sems, local_sem):
    me = lax.axis_index("gc")
    row = lax.axis_index("gr")
    rows = x_ref.shape[2]
    lines = n // line
    pos = lax.rem(me, line)
    grp = me // line
    base = grp * line

    def line_peer(k):
        return base + lax.rem(pos + k, line)

    def cross_peer(k):
        return lax.rem(grp + k, lines) * line + pos

    part_rows, part_width = p_ref.shape[1], p_ref.shape[2]
    precv[...] = jnp.zeros(precv.shape, precv.dtype)
    recv_piece[...] = jnp.zeros(recv_piece.shape, recv_piece.dtype)
    cross_slots[...] = jnp.zeros(cross_slots.shape, cross_slots.dtype)
    barrier = pltpu.get_barrier_semaphore()

    def greet(k, carry):
        pl.semaphore_signal(barrier, inc=1, device_id=(row, lax.rem(me + k, n)), device_id_type=MESH_ID)
        return carry

    def greet_gr(k, carry):
        pl.semaphore_signal(barrier, inc=1, device_id=(lax.rem(row + k, n_gr), me), device_id_type=MESH_ID)
        return carry

    lax.fori_loop(1, n, greet, 0)
    lax.fori_loop(1, n_gr, greet_gr, 0)
    pl.semaphore_wait(barrier, n + n_gr - 2)

    def part_copy(k, sender, cols):
        peer = lax.rem(me + k, n)
        return pltpu.make_async_remote_copy(
            src_ref=p_ref.at[peer, :, pl.ds(0, cols)],
            dst_ref=precv.at[sender, :, pl.ds(0, cols)],
            send_sem=psems.at[0, k],
            recv_sem=psems.at[1, sender],
            device_id=(row, peer),
            device_id_type=MESH_ID,
        )

    def send_parts(k, carry):
        by_width(lax.rem(me + k, n), part_rows, part_width, lambda cols: part_copy(k, me, cols).start())
        return carry

    lax.fori_loop(1, n, send_parts, 0)

    own = pltpu.make_async_copy(x_ref, out_ref.at[:, :, pl.ds(me * rows, rows), :], local_sem)
    own.start()

    def first(k, sender_pos):
        return pltpu.make_async_remote_copy(
            src_ref=x_ref,
            dst_ref=out_ref.at[:, :, pl.ds((base + sender_pos) * rows, rows), :],
            send_sem=sems.at[0, k],
            recv_sem=sems.at[1, sender_pos],
            device_id=(row, line_peer(k)),
            device_id_type=MESH_ID,
        )

    def send_first(k, carry):
        first(k, pos).start()
        return carry

    lax.fori_loop(1, line, send_first, 0)


    span = line * rows

    def forward(k, block_pos, sender_grp):
        slot = pl.ds((grp * line + block_pos) * rows, rows)
        return pltpu.make_async_remote_copy(
            src_ref=out_ref.at[:, :, slot, :],
            dst_ref=out_ref.at[:, :, slot, :],
            send_sem=sems.at[2 + block_pos, k],
            recv_sem=sems.at[1, line + sender_grp],
            device_id=(row, cross_peer(k)),
            device_id_type=MESH_ID,
        )

    def whole_line(sender_grp):
        return pltpu.make_async_remote_copy(
            src_ref=out_ref.at[:, :, pl.ds(sender_grp * span, span), :],
            dst_ref=out_ref.at[:, :, pl.ds(sender_grp * span, span), :],
            send_sem=sems.at[0, 0],
            recv_sem=sems.at[1, line + sender_grp],
            device_id=(row, cross_peer(1)),
            device_id_type=MESH_ID,
        )

    own.wait()

    def send_own(k, carry):
        forward(k, pos, grp).start()
        return carry

    lax.fori_loop(1, lines, send_own, 0)


    precv[me] = p_ref[me]

    def wait_parts(k, carry):
        sender = lax.rem(me + n - k, n)
        by_width(lax.rem(me + k, n), part_rows, part_width, lambda cols: part_copy(k, me, cols).wait_send())
        by_width(me, part_rows, part_width, lambda cols: part_copy(k, sender, cols).wait_recv())
        return carry

    lax.fori_loop(1, n, wait_parts, 0)

    def add_part(j, total):
        return total + precv[j].astype(jnp.float32)

    piece = lax.fori_loop(0, n, add_part, jnp.zeros(recv_piece.shape[1:], jnp.float32))
    recv_piece[row] = piece

    def piece_copy(k, sender, cols):
        return pltpu.make_async_remote_copy(
            src_ref=recv_piece.at[row, :, pl.ds(0, cols)],
            dst_ref=recv_piece.at[sender, :, pl.ds(0, cols)],
            send_sem=psems.at[2, k],
            recv_sem=psems.at[3, sender],
            device_id=(lax.rem(row + k, n_gr), me),
            device_id_type=MESH_ID,
        )

    def send_piece(k, carry):
        by_width(me, part_rows, part_width, lambda cols: piece_copy(k, row, cols).start())
        return carry

    lax.fori_loop(1, n_gr, send_piece, 0)

    def relay(k, carry):
        sender_pos = lax.rem(pos + line - k, line)
        first(k, sender_pos).wait_recv()

        def out(j, inner):
            forward(j, sender_pos, grp).start()
            return inner

        return lax.fori_loop(1, lines, out, carry)

    lax.fori_loop(1, line, relay, 0)

    def wait_piece(k, carry):
        sender = lax.rem(row + n_gr - k, n_gr)
        by_width(me, part_rows, part_width, lambda cols: piece_copy(k, row, cols).wait_send())
        by_width(me, part_rows, part_width, lambda cols: piece_copy(k, sender, cols).wait_recv())
        return carry

    lax.fori_loop(1, n_gr, wait_piece, 0)

    def add_piece(j, total):
        return total + recv_piece[j]

    summed = lax.fori_loop(0, n_gr, add_piece, jnp.zeros(recv_piece.shape[1:], jnp.float32))
    cross_slots[me] = summed.astype(cross_slots.dtype)

    def cross_copy(k, sender, cols):
        return pltpu.make_async_remote_copy(
            src_ref=cross_slots.at[me, :, pl.ds(0, cols)],
            dst_ref=cross_slots.at[sender, :, pl.ds(0, cols)],
            send_sem=psems.at[4, k],
            recv_sem=psems.at[5, sender],
            device_id=(row, lax.rem(me + k, n)),
            device_id_type=MESH_ID,
        )

    def send_cross(k, carry):
        by_width(me, part_rows, part_width, lambda cols: cross_copy(k, me, cols).start())
        return carry

    lax.fori_loop(1, n, send_cross, 0)

    def prior_copy(k, sender):
        return pltpu.make_async_remote_copy(
            src_ref=prior_ref,
            dst_ref=prior_slots.at[sender],
            send_sem=psems.at[6, k],
            recv_sem=psems.at[7, sender],
            device_id=(lax.rem(row + k, n_gr), me),
            device_id_type=MESH_ID,
        )

    def send_prior(k, carry):
        prior_copy(k, row).start()
        return carry

    lax.fori_loop(1, n_gr, send_prior, 0)
    prior_slots[row] = prior_ref[...]

    def wait_first(k, carry):
        first(k, pos).wait_send()
        return carry

    lax.fori_loop(1, line, wait_first, 0)

    def wait_sent(k, carry):
        def done(j, inner):
            forward(j, k, grp).wait_send()
            return inner

        return lax.fori_loop(1, lines, done, carry)

    lax.fori_loop(0, line, wait_sent, 0)

    def wait_lines(k, carry):
        whole_line(lax.rem(grp + lines - k, lines)).wait_recv()
        return carry

    lax.fori_loop(1, lines, wait_lines, 0)

    def wait_cross(k, carry):
        sender = lax.rem(me + n - k, n)
        by_width(me, part_rows, part_width, lambda cols: cross_copy(k, me, cols).wait_send())
        by_width(sender, part_rows, part_width, lambda cols: cross_copy(k, sender, cols).wait_recv())
        return carry

    lax.fori_loop(1, n, wait_cross, 0)
    cross_out[...] = cross_slots[...]

    def wait_prior(k, carry):
        prior_copy(k, row).wait_send()
        prior_copy(k, lax.rem(row + n_gr - k, n_gr)).wait_recv()
        return carry

    lax.fori_loop(1, n_gr, wait_prior, 0)
    prior_out[...] = prior_slots[...]


def gather_gc(block, part, prior_rows, n, line, n_gr):
    count, tiles, rows, width = block.shape
    vmem = pl.BlockSpec(memory_space=pltpu.VMEM)
    return pl.pallas_call(
        functools.partial(gather_kernel, n, line, n_gr),
        out_shape=(
            jax.ShapeDtypeStruct((count, tiles, rows * n, width), block.dtype),
            jax.ShapeDtypeStruct(part.shape, jnp.bfloat16),
            jax.ShapeDtypeStruct((n_gr,) + prior_rows.shape, prior_rows.dtype),
        ),
        in_specs=[pl.BlockSpec(memory_space=pl.ANY), vmem, vmem],
        out_specs=(pl.BlockSpec(memory_space=pl.ANY), vmem, vmem),
        scratch_shapes=[
            pltpu.VMEM(part.shape, part.dtype),
            pltpu.VMEM((n_gr,) + part.shape[1:], jnp.float32),
            pltpu.VMEM(part.shape, jnp.bfloat16),
            pltpu.VMEM((n_gr,) + prior_rows.shape, prior_rows.dtype),
            pltpu.SemaphoreType.DMA((8, max(n, n_gr))),
            pltpu.SemaphoreType.DMA((2 + line, line + n // line)),
            pltpu.SemaphoreType.DMA,
        ],
        compiler_params=pltpu.CompilerParams(collective_id=0, has_side_effects=True),
    )(block, part, prior_rows)


def reduce_kernel(n, crossing_ref, crossing_out, recv_crossing, sems):
    me = lax.axis_index("gr")
    col = lax.axis_index("gc")
    rows = crossing_out.shape[0]

    barrier = pltpu.get_barrier_semaphore()

    def greet_gr(k, carry):
        pl.semaphore_signal(barrier, inc=1, device_id=(lax.rem(me + k, n), col), device_id_type=MESH_ID)
        return carry

    lax.fori_loop(1, n, greet_gr, 0)
    pl.semaphore_wait(barrier, n - 1)

    def gr_copy(k, sender, src, dst, index):
        return pltpu.make_async_remote_copy(
            src_ref=src,
            dst_ref=dst.at[sender],
            send_sem=sems.at[index, k],
            recv_sem=sems.at[index + 1, sender],
            device_id=(lax.rem(me + k, n), col),
            device_id_type=MESH_ID,
        )

    def crossing_copy(k, sender):
        peer = lax.rem(me + k, n)
        src = crossing_ref.at[pl.ds(pl.multiple_of(peer * rows, rows), rows), :]
        return gr_copy(k, sender, src, recv_crossing, 0)

    def send(k, carry):
        crossing_copy(k, me).start()
        return carry

    lax.fori_loop(1, n, send, 0)
    recv_crossing[me] = crossing_ref[pl.ds(pl.multiple_of(me * rows, rows), rows), :]

    def wait(k, carry):
        sender = lax.rem(me + n - k, n)
        crossing_copy(k, me).wait_send()
        crossing_copy(k, sender).wait_recv()
        return carry

    lax.fori_loop(1, n, wait, 0)

    def add_crossing(j, total):
        return total + recv_crossing[j].astype(jnp.float32)

    crossing_out[...] = lax.fori_loop(0, n, add_crossing, jnp.zeros(crossing_out.shape, jnp.float32))


def reduce_gr(crossing_part, n):
    rows = crossing_part.shape[0] // n
    cols = crossing_part.shape[1]
    vmem = pl.BlockSpec(memory_space=pltpu.VMEM)
    return pl.pallas_call(
        functools.partial(reduce_kernel, n),
        out_shape=jax.ShapeDtypeStruct((rows, cols), jnp.float32),
        in_specs=[vmem],
        out_specs=vmem,
        scratch_shapes=[
            pltpu.VMEM((n, rows, cols), crossing_part.dtype),
            pltpu.SemaphoreType.DMA((2, n)),
        ],
        compiler_params=pltpu.CompilerParams(collective_id=1, has_side_effects=True),
    )(crossing_part)


def prior_factor_rows(prior_rows, below_shape):
    return prior_rows.reshape(-1, below_shape[3], below_shape[5])


def local(
    n_gc,
    n_gr,
    line,
    below_factor,
    panel_factor,
    prior_factor,
    diag_factor,
    diag_inverse,
    below_adjoint,
    panel_adjoint,
    prior_adjoint,
    diag_adjoint,
):
    tile_count = below_factor.shape[0]
    tile_rows = below_factor.shape[2]
    local_rows = tile_count * tile_rows
    local_cols = below_factor.shape[3] * below_factor.shape[5]
    own_rows = panel_factor.shape[2]
    width = panel_factor.shape[3]
    prior_local = prior_factor.shape[0]
    below_mat = below_factor.reshape(local_rows, local_cols)
    below_bar = below_adjoint.reshape(local_rows, local_cols)
    inverse_bf = diag_inverse.astype(jnp.bfloat16)
    own_grad = lax.dot_general(
        panel_adjoint.reshape(tile_count, own_rows, width),
        inverse_bf,
        (((2,), (0,)), ((), ())),
        preferred_element_type=jnp.float32,
    ).astype(jnp.bfloat16)
    panel_grad = own_grad.reshape(panel_adjoint.shape)
    own_part = lax.dot_general(
        own_grad,
        panel_factor.reshape(tile_count, own_rows, width),
        (((0, 1), (0, 1)), ((), ())),
        preferred_element_type=jnp.float32,
    ).astype(jnp.bfloat16)
    prior_here = prior_factor.reshape(prior_local, local_cols)
    whole, cross_rows, prior_rows = gather_gc(
        own_grad.reshape(1, tile_count, own_rows, width),
        own_part.reshape(n_gc, width // n_gc, width),
        prior_here,
        n_gc,
        line,
        n_gr,
    )
    grad_rows = whole[0].reshape(local_rows, width)
    crossing_part = lax.dot_general(
        grad_rows.reshape(tile_count, tile_rows, width),
        below_factor.reshape(tile_count, tile_rows, local_cols),
        (((0, 1), (0, 1)), ((), ())),
        preferred_element_type=jnp.float32,
    ).astype(jnp.bfloat16)
    crossing = reduce_gr(crossing_part, n_gr)
    summed = cross_rows.reshape(width, width).astype(jnp.float32)
    prior_whole = prior_rows.reshape(width, local_cols)
    diag_reduced = jnp.tril(diag_adjoint - summed)
    diag_gradient = diag_solve(diag_factor, diag_inverse, diag_reduced)
    below_prod = lax.dot_general(
        grad_rows.reshape(tile_count, tile_rows, width),
        prior_factor_rows(prior_rows, below_factor.shape),
        (((2,), (0,)), ((), ())),
        preferred_element_type=jnp.float32,
    ).reshape(below_adjoint.shape)
    below_new = (below_adjoint.astype(jnp.float32) - below_prod).astype(jnp.bfloat16)
    grid_row = lax.axis_index("gr")
    twice_rows = lax.dynamic_slice_in_dim(
        2.0 * diag_gradient, grid_row * prior_local, prior_local, 0
    ).astype(jnp.bfloat16)
    curvature = jnp.dot(twice_rows, prior_whole, preferred_element_type=jnp.float32)
    prior_bar = prior_adjoint.reshape(prior_local, local_cols).astype(jnp.float32)
    prior_new = (prior_bar - crossing - curvature).astype(jnp.bfloat16)
    return (
        below_new,
        panel_grad,
        prior_new.reshape(prior_adjoint.shape),
        diag_gradient,
    )


def line_length(mesh):
    column = list(mesh.devices[0])
    coords = [getattr(d, "coords", None) for d in column]
    if any(c is None for c in coords):
        return 8 if len(column) % 8 == 0 else len(column)
    first = coords[0][0]
    count = 0
    for c in coords:
        if c[0] != first:
            break
        count += 1
    return count if len(column) % count == 0 else len(column)


def solution(mesh):
    in_specs = (
        P(None, "gr", None, None, "gc", None),
        P(None, "gr", "gc", None),
        P("gr", None, "gc", None),
        P(),
        P(),
        P(None, "gr", None, None, "gc", None),
        P(None, "gr", "gc", None),
        P("gr", None, "gc", None),
        P(),
    )
    out_specs = (
        P(None, "gr", None, None, "gc", None),
        P(None, "gr", "gc", None),
        P("gr", None, "gc", None),
        P(),
    )
    return jax.shard_map(
        functools.partial(local, mesh.shape["gc"], mesh.shape["gr"], line_length(mesh)),
        mesh=mesh,
        in_specs=in_specs,
        out_specs=out_specs,
        check_vma=False,
    )
```

```python
import functools

import jax
import jax.numpy as jnp
from jax import lax
from jax.experimental import pallas as pl
from jax.experimental.pallas import tpu as pltpu
from jax.sharding import PartitionSpec as P

MESH_ID = pl.DeviceIdType.MESH


def row_product(left_rows, right_rows):
    return lax.dot_general(
        left_rows, right_rows, (((0,), (0,)), ((), ())), preferred_element_type=jnp.float32
    )


def diag_solve(diag_factor, diag_inverse, diag_reduced):
    highest = lax.Precision.HIGH
    chol_proj = jnp.dot(diag_factor.T, diag_reduced, precision=highest)
    index_row = lax.broadcasted_iota(jnp.int32, chol_proj.shape, 0)
    index_col = lax.broadcasted_iota(jnp.int32, chol_proj.shape, 1)
    phi_lower = jnp.where(
        index_row > index_col,
        chol_proj,
        jnp.where(index_row == index_col, chol_proj - 0.5 * chol_proj, 0.0),
    )
    symmetric = 0.5 * (phi_lower + phi_lower.T)
    left_side = jnp.dot(diag_inverse.T, symmetric, precision=highest)
    return jnp.dot(left_side, diag_inverse, precision=highest)


def by_width(index, rows, width, action):
    group = (rows * (index + 1) - 1) // 128
    for j in range(width // 128):
        @pl.when(group == j)
        def _():
            action(128 * (j + 1))


def gather_kernel(n, line, n_gr, x_ref, p_ref, prior_ref, out_ref, cross_out, prior_out, precv, recv_piece,
                  cross_slots, prior_slots, psems, sems, local_sem):
    me = lax.axis_index("gc")
    row = lax.axis_index("gr")
    rows = x_ref.shape[2]
    lines = n // line
    pos = lax.rem(me, line)
    grp = me // line
    base = grp * line

    def line_peer(k):
        return base + lax.rem(pos + k, line)

    def cross_peer(k):
        return lax.rem(grp + k, lines) * line + pos

    part_rows, part_width = p_ref.shape[1], p_ref.shape[2]
    precv[...] = jnp.zeros(precv.shape, precv.dtype)
    recv_piece[...] = jnp.zeros(recv_piece.shape, recv_piece.dtype)
    cross_slots[...] = jnp.zeros(cross_slots.shape, cross_slots.dtype)
    barrier = pltpu.get_barrier_semaphore()

    def greet(k, carry):
        pl.semaphore_signal(barrier, inc=1, device_id=(row, lax.rem(me + k, n)), device_id_type=MESH_ID)
        return carry

    def greet_gr(k, carry):
        pl.semaphore_signal(barrier, inc=1, device_id=(lax.rem(row + k, n_gr), me), device_id_type=MESH_ID)
        return carry

    lax.fori_loop(1, n, greet, 0)
    lax.fori_loop(1, n_gr, greet_gr, 0)
    pl.semaphore_wait(barrier, n + n_gr - 2)

    def part_copy(k, sender, cols):
        peer = lax.rem(me + k, n)
        return pltpu.make_async_remote_copy(
            src_ref=p_ref.at[peer, :, pl.ds(0, cols)],
            dst_ref=precv.at[sender, :, pl.ds(0, cols)],
            send_sem=psems.at[0, k],
            recv_sem=psems.at[1, sender],
            device_id=(row, peer),
            device_id_type=MESH_ID,
        )

    def send_parts(k, carry):
        by_width(lax.rem(me + k, n), part_rows, part_width, lambda cols: part_copy(k, me, cols).start())
        return carry

    lax.fori_loop(1, n, send_parts, 0)

    own = pltpu.make_async_copy(x_ref, out_ref.at[:, :, pl.ds(me * rows, rows), :], local_sem)
    own.start()

    def first(k, sender_pos):
        return pltpu.make_async_remote_copy(
            src_ref=x_ref,
            dst_ref=out_ref.at[:, :, pl.ds((base + sender_pos) * rows, rows), :],
            send_sem=sems.at[0, k],
            recv_sem=sems.at[1, sender_pos],
            device_id=(row, line_peer(k)),
            device_id_type=MESH_ID,
        )

    def send_first(k, carry):
        first(k, pos).start()
        return carry

    lax.fori_loop(1, line, send_first, 0)


    span = line * rows

    def forward(k, block_pos, sender_grp):
        slot = pl.ds((grp * line + block_pos) * rows, rows)
        return pltpu.make_async_remote_copy(
            src_ref=out_ref.at[:, :, slot, :],
            dst_ref=out_ref.at[:, :, slot, :],
            send_sem=sems.at[2 + block_pos, k],
            recv_sem=sems.at[1, line + sender_grp],
            device_id=(row, cross_peer(k)),
            device_id_type=MESH_ID,
        )

    def whole_line(sender_grp):
        return pltpu.make_async_remote_copy(
            src_ref=out_ref.at[:, :, pl.ds(sender_grp * span, span), :],
            dst_ref=out_ref.at[:, :, pl.ds(sender_grp * span, span), :],
            send_sem=sems.at[0, 0],
            recv_sem=sems.at[1, line + sender_grp],
            device_id=(row, cross_peer(1)),
            device_id_type=MESH_ID,
        )

    own.wait()

    def send_own(k, carry):
        forward(k, pos, grp).start()
        return carry

    lax.fori_loop(1, lines, send_own, 0)


    precv[me] = p_ref[me]

    def wait_parts(k, carry):
        sender = lax.rem(me + n - k, n)
        by_width(lax.rem(me + k, n), part_rows, part_width, lambda cols: part_copy(k, me, cols).wait_send())
        by_width(me, part_rows, part_width, lambda cols: part_copy(k, sender, cols).wait_recv())
        return carry

    lax.fori_loop(1, n, wait_parts, 0)

    def add_part(j, total):
        return total + precv[j].astype(jnp.float32)

    piece = lax.fori_loop(0, n, add_part, jnp.zeros(recv_piece.shape[1:], jnp.float32))
    recv_piece[row] = piece.astype(recv_piece.dtype)

    def piece_copy(k, sender, cols):
        return pltpu.make_async_remote_copy(
            src_ref=recv_piece.at[row, :, pl.ds(0, cols)],
            dst_ref=recv_piece.at[sender, :, pl.ds(0, cols)],
            send_sem=psems.at[2, k],
            recv_sem=psems.at[3, sender],
            device_id=(lax.rem(row + k, n_gr), me),
            device_id_type=MESH_ID,
        )

    def send_piece(k, carry):
        by_width(me, part_rows, part_width, lambda cols: piece_copy(k, row, cols).start())
        return carry

    lax.fori_loop(1, n_gr, send_piece, 0)

    def relay(k, carry):
        sender_pos = lax.rem(pos + line - k, line)
        first(k, sender_pos).wait_recv()

        def out(j, inner):
            forward(j, sender_pos, grp).start()
            return inner

        return lax.fori_loop(1, lines, out, carry)

    lax.fori_loop(1, line, relay, 0)

    def wait_piece(k, carry):
        sender = lax.rem(row + n_gr - k, n_gr)
        by_width(me, part_rows, part_width, lambda cols: piece_copy(k, row, cols).wait_send())
        by_width(me, part_rows, part_width, lambda cols: piece_copy(k, sender, cols).wait_recv())
        return carry

    lax.fori_loop(1, n_gr, wait_piece, 0)

    def add_piece(j, total):
        return total + recv_piece[j].astype(jnp.float32)

    summed = lax.fori_loop(0, n_gr, add_piece, jnp.zeros(recv_piece.shape[1:], jnp.float32))
    cross_slots[me] = summed.astype(cross_slots.dtype)

    def cross_copy(k, sender, cols):
        return pltpu.make_async_remote_copy(
            src_ref=cross_slots.at[me, :, pl.ds(0, cols)],
            dst_ref=cross_slots.at[sender, :, pl.ds(0, cols)],
            send_sem=psems.at[4, k],
            recv_sem=psems.at[5, sender],
            device_id=(row, lax.rem(me + k, n)),
            device_id_type=MESH_ID,
        )

    def send_cross(k, carry):
        by_width(me, part_rows, part_width, lambda cols: cross_copy(k, me, cols).start())
        return carry

    lax.fori_loop(1, n, send_cross, 0)

    def prior_copy(k, sender):
        return pltpu.make_async_remote_copy(
            src_ref=prior_ref,
            dst_ref=prior_slots.at[sender],
            send_sem=psems.at[6, k],
            recv_sem=psems.at[7, sender],
            device_id=(lax.rem(row + k, n_gr), me),
            device_id_type=MESH_ID,
        )

    def send_prior(k, carry):
        prior_copy(k, row).start()
        return carry

    lax.fori_loop(1, n_gr, send_prior, 0)
    prior_slots[row] = prior_ref[...]

    def wait_first(k, carry):
        first(k, pos).wait_send()
        return carry

    lax.fori_loop(1, line, wait_first, 0)

    def wait_sent(k, carry):
        def done(j, inner):
            forward(j, k, grp).wait_send()
            return inner

        return lax.fori_loop(1, lines, done, carry)

    lax.fori_loop(0, line, wait_sent, 0)

    def wait_lines(k, carry):
        whole_line(lax.rem(grp + lines - k, lines)).wait_recv()
        return carry

    lax.fori_loop(1, lines, wait_lines, 0)

    def wait_cross(k, carry):
        sender = lax.rem(me + n - k, n)
        by_width(me, part_rows, part_width, lambda cols: cross_copy(k, me, cols).wait_send())
        by_width(sender, part_rows, part_width, lambda cols: cross_copy(k, sender, cols).wait_recv())
        return carry

    lax.fori_loop(1, n, wait_cross, 0)
    cross_out[...] = cross_slots[...]

    def wait_prior(k, carry):
        prior_copy(k, row).wait_send()
        prior_copy(k, lax.rem(row + n_gr - k, n_gr)).wait_recv()
        return carry

    lax.fori_loop(1, n_gr, wait_prior, 0)
    prior_out[...] = prior_slots[...]


def gather_gc(block, part, prior_rows, n, line, n_gr):
    count, tiles, rows, width = block.shape
    vmem = pl.BlockSpec(memory_space=pltpu.VMEM)
    return pl.pallas_call(
        functools.partial(gather_kernel, n, line, n_gr),
        out_shape=(
            jax.ShapeDtypeStruct((count, tiles, rows * n, width), block.dtype),
            jax.ShapeDtypeStruct(part.shape, jnp.bfloat16),
            jax.ShapeDtypeStruct((n_gr,) + prior_rows.shape, prior_rows.dtype),
        ),
        in_specs=[pl.BlockSpec(memory_space=pl.ANY), vmem, vmem],
        out_specs=(pl.BlockSpec(memory_space=pl.ANY), vmem, vmem),
        scratch_shapes=[
            pltpu.VMEM(part.shape, part.dtype),
            pltpu.VMEM((n_gr,) + part.shape[1:], jnp.bfloat16),
            pltpu.VMEM(part.shape, jnp.bfloat16),
            pltpu.VMEM((n_gr,) + prior_rows.shape, prior_rows.dtype),
            pltpu.SemaphoreType.DMA((8, max(n, n_gr))),
            pltpu.SemaphoreType.DMA((2 + line, line + n // line)),
            pltpu.SemaphoreType.DMA,
        ],
        compiler_params=pltpu.CompilerParams(collective_id=0, has_side_effects=True),
    )(block, part, prior_rows)


def reduce_kernel(n, crossing_ref, crossing_out, recv_crossing, sems):
    me = lax.axis_index("gr")
    col = lax.axis_index("gc")
    rows = crossing_out.shape[0]

    barrier = pltpu.get_barrier_semaphore()

    def greet_gr(k, carry):
        pl.semaphore_signal(barrier, inc=1, device_id=(lax.rem(me + k, n), col), device_id_type=MESH_ID)
        return carry

    lax.fori_loop(1, n, greet_gr, 0)
    pl.semaphore_wait(barrier, n - 1)

    def gr_copy(k, sender, src, dst, index):
        return pltpu.make_async_remote_copy(
            src_ref=src,
            dst_ref=dst.at[sender],
            send_sem=sems.at[index, k],
            recv_sem=sems.at[index + 1, sender],
            device_id=(lax.rem(me + k, n), col),
            device_id_type=MESH_ID,
        )

    def crossing_copy(k, sender):
        peer = lax.rem(me + k, n)
        src = crossing_ref.at[pl.ds(pl.multiple_of(peer * rows, rows), rows), :]
        return gr_copy(k, sender, src, recv_crossing, 0)

    def send(k, carry):
        crossing_copy(k, me).start()
        return carry

    lax.fori_loop(1, n, send, 0)
    recv_crossing[me] = crossing_ref[pl.ds(pl.multiple_of(me * rows, rows), rows), :]

    def wait(k, carry):
        sender = lax.rem(me + n - k, n)
        crossing_copy(k, me).wait_send()
        crossing_copy(k, sender).wait_recv()
        return carry

    lax.fori_loop(1, n, wait, 0)

    def add_crossing(j, total):
        return total + recv_crossing[j].astype(jnp.float32)

    crossing_out[...] = lax.fori_loop(0, n, add_crossing, jnp.zeros(crossing_out.shape, jnp.float32))


def reduce_gr(crossing_part, n):
    rows = crossing_part.shape[0] // n
    cols = crossing_part.shape[1]
    vmem = pl.BlockSpec(memory_space=pltpu.VMEM)
    return pl.pallas_call(
        functools.partial(reduce_kernel, n),
        out_shape=jax.ShapeDtypeStruct((rows, cols), jnp.float32),
        in_specs=[vmem],
        out_specs=vmem,
        scratch_shapes=[
            pltpu.VMEM((n, rows, cols), crossing_part.dtype),
            pltpu.SemaphoreType.DMA((2, n)),
        ],
        compiler_params=pltpu.CompilerParams(collective_id=1, has_side_effects=True),
    )(crossing_part)


def prior_factor_rows(prior_rows, below_shape):
    return prior_rows.reshape(-1, below_shape[3], below_shape[5])


def local(
    n_gc,
    n_gr,
    line,
    below_factor,
    panel_factor,
    prior_factor,
    diag_factor,
    diag_inverse,
    below_adjoint,
    panel_adjoint,
    prior_adjoint,
    diag_adjoint,
):
    tile_count = below_factor.shape[0]
    tile_rows = below_factor.shape[2]
    local_rows = tile_count * tile_rows
    local_cols = below_factor.shape[3] * below_factor.shape[5]
    own_rows = panel_factor.shape[2]
    width = panel_factor.shape[3]
    prior_local = prior_factor.shape[0]
    below_mat = below_factor.reshape(local_rows, local_cols)
    below_bar = below_adjoint.reshape(local_rows, local_cols)
    inverse_bf = diag_inverse.astype(jnp.bfloat16)
    own_grad = lax.dot_general(
        panel_adjoint.reshape(tile_count, own_rows, width),
        inverse_bf,
        (((2,), (0,)), ((), ())),
        preferred_element_type=jnp.float32,
    ).astype(jnp.bfloat16)
    panel_grad = own_grad.reshape(panel_adjoint.shape)
    own_part = lax.dot_general(
        own_grad,
        panel_factor.reshape(tile_count, own_rows, width),
        (((0, 1), (0, 1)), ((), ())),
        preferred_element_type=jnp.float32,
    ).astype(jnp.bfloat16)
    prior_here = prior_factor.reshape(prior_local, local_cols)
    whole, cross_rows, prior_rows = gather_gc(
        own_grad.reshape(1, tile_count, own_rows, width),
        own_part.reshape(n_gc, width // n_gc, width),
        prior_here,
        n_gc,
        line,
        n_gr,
    )
    grad_rows = whole[0].reshape(local_rows, width)
    crossing_part = row_product(grad_rows, below_mat).astype(jnp.bfloat16)
    crossing = reduce_gr(crossing_part, n_gr)
    summed = cross_rows.reshape(width, width).astype(jnp.float32)
    prior_whole = prior_rows.reshape(width, local_cols)
    diag_reduced = jnp.tril(diag_adjoint - summed)
    diag_gradient = diag_solve(diag_factor, diag_inverse, diag_reduced)
    below_prod = lax.dot_general(
        grad_rows.reshape(tile_count, tile_rows, width),
        prior_factor_rows(prior_rows, below_factor.shape),
        (((2,), (0,)), ((), ())),
        preferred_element_type=jnp.float32,
    ).reshape(below_adjoint.shape)
    below_new = (below_adjoint.astype(jnp.float32) - below_prod).astype(jnp.bfloat16)
    grid_row = lax.axis_index("gr")
    twice_rows = lax.dynamic_slice_in_dim(
        2.0 * diag_gradient, grid_row * prior_local, prior_local, 0
    ).astype(jnp.bfloat16)
    curvature = jnp.dot(twice_rows, prior_whole, preferred_element_type=jnp.float32)
    prior_bar = prior_adjoint.reshape(prior_local, local_cols).astype(jnp.float32)
    prior_new = (prior_bar - crossing - curvature).astype(jnp.bfloat16)
    return (
        below_new,
        panel_grad,
        prior_new.reshape(prior_adjoint.shape),
        diag_gradient,
    )


def line_length(mesh):
    column = list(mesh.devices[0])
    coords = [getattr(d, "coords", None) for d in column]
    if any(c is None for c in coords):
        return 8 if len(column) % 8 == 0 else len(column)
    first = coords[0][0]
    count = 0
    for c in coords:
        if c[0] != first:
            break
        count += 1
    return count if len(column) % count == 0 else len(column)


def solution(mesh):
    in_specs = (
        P(None, "gr", None, None, "gc", None),
        P(None, "gr", "gc", None),
        P("gr", None, "gc", None),
        P(),
        P(),
        P(None, "gr", None, None, "gc", None),
        P(None, "gr", "gc", None),
        P("gr", None, "gc", None),
        P(),
    )
    out_specs = (
        P(None, "gr", None, None, "gc", None),
        P(None, "gr", "gc", None),
        P("gr", None, "gc", None),
        P(),
    )
    return jax.shard_map(
        functools.partial(local, mesh.shape["gc"], mesh.shape["gr"], line_length(mesh)),
        mesh=mesh,
        in_specs=in_specs,
        out_specs=out_specs,
        check_vma=False,
    )
```

```python
import functools

import jax
import jax.numpy as jnp
from jax import lax
from jax.experimental import pallas as pl
from jax.experimental.pallas import tpu as pltpu
from jax.sharding import PartitionSpec as P

MESH_ID = pl.DeviceIdType.MESH


def row_product(left_rows, right_rows):
    return lax.dot_general(
        left_rows, right_rows, (((0,), (0,)), ((), ())), preferred_element_type=jnp.float32
    )


def diag_solve(diag_factor, diag_inverse, diag_reduced):
    highest = lax.Precision.HIGH
    chol_proj = jnp.dot(diag_factor.T, diag_reduced, precision=highest)
    index_row = lax.broadcasted_iota(jnp.int32, chol_proj.shape, 0)
    index_col = lax.broadcasted_iota(jnp.int32, chol_proj.shape, 1)
    phi_lower = jnp.where(
        index_row > index_col,
        chol_proj,
        jnp.where(index_row == index_col, chol_proj - 0.5 * chol_proj, 0.0),
    )
    symmetric = 0.5 * (phi_lower + phi_lower.T)
    left_side = jnp.dot(diag_inverse.T, symmetric, precision=highest)
    return jnp.dot(left_side, diag_inverse, precision=highest)


def by_width(index, rows, width, action):
    group = (rows * (index + 1) - 1) // 128
    for j in range(width // 128):
        @pl.when(group == j)
        def _():
            action(128 * (j + 1))


def gather_kernel(n, line, n_gr, x_ref, p_ref, prior_ref, out_ref, cross_out, prior_out, precv, recv_piece,
                  cross_slots, prior_slots, psems, sems, local_sem):
    me = lax.axis_index("gc")
    row = lax.axis_index("gr")
    rows = x_ref.shape[2]
    lines = n // line
    pos = lax.rem(me, line)
    grp = me // line
    base = grp * line

    def line_peer(k):
        return base + lax.rem(pos + k, line)

    def cross_peer(k):
        return lax.rem(grp + k, lines) * line + pos

    part_rows, part_width = p_ref.shape[1], p_ref.shape[2]
    precv[...] = jnp.zeros(precv.shape, precv.dtype)
    recv_piece[...] = jnp.zeros(recv_piece.shape, recv_piece.dtype)
    cross_slots[...] = jnp.zeros(cross_slots.shape, cross_slots.dtype)
    barrier = pltpu.get_barrier_semaphore()

    def greet(k, carry):
        pl.semaphore_signal(barrier, inc=1, device_id=(row, lax.rem(me + k, n)), device_id_type=MESH_ID)
        return carry

    def greet_gr(k, carry):
        pl.semaphore_signal(barrier, inc=1, device_id=(lax.rem(row + k, n_gr), me), device_id_type=MESH_ID)
        return carry

    lax.fori_loop(1, n, greet, 0)
    lax.fori_loop(1, n_gr, greet_gr, 0)
    pl.semaphore_wait(barrier, n + n_gr - 2)

    def part_copy(k, sender, cols):
        peer = lax.rem(me + k, n)
        return pltpu.make_async_remote_copy(
            src_ref=p_ref.at[peer, :, pl.ds(0, cols)],
            dst_ref=precv.at[sender, :, pl.ds(0, cols)],
            send_sem=psems.at[0, k],
            recv_sem=psems.at[1, sender],
            device_id=(row, peer),
            device_id_type=MESH_ID,
        )

    def send_parts(k, carry):
        by_width(lax.rem(me + k, n), part_rows, part_width, lambda cols: part_copy(k, me, cols).start())
        return carry

    lax.fori_loop(1, n, send_parts, 0)

    own = pltpu.make_async_copy(x_ref, out_ref.at[:, :, pl.ds(me * rows, rows), :], local_sem)
    own.start()

    def first(k, sender_pos):
        return pltpu.make_async_remote_copy(
            src_ref=x_ref,
            dst_ref=out_ref.at[:, :, pl.ds((base + sender_pos) * rows, rows), :],
            send_sem=sems.at[0, k],
            recv_sem=sems.at[1, sender_pos],
            device_id=(row, line_peer(k)),
            device_id_type=MESH_ID,
        )

    def send_first(k, carry):
        first(k, pos).start()
        return carry

    lax.fori_loop(1, line, send_first, 0)


    span = line * rows

    def forward(k, block_pos, sender_grp):
        slot = pl.ds((grp * line + block_pos) * rows, rows)
        return pltpu.make_async_remote_copy(
            src_ref=out_ref.at[:, :, slot, :],
            dst_ref=out_ref.at[:, :, slot, :],
            send_sem=sems.at[2 + block_pos, k],
            recv_sem=sems.at[1, line + sender_grp],
            device_id=(row, cross_peer(k)),
            device_id_type=MESH_ID,
        )

    def whole_line(sender_grp):
        return pltpu.make_async_remote_copy(
            src_ref=out_ref.at[:, :, pl.ds(sender_grp * span, span), :],
            dst_ref=out_ref.at[:, :, pl.ds(sender_grp * span, span), :],
            send_sem=sems.at[0, 0],
            recv_sem=sems.at[1, line + sender_grp],
            device_id=(row, cross_peer(1)),
            device_id_type=MESH_ID,
        )

    own.wait()

    def send_own(k, carry):
        forward(k, pos, grp).start()
        return carry

    lax.fori_loop(1, lines, send_own, 0)


    precv[me] = p_ref[me]

    def wait_parts(k, carry):
        sender = lax.rem(me + n - k, n)
        by_width(lax.rem(me + k, n), part_rows, part_width, lambda cols: part_copy(k, me, cols).wait_send())
        by_width(me, part_rows, part_width, lambda cols: part_copy(k, sender, cols).wait_recv())
        return carry

    lax.fori_loop(1, n, wait_parts, 0)

    def add_part(j, total):
        return total + precv[j].astype(jnp.float32)

    piece = lax.fori_loop(0, n, add_part, jnp.zeros(recv_piece.shape[1:], jnp.float32))
    recv_piece[row] = piece

    def piece_copy(k, sender, cols):
        return pltpu.make_async_remote_copy(
            src_ref=recv_piece.at[row, :, pl.ds(0, cols)],
            dst_ref=recv_piece.at[sender, :, pl.ds(0, cols)],
            send_sem=psems.at[2, k],
            recv_sem=psems.at[3, sender],
            device_id=(lax.rem(row + k, n_gr), me),
            device_id_type=MESH_ID,
        )

    def send_piece(k, carry):
        by_width(me, part_rows, part_width, lambda cols: piece_copy(k, row, cols).start())
        return carry

    lax.fori_loop(1, n_gr, send_piece, 0)

    def relay(k, carry):
        sender_pos = lax.rem(pos + line - k, line)
        first(k, sender_pos).wait_recv()

        def out(j, inner):
            forward(j, sender_pos, grp).start()
            return inner

        return lax.fori_loop(1, lines, out, carry)

    lax.fori_loop(1, line, relay, 0)

    def wait_piece(k, carry):
        sender = lax.rem(row + n_gr - k, n_gr)
        by_width(me, part_rows, part_width, lambda cols: piece_copy(k, row, cols).wait_send())
        by_width(me, part_rows, part_width, lambda cols: piece_copy(k, sender, cols).wait_recv())
        return carry

    lax.fori_loop(1, n_gr, wait_piece, 0)

    def add_piece(j, total):
        return total + recv_piece[j]

    summed = lax.fori_loop(0, n_gr, add_piece, jnp.zeros(recv_piece.shape[1:], jnp.float32))
    cross_slots[me] = summed.astype(cross_slots.dtype)

    def cross_copy(k, sender, cols):
        return pltpu.make_async_remote_copy(
            src_ref=cross_slots.at[me, :, pl.ds(0, cols)],
            dst_ref=cross_slots.at[sender, :, pl.ds(0, cols)],
            send_sem=psems.at[4, k],
            recv_sem=psems.at[5, sender],
            device_id=(row, lax.rem(me + k, n)),
            device_id_type=MESH_ID,
        )

    def send_cross(k, carry):
        by_width(me, part_rows, part_width, lambda cols: cross_copy(k, me, cols).start())
        return carry

    lax.fori_loop(1, n, send_cross, 0)

    def prior_copy(k, sender):
        return pltpu.make_async_remote_copy(
            src_ref=prior_ref,
            dst_ref=prior_slots.at[sender],
            send_sem=psems.at[6, k],
            recv_sem=psems.at[7, sender],
            device_id=(lax.rem(row + k, n_gr), me),
            device_id_type=MESH_ID,
        )

    def send_prior(k, carry):
        prior_copy(k, row).start()
        return carry

    lax.fori_loop(1, n_gr, send_prior, 0)
    prior_slots[row] = prior_ref[...]

    def wait_first(k, carry):
        first(k, pos).wait_send()
        return carry

    lax.fori_loop(1, line, wait_first, 0)

    def wait_sent(k, carry):
        def done(j, inner):
            forward(j, k, grp).wait_send()
            return inner

        return lax.fori_loop(1, lines, done, carry)

    lax.fori_loop(0, line, wait_sent, 0)

    def wait_lines(k, carry):
        whole_line(lax.rem(grp + lines - k, lines)).wait_recv()
        return carry

    lax.fori_loop(1, lines, wait_lines, 0)

    def wait_cross(k, carry):
        sender = lax.rem(me + n - k, n)
        by_width(me, part_rows, part_width, lambda cols: cross_copy(k, me, cols).wait_send())
        by_width(sender, part_rows, part_width, lambda cols: cross_copy(k, sender, cols).wait_recv())
        return carry

    lax.fori_loop(1, n, wait_cross, 0)
    cross_out[...] = cross_slots[...]

    def wait_prior(k, carry):
        prior_copy(k, row).wait_send()
        prior_copy(k, lax.rem(row + n_gr - k, n_gr)).wait_recv()
        return carry

    lax.fori_loop(1, n_gr, wait_prior, 0)
    prior_out[...] = prior_slots[...]


def gather_gc(block, part, prior_rows, n, line, n_gr):
    tiles, count, rows, width = block.shape
    vmem = pl.BlockSpec(memory_space=pltpu.VMEM)
    return pl.pallas_call(
        functools.partial(gather_kernel, n, line, n_gr),
        out_shape=(
            jax.ShapeDtypeStruct((tiles, count, rows * n, width), block.dtype),
            jax.ShapeDtypeStruct(part.shape, jnp.bfloat16),
            jax.ShapeDtypeStruct((n_gr,) + prior_rows.shape, prior_rows.dtype),
        ),
        in_specs=[pl.BlockSpec(memory_space=pl.ANY), vmem, vmem],
        out_specs=(pl.BlockSpec(memory_space=pl.ANY), vmem, vmem),
        scratch_shapes=[
            pltpu.VMEM(part.shape, part.dtype),
            pltpu.VMEM((n_gr,) + part.shape[1:], jnp.float32),
            pltpu.VMEM(part.shape, jnp.bfloat16),
            pltpu.VMEM((n_gr,) + prior_rows.shape, prior_rows.dtype),
            pltpu.SemaphoreType.DMA((8, max(n, n_gr))),
            pltpu.SemaphoreType.DMA((2 + line, line + n // line)),
            pltpu.SemaphoreType.DMA,
        ],
        compiler_params=pltpu.CompilerParams(collective_id=0, has_side_effects=True),
    )(block, part, prior_rows)


def reduce_kernel(n, crossing_ref, crossing_out, recv_crossing, sems):
    me = lax.axis_index("gr")
    col = lax.axis_index("gc")
    rows = crossing_out.shape[0]

    barrier = pltpu.get_barrier_semaphore()

    def greet_gr(k, carry):
        pl.semaphore_signal(barrier, inc=1, device_id=(lax.rem(me + k, n), col), device_id_type=MESH_ID)
        return carry

    lax.fori_loop(1, n, greet_gr, 0)
    pl.semaphore_wait(barrier, n - 1)

    def gr_copy(k, sender, src, dst, index):
        return pltpu.make_async_remote_copy(
            src_ref=src,
            dst_ref=dst.at[sender],
            send_sem=sems.at[index, k],
            recv_sem=sems.at[index + 1, sender],
            device_id=(lax.rem(me + k, n), col),
            device_id_type=MESH_ID,
        )

    def crossing_copy(k, sender):
        peer = lax.rem(me + k, n)
        src = crossing_ref.at[pl.ds(pl.multiple_of(peer * rows, rows), rows), :]
        return gr_copy(k, sender, src, recv_crossing, 0)

    def send(k, carry):
        crossing_copy(k, me).start()
        return carry

    lax.fori_loop(1, n, send, 0)
    recv_crossing[me] = crossing_ref[pl.ds(pl.multiple_of(me * rows, rows), rows), :]

    def wait(k, carry):
        sender = lax.rem(me + n - k, n)
        crossing_copy(k, me).wait_send()
        crossing_copy(k, sender).wait_recv()
        return carry

    lax.fori_loop(1, n, wait, 0)

    def add_crossing(j, total):
        return total + recv_crossing[j].astype(jnp.float32)

    crossing_out[...] = lax.fori_loop(0, n, add_crossing, jnp.zeros(crossing_out.shape, jnp.float32))


def reduce_gr(crossing_part, n):
    rows = crossing_part.shape[0] // n
    cols = crossing_part.shape[1]
    vmem = pl.BlockSpec(memory_space=pltpu.VMEM)
    return pl.pallas_call(
        functools.partial(reduce_kernel, n),
        out_shape=jax.ShapeDtypeStruct((rows, cols), jnp.float32),
        in_specs=[vmem],
        out_specs=vmem,
        scratch_shapes=[
            pltpu.VMEM((n, rows, cols), crossing_part.dtype),
            pltpu.SemaphoreType.DMA((2, n)),
        ],
        compiler_params=pltpu.CompilerParams(collective_id=1, has_side_effects=True),
    )(crossing_part)


def prior_factor_rows(prior_rows, below_shape):
    return prior_rows.reshape(-1, below_shape[3], below_shape[5])


def local(
    n_gc,
    n_gr,
    line,
    below_factor,
    panel_factor,
    prior_factor,
    diag_factor,
    diag_inverse,
    below_adjoint,
    panel_adjoint,
    prior_adjoint,
    diag_adjoint,
):
    tile_count = below_factor.shape[0]
    tile_rows = below_factor.shape[2]
    local_rows = tile_count * tile_rows
    local_cols = below_factor.shape[3] * below_factor.shape[5]
    own_rows = panel_factor.shape[2]
    width = panel_factor.shape[3]
    prior_local = prior_factor.shape[0]
    below_mat = below_factor.reshape(local_rows, local_cols)
    below_bar = below_adjoint.reshape(local_rows, local_cols)
    inverse_bf = diag_inverse.astype(jnp.bfloat16)
    own_grad = lax.dot_general(
        panel_adjoint.reshape(tile_count, own_rows, width),
        inverse_bf,
        (((2,), (0,)), ((), ())),
        preferred_element_type=jnp.float32,
    ).astype(jnp.bfloat16)
    panel_grad = own_grad.reshape(panel_adjoint.shape)
    own_part = lax.dot_general(
        own_grad,
        panel_factor.reshape(tile_count, own_rows, width),
        (((0, 1), (0, 1)), ((), ())),
        preferred_element_type=jnp.float32,
    ).astype(jnp.bfloat16)
    prior_here = prior_factor.reshape(prior_local, local_cols)
    whole, cross_rows, prior_rows = gather_gc(
        panel_grad,
        own_part.reshape(n_gc, width // n_gc, width),
        prior_here,
        n_gc,
        line,
        n_gr,
    )
    grad_rows = whole.reshape(local_rows, width)
    crossing_part = row_product(grad_rows, below_mat).astype(jnp.bfloat16)
    crossing = reduce_gr(crossing_part, n_gr)
    summed = cross_rows.reshape(width, width).astype(jnp.float32)
    prior_whole = prior_rows.reshape(width, local_cols)
    diag_reduced = jnp.tril(diag_adjoint - summed)
    diag_gradient = diag_solve(diag_factor, diag_inverse, diag_reduced)
    below_prod = lax.dot_general(
        grad_rows.reshape(tile_count, tile_rows, width),
        prior_factor_rows(prior_rows, below_factor.shape),
        (((2,), (0,)), ((), ())),
        preferred_element_type=jnp.float32,
    ).reshape(below_adjoint.shape)
    below_new = (below_adjoint.astype(jnp.float32) - below_prod).astype(jnp.bfloat16)
    grid_row = lax.axis_index("gr")
    twice_rows = lax.dynamic_slice_in_dim(
        2.0 * diag_gradient, grid_row * prior_local, prior_local, 0
    ).astype(jnp.bfloat16)
    curvature = jnp.dot(twice_rows, prior_whole, preferred_element_type=jnp.float32)
    prior_bar = prior_adjoint.reshape(prior_local, local_cols).astype(jnp.float32)
    prior_new = (prior_bar - crossing - curvature).astype(jnp.bfloat16)
    return (
        below_new,
        panel_grad,
        prior_new.reshape(prior_adjoint.shape),
        diag_gradient,
    )


def line_length(mesh):
    column = list(mesh.devices[0])
    coords = [getattr(d, "coords", None) for d in column]
    if any(c is None for c in coords):
        return 8 if len(column) % 8 == 0 else len(column)
    first = coords[0][0]
    count = 0
    for c in coords:
        if c[0] != first:
            break
        count += 1
    return count if len(column) % count == 0 else len(column)


def solution(mesh):
    in_specs = (
        P(None, "gr", None, None, "gc", None),
        P(None, "gr", "gc", None),
        P("gr", None, "gc", None),
        P(),
        P(),
        P(None, "gr", None, None, "gc", None),
        P(None, "gr", "gc", None),
        P("gr", None, "gc", None),
        P(),
    )
    out_specs = (
        P(None, "gr", None, None, "gc", None),
        P(None, "gr", "gc", None),
        P("gr", None, "gc", None),
        P(),
    )
    return jax.shard_map(
        functools.partial(local, mesh.shape["gc"], mesh.shape["gr"], line_length(mesh)),
        mesh=mesh,
        in_specs=in_specs,
        out_specs=out_specs,
        check_vma=False,
    )
```

```python
import functools

import jax
import jax.numpy as jnp
from jax import lax
from jax.experimental import pallas as pl
from jax.experimental.pallas import tpu as pltpu
from jax.sharding import PartitionSpec as P

MESH_ID = pl.DeviceIdType.MESH


def row_product(left_rows, right_rows):
    return lax.dot_general(
        left_rows, right_rows, (((0,), (0,)), ((), ())), preferred_element_type=jnp.float32
    )


def diag_solve(diag_factor, diag_inverse, diag_reduced):
    highest = lax.Precision.HIGH
    chol_proj = jnp.dot(diag_factor.T, diag_reduced, precision=highest)
    index_row = lax.broadcasted_iota(jnp.int32, chol_proj.shape, 0)
    index_col = lax.broadcasted_iota(jnp.int32, chol_proj.shape, 1)
    phi_lower = jnp.where(
        index_row > index_col,
        chol_proj,
        jnp.where(index_row == index_col, chol_proj - 0.5 * chol_proj, 0.0),
    )
    symmetric = 0.5 * (phi_lower + phi_lower.T)
    left_side = jnp.dot(diag_inverse.T, symmetric, precision=highest)
    return jnp.dot(left_side, diag_inverse, precision=highest)


def by_width(index, rows, width, action):
    group = (rows * (index + 1) - 1) // 128
    for j in range(width // 128):
        @pl.when(group == j)
        def _():
            action(128 * (j + 1))


def gather_kernel(n, line, n_gr, x_ref, p_ref, prior_ref, out_ref, cross_out, prior_out, precv, recv_piece,
                  cross_slots, psems, sems, local_sem):
    me = lax.axis_index("gc")
    row = lax.axis_index("gr")
    rows = x_ref.shape[2]
    lines = n // line
    pos = lax.rem(me, line)
    grp = me // line
    base = grp * line

    def line_peer(k):
        return base + lax.rem(pos + k, line)

    def cross_peer(k):
        return lax.rem(grp + k, lines) * line + pos

    part_rows, part_width = p_ref.shape[1], p_ref.shape[2]
    precv[...] = jnp.zeros(precv.shape, precv.dtype)
    recv_piece[...] = jnp.zeros(recv_piece.shape, recv_piece.dtype)
    cross_slots[...] = jnp.zeros(cross_slots.shape, cross_slots.dtype)
    barrier = pltpu.get_barrier_semaphore()

    def greet(k, carry):
        pl.semaphore_signal(barrier, inc=1, device_id=(row, lax.rem(me + k, n)), device_id_type=MESH_ID)
        return carry

    def greet_gr(k, carry):
        pl.semaphore_signal(barrier, inc=1, device_id=(lax.rem(row + k, n_gr), me), device_id_type=MESH_ID)
        return carry

    lax.fori_loop(1, n, greet, 0)
    lax.fori_loop(1, n_gr, greet_gr, 0)
    pl.semaphore_wait(barrier, n + n_gr - 2)

    def part_copy(k, sender, cols):
        peer = lax.rem(me + k, n)
        return pltpu.make_async_remote_copy(
            src_ref=p_ref.at[peer, :, pl.ds(0, cols)],
            dst_ref=precv.at[sender, :, pl.ds(0, cols)],
            send_sem=psems.at[0, k],
            recv_sem=psems.at[1, sender],
            device_id=(row, peer),
            device_id_type=MESH_ID,
        )

    def send_parts(k, carry):
        by_width(lax.rem(me + k, n), part_rows, part_width, lambda cols: part_copy(k, me, cols).start())
        return carry

    lax.fori_loop(1, n, send_parts, 0)

    own = pltpu.make_async_copy(x_ref, out_ref.at[:, :, pl.ds(me * rows, rows), :], local_sem)
    own.start()

    def first(k, sender_pos):
        return pltpu.make_async_remote_copy(
            src_ref=x_ref,
            dst_ref=out_ref.at[:, :, pl.ds((base + sender_pos) * rows, rows), :],
            send_sem=sems.at[0, k],
            recv_sem=sems.at[1, sender_pos],
            device_id=(row, line_peer(k)),
            device_id_type=MESH_ID,
        )

    def send_first(k, carry):
        first(k, pos).start()
        return carry

    lax.fori_loop(1, line, send_first, 0)


    span = line * rows

    def forward(k, block_pos, sender_grp):
        slot = pl.ds((grp * line + block_pos) * rows, rows)
        return pltpu.make_async_remote_copy(
            src_ref=out_ref.at[:, :, slot, :],
            dst_ref=out_ref.at[:, :, slot, :],
            send_sem=sems.at[2 + block_pos, k],
            recv_sem=sems.at[1, line + sender_grp],
            device_id=(row, cross_peer(k)),
            device_id_type=MESH_ID,
        )

    def whole_line(sender_grp):
        return pltpu.make_async_remote_copy(
            src_ref=out_ref.at[:, :, pl.ds(sender_grp * span, span), :],
            dst_ref=out_ref.at[:, :, pl.ds(sender_grp * span, span), :],
            send_sem=sems.at[0, 0],
            recv_sem=sems.at[1, line + sender_grp],
            device_id=(row, cross_peer(1)),
            device_id_type=MESH_ID,
        )

    own.wait()

    def send_own(k, carry):
        forward(k, pos, grp).start()
        return carry

    lax.fori_loop(1, lines, send_own, 0)


    precv[me] = p_ref[me]

    def wait_parts(k, carry):
        sender = lax.rem(me + n - k, n)
        by_width(lax.rem(me + k, n), part_rows, part_width, lambda cols: part_copy(k, me, cols).wait_send())
        by_width(me, part_rows, part_width, lambda cols: part_copy(k, sender, cols).wait_recv())
        return carry

    lax.fori_loop(1, n, wait_parts, 0)

    def add_part(j, total):
        return total + precv[j].astype(jnp.float32)

    piece = lax.fori_loop(0, n, add_part, jnp.zeros(recv_piece.shape[1:], jnp.float32))
    recv_piece[row] = piece

    def piece_copy(k, sender, cols):
        return pltpu.make_async_remote_copy(
            src_ref=recv_piece.at[row, :, pl.ds(0, cols)],
            dst_ref=recv_piece.at[sender, :, pl.ds(0, cols)],
            send_sem=psems.at[2, k],
            recv_sem=psems.at[3, sender],
            device_id=(lax.rem(row + k, n_gr), me),
            device_id_type=MESH_ID,
        )

    def send_piece(k, carry):
        by_width(me, part_rows, part_width, lambda cols: piece_copy(k, row, cols).start())
        return carry

    lax.fori_loop(1, n_gr, send_piece, 0)

    def relay(k, carry):
        sender_pos = lax.rem(pos + line - k, line)
        first(k, sender_pos).wait_recv()

        def out(j, inner):
            forward(j, sender_pos, grp).start()
            return inner

        return lax.fori_loop(1, lines, out, carry)

    lax.fori_loop(1, line, relay, 0)

    def wait_piece(k, carry):
        sender = lax.rem(row + n_gr - k, n_gr)
        by_width(me, part_rows, part_width, lambda cols: piece_copy(k, row, cols).wait_send())
        by_width(me, part_rows, part_width, lambda cols: piece_copy(k, sender, cols).wait_recv())
        return carry

    lax.fori_loop(1, n_gr, wait_piece, 0)

    def add_piece(j, total):
        return total + recv_piece[j]

    summed = lax.fori_loop(0, n_gr, add_piece, jnp.zeros(recv_piece.shape[1:], jnp.float32))
    cross_slots[me] = summed.astype(cross_slots.dtype)

    def cross_copy(k, sender, cols):
        return pltpu.make_async_remote_copy(
            src_ref=cross_slots.at[me, :, pl.ds(0, cols)],
            dst_ref=cross_slots.at[sender, :, pl.ds(0, cols)],
            send_sem=psems.at[4, k],
            recv_sem=psems.at[5, sender],
            device_id=(row, lax.rem(me + k, n)),
            device_id_type=MESH_ID,
        )

    def send_cross(k, carry):
        by_width(me, part_rows, part_width, lambda cols: cross_copy(k, me, cols).start())
        return carry

    lax.fori_loop(1, n, send_cross, 0)

    def prior_copy(k, sender):
        return pltpu.make_async_remote_copy(
            src_ref=prior_ref,
            dst_ref=prior_out.at[sender],
            send_sem=psems.at[6, k],
            recv_sem=psems.at[7, sender],
            device_id=(lax.rem(row + k, n_gr), me),
            device_id_type=MESH_ID,
        )

    def send_prior(k, carry):
        prior_copy(k, row).start()
        return carry

    lax.fori_loop(1, n_gr, send_prior, 0)
    own_prior = pltpu.make_async_copy(prior_ref, prior_out.at[row], psems.at[6, 0])
    own_prior.start()

    def wait_first(k, carry):
        first(k, pos).wait_send()
        return carry

    lax.fori_loop(1, line, wait_first, 0)

    def wait_sent(k, carry):
        def done(j, inner):
            forward(j, k, grp).wait_send()
            return inner

        return lax.fori_loop(1, lines, done, carry)

    lax.fori_loop(0, line, wait_sent, 0)

    def wait_lines(k, carry):
        whole_line(lax.rem(grp + lines - k, lines)).wait_recv()
        return carry

    lax.fori_loop(1, lines, wait_lines, 0)

    def wait_cross(k, carry):
        sender = lax.rem(me + n - k, n)
        by_width(me, part_rows, part_width, lambda cols: cross_copy(k, me, cols).wait_send())
        by_width(sender, part_rows, part_width, lambda cols: cross_copy(k, sender, cols).wait_recv())
        return carry

    lax.fori_loop(1, n, wait_cross, 0)
    cross_out[...] = cross_slots[...]

    def wait_prior(k, carry):
        prior_copy(k, row).wait_send()
        prior_copy(k, lax.rem(row + n_gr - k, n_gr)).wait_recv()
        return carry

    lax.fori_loop(1, n_gr, wait_prior, 0)
    own_prior.wait()


def gather_gc(block, part, prior_rows, n, line, n_gr):
    tiles, count, rows, width = block.shape
    vmem = pl.BlockSpec(memory_space=pltpu.VMEM)
    return pl.pallas_call(
        functools.partial(gather_kernel, n, line, n_gr),
        out_shape=(
            jax.ShapeDtypeStruct((tiles, count, rows * n, width), block.dtype),
            jax.ShapeDtypeStruct(part.shape, jnp.bfloat16),
            jax.ShapeDtypeStruct((n_gr,) + prior_rows.shape, prior_rows.dtype),
        ),
        in_specs=[pl.BlockSpec(memory_space=pl.ANY), vmem, pl.BlockSpec(memory_space=pl.ANY)],
        out_specs=(pl.BlockSpec(memory_space=pl.ANY), vmem, pl.BlockSpec(memory_space=pl.ANY)),
        scratch_shapes=[
            pltpu.VMEM(part.shape, part.dtype),
            pltpu.VMEM((n_gr,) + part.shape[1:], jnp.float32),
            pltpu.VMEM(part.shape, jnp.bfloat16),
            pltpu.SemaphoreType.DMA((8, max(n, n_gr))),
            pltpu.SemaphoreType.DMA((2 + line, line + n // line)),
            pltpu.SemaphoreType.DMA,
        ],
        compiler_params=pltpu.CompilerParams(collective_id=0, has_side_effects=True),
    )(block, part, prior_rows)


def reduce_kernel(n, crossing_ref, crossing_out, recv_crossing, sems):
    me = lax.axis_index("gr")
    col = lax.axis_index("gc")
    rows = crossing_out.shape[0]

    barrier = pltpu.get_barrier_semaphore()

    def greet_gr(k, carry):
        pl.semaphore_signal(barrier, inc=1, device_id=(lax.rem(me + k, n), col), device_id_type=MESH_ID)
        return carry

    lax.fori_loop(1, n, greet_gr, 0)
    pl.semaphore_wait(barrier, n - 1)

    def gr_copy(k, sender, src, dst, index):
        return pltpu.make_async_remote_copy(
            src_ref=src,
            dst_ref=dst.at[sender],
            send_sem=sems.at[index, k],
            recv_sem=sems.at[index + 1, sender],
            device_id=(lax.rem(me + k, n), col),
            device_id_type=MESH_ID,
        )

    def crossing_copy(k, sender):
        peer = lax.rem(me + k, n)
        src = crossing_ref.at[pl.ds(pl.multiple_of(peer * rows, rows), rows), :]
        return gr_copy(k, sender, src, recv_crossing, 0)

    def send(k, carry):
        crossing_copy(k, me).start()
        return carry

    lax.fori_loop(1, n, send, 0)
    recv_crossing[me] = crossing_ref[pl.ds(pl.multiple_of(me * rows, rows), rows), :]

    def wait(k, carry):
        sender = lax.rem(me + n - k, n)
        crossing_copy(k, me).wait_send()
        crossing_copy(k, sender).wait_recv()
        return carry

    lax.fori_loop(1, n, wait, 0)

    def add_crossing(j, total):
        return total + recv_crossing[j].astype(jnp.float32)

    crossing_out[...] = lax.fori_loop(0, n, add_crossing, jnp.zeros(crossing_out.shape, jnp.float32))


def reduce_gr(crossing_part, n):
    rows = crossing_part.shape[0] // n
    cols = crossing_part.shape[1]
    vmem = pl.BlockSpec(memory_space=pltpu.VMEM)
    return pl.pallas_call(
        functools.partial(reduce_kernel, n),
        out_shape=jax.ShapeDtypeStruct((rows, cols), jnp.float32),
        in_specs=[vmem],
        out_specs=vmem,
        scratch_shapes=[
            pltpu.VMEM((n, rows, cols), crossing_part.dtype),
            pltpu.SemaphoreType.DMA((2, n)),
        ],
        compiler_params=pltpu.CompilerParams(collective_id=1, has_side_effects=True),
    )(crossing_part)


def prior_factor_rows(prior_rows, below_shape):
    return prior_rows.reshape(-1, below_shape[3], below_shape[5])


def local(
    n_gc,
    n_gr,
    line,
    below_factor,
    panel_factor,
    prior_factor,
    diag_factor,
    diag_inverse,
    below_adjoint,
    panel_adjoint,
    prior_adjoint,
    diag_adjoint,
):
    tile_count = below_factor.shape[0]
    tile_rows = below_factor.shape[2]
    local_rows = tile_count * tile_rows
    local_cols = below_factor.shape[3] * below_factor.shape[5]
    own_rows = panel_factor.shape[2]
    width = panel_factor.shape[3]
    prior_local = prior_factor.shape[0]
    below_mat = below_factor.reshape(local_rows, local_cols)
    below_bar = below_adjoint.reshape(local_rows, local_cols)
    inverse_bf = diag_inverse.astype(jnp.bfloat16)
    own_grad = lax.dot_general(
        panel_adjoint.reshape(tile_count, own_rows, width),
        inverse_bf,
        (((2,), (0,)), ((), ())),
        preferred_element_type=jnp.float32,
    ).astype(jnp.bfloat16)
    panel_grad = own_grad.reshape(panel_adjoint.shape)
    own_part = lax.dot_general(
        own_grad,
        panel_factor.reshape(tile_count, own_rows, width),
        (((0, 1), (0, 1)), ((), ())),
        preferred_element_type=jnp.float32,
    ).astype(jnp.bfloat16)
    prior_here = prior_factor.reshape(prior_local, below_factor.shape[3], below_factor.shape[5])
    whole, cross_rows, prior_rows = gather_gc(
        panel_grad,
        own_part.reshape(n_gc, width // n_gc, width),
        prior_here,
        n_gc,
        line,
        n_gr,
    )
    grad_rows = whole.reshape(local_rows, width)
    crossing_part = row_product(grad_rows, below_mat).astype(jnp.bfloat16)
    crossing = reduce_gr(crossing_part, n_gr)
    summed = cross_rows.reshape(width, width).astype(jnp.float32)
    prior_whole = prior_rows.reshape(width, local_cols)
    diag_reduced = jnp.tril(diag_adjoint - summed)
    diag_gradient = diag_solve(diag_factor, diag_inverse, diag_reduced)
    below_prod = lax.dot_general(
        grad_rows.reshape(tile_count, tile_rows, width),
        prior_factor_rows(prior_rows, below_factor.shape),
        (((2,), (0,)), ((), ())),
        preferred_element_type=jnp.float32,
    ).reshape(below_adjoint.shape)
    below_new = (below_adjoint.astype(jnp.float32) - below_prod).astype(jnp.bfloat16)
    grid_row = lax.axis_index("gr")
    twice_rows = lax.dynamic_slice_in_dim(
        2.0 * diag_gradient, grid_row * prior_local, prior_local, 0
    ).astype(jnp.bfloat16)
    curvature = jnp.dot(twice_rows, prior_whole, preferred_element_type=jnp.float32)
    prior_bar = prior_adjoint.reshape(prior_local, local_cols).astype(jnp.float32)
    prior_new = (prior_bar - crossing - curvature).astype(jnp.bfloat16)
    return (
        below_new,
        panel_grad,
        prior_new.reshape(prior_adjoint.shape),
        diag_gradient,
    )


def line_length(mesh):
    column = list(mesh.devices[0])
    coords = [getattr(d, "coords", None) for d in column]
    if any(c is None for c in coords):
        return 8 if len(column) % 8 == 0 else len(column)
    first = coords[0][0]
    count = 0
    for c in coords:
        if c[0] != first:
            break
        count += 1
    return count if len(column) % count == 0 else len(column)


def solution(mesh):
    in_specs = (
        P(None, "gr", None, None, "gc", None),
        P(None, "gr", "gc", None),
        P("gr", None, "gc", None),
        P(),
        P(),
        P(None, "gr", None, None, "gc", None),
        P(None, "gr", "gc", None),
        P("gr", None, "gc", None),
        P(),
    )
    out_specs = (
        P(None, "gr", None, None, "gc", None),
        P(None, "gr", "gc", None),
        P("gr", None, "gc", None),
        P(),
    )
    return jax.shard_map(
        functools.partial(local, mesh.shape["gc"], mesh.shape["gr"], line_length(mesh)),
        mesh=mesh,
        in_specs=in_specs,
        out_specs=out_specs,
        check_vma=False,
    )
```

```python
import functools

import jax
import jax.numpy as jnp
from jax import lax
from jax.experimental import pallas as pl
from jax.experimental.pallas import tpu as pltpu
from jax.sharding import PartitionSpec as P

MESH_ID = pl.DeviceIdType.MESH


def row_product(left_rows, right_rows):
    return lax.dot_general(
        left_rows, right_rows, (((0,), (0,)), ((), ())), preferred_element_type=jnp.float32
    )


def diag_solve(diag_factor, diag_inverse, diag_reduced):
    highest = lax.Precision.HIGH
    chol_proj = jnp.dot(diag_factor.T, diag_reduced, precision=highest)
    index_row = lax.broadcasted_iota(jnp.int32, chol_proj.shape, 0)
    index_col = lax.broadcasted_iota(jnp.int32, chol_proj.shape, 1)
    phi_lower = jnp.where(
        index_row > index_col,
        chol_proj,
        jnp.where(index_row == index_col, chol_proj - 0.5 * chol_proj, 0.0),
    )
    symmetric = 0.5 * (phi_lower + phi_lower.T)
    left_side = jnp.dot(diag_inverse.T, symmetric, precision=highest)
    return jnp.dot(left_side, diag_inverse, precision=highest)


def by_width(index, rows, width, action):
    group = (rows * (index + 1) - 1) // 128
    for j in range(width // 128):
        @pl.when(group == j)
        def _():
            action(128 * (j + 1))


def gather_kernel(n, line, n_gr, x_ref, p_ref, prior_ref, out_ref, cross_out, prior_out, precv, recv_piece,
                  cross_slots, psems, sems, local_sem):
    me = lax.axis_index("gc")
    row = lax.axis_index("gr")
    rows = x_ref.shape[2]
    lines = n // line
    pos = lax.rem(me, line)
    grp = me // line
    base = grp * line

    def line_peer(k):
        return base + lax.rem(pos + k, line)

    def cross_peer(k):
        return lax.rem(grp + k, lines) * line + pos

    part_rows, part_width = p_ref.shape[1], p_ref.shape[2]
    kept = lax.broadcasted_iota(jnp.int32, p_ref.shape[1:], 1) < 128 * ((p_ref.shape[1] * (me + 1) - 1) // 128 + 1)
    barrier = pltpu.get_barrier_semaphore()

    def greet(k, carry):
        pl.semaphore_signal(barrier, inc=1, device_id=(row, lax.rem(me + k, n)), device_id_type=MESH_ID)
        return carry

    def greet_gr(k, carry):
        pl.semaphore_signal(barrier, inc=1, device_id=(lax.rem(row + k, n_gr), me), device_id_type=MESH_ID)
        return carry

    lax.fori_loop(1, n, greet, 0)
    lax.fori_loop(1, n_gr, greet_gr, 0)
    pl.semaphore_wait(barrier, n + n_gr - 2)

    def part_copy(k, sender, cols):
        peer = lax.rem(me + k, n)
        return pltpu.make_async_remote_copy(
            src_ref=p_ref.at[peer, :, pl.ds(0, cols)],
            dst_ref=precv.at[sender, :, pl.ds(0, cols)],
            send_sem=psems.at[0, k],
            recv_sem=psems.at[1, sender],
            device_id=(row, peer),
            device_id_type=MESH_ID,
        )

    def send_parts(k, carry):
        by_width(lax.rem(me + k, n), part_rows, part_width, lambda cols: part_copy(k, me, cols).start())
        return carry

    lax.fori_loop(1, n, send_parts, 0)

    own = pltpu.make_async_copy(x_ref, out_ref.at[:, :, pl.ds(me * rows, rows), :], local_sem)
    own.start()

    def first(k, sender_pos):
        return pltpu.make_async_remote_copy(
            src_ref=x_ref,
            dst_ref=out_ref.at[:, :, pl.ds((base + sender_pos) * rows, rows), :],
            send_sem=sems.at[0, k],
            recv_sem=sems.at[1, sender_pos],
            device_id=(row, line_peer(k)),
            device_id_type=MESH_ID,
        )

    def send_first(k, carry):
        first(k, pos).start()
        return carry

    lax.fori_loop(1, line, send_first, 0)


    span = line * rows

    def forward(k, block_pos, sender_grp):
        slot = pl.ds((grp * line + block_pos) * rows, rows)
        return pltpu.make_async_remote_copy(
            src_ref=out_ref.at[:, :, slot, :],
            dst_ref=out_ref.at[:, :, slot, :],
            send_sem=sems.at[2 + block_pos, k],
            recv_sem=sems.at[1, line + sender_grp],
            device_id=(row, cross_peer(k)),
            device_id_type=MESH_ID,
        )

    def whole_line(sender_grp):
        return pltpu.make_async_remote_copy(
            src_ref=out_ref.at[:, :, pl.ds(sender_grp * span, span), :],
            dst_ref=out_ref.at[:, :, pl.ds(sender_grp * span, span), :],
            send_sem=sems.at[0, 0],
            recv_sem=sems.at[1, line + sender_grp],
            device_id=(row, cross_peer(1)),
            device_id_type=MESH_ID,
        )

    own.wait()

    def send_own(k, carry):
        forward(k, pos, grp).start()
        return carry

    lax.fori_loop(1, lines, send_own, 0)


    precv[me] = p_ref[me]

    def wait_parts(k, carry):
        sender = lax.rem(me + n - k, n)
        by_width(lax.rem(me + k, n), part_rows, part_width, lambda cols: part_copy(k, me, cols).wait_send())
        by_width(me, part_rows, part_width, lambda cols: part_copy(k, sender, cols).wait_recv())
        return carry

    lax.fori_loop(1, n, wait_parts, 0)

    def add_part(j, total):
        return total + precv[j].astype(jnp.float32)

    piece = lax.fori_loop(0, n, add_part, jnp.zeros(recv_piece.shape[1:], jnp.float32))
    recv_piece[row] = jnp.where(kept, piece, 0.0)

    def piece_copy(k, sender, cols):
        return pltpu.make_async_remote_copy(
            src_ref=recv_piece.at[row, :, pl.ds(0, cols)],
            dst_ref=recv_piece.at[sender, :, pl.ds(0, cols)],
            send_sem=psems.at[2, k],
            recv_sem=psems.at[3, sender],
            device_id=(lax.rem(row + k, n_gr), me),
            device_id_type=MESH_ID,
        )

    def send_piece(k, carry):
        by_width(me, part_rows, part_width, lambda cols: piece_copy(k, row, cols).start())
        return carry

    lax.fori_loop(1, n_gr, send_piece, 0)

    def relay(k, carry):
        sender_pos = lax.rem(pos + line - k, line)
        first(k, sender_pos).wait_recv()

        def out(j, inner):
            forward(j, sender_pos, grp).start()
            return inner

        return lax.fori_loop(1, lines, out, carry)

    lax.fori_loop(1, line, relay, 0)

    def wait_piece(k, carry):
        sender = lax.rem(row + n_gr - k, n_gr)
        by_width(me, part_rows, part_width, lambda cols: piece_copy(k, row, cols).wait_send())
        by_width(me, part_rows, part_width, lambda cols: piece_copy(k, sender, cols).wait_recv())
        return carry

    lax.fori_loop(1, n_gr, wait_piece, 0)

    def add_piece(j, total):
        return total + recv_piece[j]

    summed = lax.fori_loop(0, n_gr, add_piece, jnp.zeros(recv_piece.shape[1:], jnp.float32))
    cross_slots[me] = jnp.where(kept, summed, 0.0).astype(cross_slots.dtype)

    def cross_copy(k, sender, cols):
        return pltpu.make_async_remote_copy(
            src_ref=cross_slots.at[me, :, pl.ds(0, cols)],
            dst_ref=cross_slots.at[sender, :, pl.ds(0, cols)],
            send_sem=psems.at[4, k],
            recv_sem=psems.at[5, sender],
            device_id=(row, lax.rem(me + k, n)),
            device_id_type=MESH_ID,
        )

    def send_cross(k, carry):
        by_width(me, part_rows, part_width, lambda cols: cross_copy(k, me, cols).start())
        return carry

    lax.fori_loop(1, n, send_cross, 0)

    def prior_copy(k, sender):
        return pltpu.make_async_remote_copy(
            src_ref=prior_ref,
            dst_ref=prior_out.at[sender],
            send_sem=psems.at[6, k],
            recv_sem=psems.at[7, sender],
            device_id=(lax.rem(row + k, n_gr), me),
            device_id_type=MESH_ID,
        )

    def send_prior(k, carry):
        prior_copy(k, row).start()
        return carry

    lax.fori_loop(1, n_gr, send_prior, 0)
    own_prior = pltpu.make_async_copy(prior_ref, prior_out.at[row], psems.at[6, 0])
    own_prior.start()

    def wait_first(k, carry):
        first(k, pos).wait_send()
        return carry

    lax.fori_loop(1, line, wait_first, 0)

    def wait_sent(k, carry):
        def done(j, inner):
            forward(j, k, grp).wait_send()
            return inner

        return lax.fori_loop(1, lines, done, carry)

    lax.fori_loop(0, line, wait_sent, 0)

    def wait_lines(k, carry):
        whole_line(lax.rem(grp + lines - k, lines)).wait_recv()
        return carry

    lax.fori_loop(1, lines, wait_lines, 0)

    def wait_cross(k, carry):
        sender = lax.rem(me + n - k, n)
        by_width(me, part_rows, part_width, lambda cols: cross_copy(k, me, cols).wait_send())
        by_width(sender, part_rows, part_width, lambda cols: cross_copy(k, sender, cols).wait_recv())
        return carry

    lax.fori_loop(1, n, wait_cross, 0)
    cross_out[...] = cross_slots[...]

    def wait_prior(k, carry):
        prior_copy(k, row).wait_send()
        prior_copy(k, lax.rem(row + n_gr - k, n_gr)).wait_recv()
        return carry

    lax.fori_loop(1, n_gr, wait_prior, 0)
    own_prior.wait()


def gather_gc(block, part, prior_rows, n, line, n_gr):
    tiles, count, rows, width = block.shape
    vmem = pl.BlockSpec(memory_space=pltpu.VMEM)
    return pl.pallas_call(
        functools.partial(gather_kernel, n, line, n_gr),
        out_shape=(
            jax.ShapeDtypeStruct((tiles, count, rows * n, width), block.dtype),
            jax.ShapeDtypeStruct(part.shape, jnp.bfloat16),
            jax.ShapeDtypeStruct((n_gr,) + prior_rows.shape, prior_rows.dtype),
        ),
        in_specs=[pl.BlockSpec(memory_space=pl.ANY), vmem, pl.BlockSpec(memory_space=pl.ANY)],
        out_specs=(pl.BlockSpec(memory_space=pl.ANY), vmem, pl.BlockSpec(memory_space=pl.ANY)),
        scratch_shapes=[
            pltpu.VMEM(part.shape, part.dtype),
            pltpu.VMEM((n_gr,) + part.shape[1:], jnp.float32),
            pltpu.VMEM(part.shape, jnp.bfloat16),
            pltpu.SemaphoreType.DMA((8, max(n, n_gr))),
            pltpu.SemaphoreType.DMA((2 + line, line + n // line)),
            pltpu.SemaphoreType.DMA,
        ],
        compiler_params=pltpu.CompilerParams(collective_id=0, has_side_effects=True),
    )(block, part, prior_rows)


def reduce_kernel(n, crossing_ref, crossing_out, recv_crossing, sems):
    me = lax.axis_index("gr")
    col = lax.axis_index("gc")
    rows = crossing_out.shape[0]

    barrier = pltpu.get_barrier_semaphore()

    def greet_gr(k, carry):
        pl.semaphore_signal(barrier, inc=1, device_id=(lax.rem(me + k, n), col), device_id_type=MESH_ID)
        return carry

    lax.fori_loop(1, n, greet_gr, 0)
    pl.semaphore_wait(barrier, n - 1)

    def gr_copy(k, sender, src, dst, index):
        return pltpu.make_async_remote_copy(
            src_ref=src,
            dst_ref=dst.at[sender],
            send_sem=sems.at[index, k],
            recv_sem=sems.at[index + 1, sender],
            device_id=(lax.rem(me + k, n), col),
            device_id_type=MESH_ID,
        )

    def crossing_copy(k, sender):
        peer = lax.rem(me + k, n)
        src = crossing_ref.at[pl.ds(pl.multiple_of(peer * rows, rows), rows), :]
        return gr_copy(k, sender, src, recv_crossing, 0)

    def send(k, carry):
        crossing_copy(k, me).start()
        return carry

    lax.fori_loop(1, n, send, 0)
    recv_crossing[me] = crossing_ref[pl.ds(pl.multiple_of(me * rows, rows), rows), :]

    def wait(k, carry):
        sender = lax.rem(me + n - k, n)
        crossing_copy(k, me).wait_send()
        crossing_copy(k, sender).wait_recv()
        return carry

    lax.fori_loop(1, n, wait, 0)

    def add_crossing(j, total):
        return total + recv_crossing[j].astype(jnp.float32)

    crossing_out[...] = lax.fori_loop(0, n, add_crossing, jnp.zeros(crossing_out.shape, jnp.float32))


def reduce_gr(crossing_part, n):
    rows = crossing_part.shape[0] // n
    cols = crossing_part.shape[1]
    vmem = pl.BlockSpec(memory_space=pltpu.VMEM)
    return pl.pallas_call(
        functools.partial(reduce_kernel, n),
        out_shape=jax.ShapeDtypeStruct((rows, cols), jnp.float32),
        in_specs=[vmem],
        out_specs=vmem,
        scratch_shapes=[
            pltpu.VMEM((n, rows, cols), crossing_part.dtype),
            pltpu.SemaphoreType.DMA((2, n)),
        ],
        compiler_params=pltpu.CompilerParams(collective_id=1, has_side_effects=True),
    )(crossing_part)


def prior_factor_rows(prior_rows, below_shape):
    return prior_rows.reshape(-1, below_shape[3], below_shape[5])


def local(
    n_gc,
    n_gr,
    line,
    below_factor,
    panel_factor,
    prior_factor,
    diag_factor,
    diag_inverse,
    below_adjoint,
    panel_adjoint,
    prior_adjoint,
    diag_adjoint,
):
    tile_count = below_factor.shape[0]
    tile_rows = below_factor.shape[2]
    local_rows = tile_count * tile_rows
    local_cols = below_factor.shape[3] * below_factor.shape[5]
    own_rows = panel_factor.shape[2]
    width = panel_factor.shape[3]
    prior_local = prior_factor.shape[0]
    below_mat = below_factor.reshape(local_rows, local_cols)
    below_bar = below_adjoint.reshape(local_rows, local_cols)
    inverse_bf = diag_inverse.astype(jnp.bfloat16)
    own_grad = lax.dot_general(
        panel_adjoint.reshape(tile_count, own_rows, width),
        inverse_bf,
        (((2,), (0,)), ((), ())),
        preferred_element_type=jnp.float32,
    ).astype(jnp.bfloat16)
    panel_grad = own_grad.reshape(panel_adjoint.shape)
    own_part = lax.dot_general(
        own_grad,
        panel_factor.reshape(tile_count, own_rows, width),
        (((0, 1), (0, 1)), ((), ())),
        preferred_element_type=jnp.float32,
    ).astype(jnp.bfloat16)
    prior_here = prior_factor.reshape(prior_local, below_factor.shape[3], below_factor.shape[5])
    whole, cross_rows, prior_rows = gather_gc(
        panel_grad,
        own_part.reshape(n_gc, width // n_gc, width),
        prior_here,
        n_gc,
        line,
        n_gr,
    )
    grad_rows = whole.reshape(local_rows, width)
    crossing_part = row_product(grad_rows, below_mat).astype(jnp.bfloat16)
    crossing = reduce_gr(crossing_part, n_gr)
    summed = cross_rows.reshape(width, width).astype(jnp.float32)
    prior_whole = prior_rows.reshape(width, local_cols)
    diag_reduced = jnp.tril(diag_adjoint - summed)
    diag_gradient = diag_solve(diag_factor, diag_inverse, diag_reduced)
    below_prod = lax.dot_general(
        grad_rows.reshape(tile_count, tile_rows, width),
        prior_factor_rows(prior_rows, below_factor.shape),
        (((2,), (0,)), ((), ())),
        preferred_element_type=jnp.float32,
    ).reshape(below_adjoint.shape)
    below_new = (below_adjoint.astype(jnp.float32) - below_prod).astype(jnp.bfloat16)
    grid_row = lax.axis_index("gr")
    twice_rows = lax.dynamic_slice_in_dim(
        2.0 * diag_gradient, grid_row * prior_local, prior_local, 0
    ).astype(jnp.bfloat16)
    curvature = jnp.dot(twice_rows, prior_whole, preferred_element_type=jnp.float32)
    prior_bar = prior_adjoint.reshape(prior_local, local_cols).astype(jnp.float32)
    prior_new = (prior_bar - crossing - curvature).astype(jnp.bfloat16)
    return (
        below_new,
        panel_grad,
        prior_new.reshape(prior_adjoint.shape),
        diag_gradient,
    )


def line_length(mesh):
    column = list(mesh.devices[0])
    coords = [getattr(d, "coords", None) for d in column]
    if any(c is None for c in coords):
        return 8 if len(column) % 8 == 0 else len(column)
    first = coords[0][0]
    count = 0
    for c in coords:
        if c[0] != first:
            break
        count += 1
    return count if len(column) % count == 0 else len(column)


def solution(mesh):
    in_specs = (
        P(None, "gr", None, None, "gc", None),
        P(None, "gr", "gc", None),
        P("gr", None, "gc", None),
        P(),
        P(),
        P(None, "gr", None, None, "gc", None),
        P(None, "gr", "gc", None),
        P("gr", None, "gc", None),
        P(),
    )
    out_specs = (
        P(None, "gr", None, None, "gc", None),
        P(None, "gr", "gc", None),
        P("gr", None, "gc", None),
        P(),
    )
    return jax.shard_map(
        functools.partial(local, mesh.shape["gc"], mesh.shape["gr"], line_length(mesh)),
        mesh=mesh,
        in_specs=in_specs,
        out_specs=out_specs,
        check_vma=False,
    )
```

```python
import functools

import jax
import jax.numpy as jnp
from jax import lax
from jax.experimental import pallas as pl
from jax.experimental.pallas import tpu as pltpu
from jax.sharding import PartitionSpec as P

MESH_ID = pl.DeviceIdType.MESH


def row_product(left_rows, right_rows):
    return lax.dot_general(
        left_rows, right_rows, (((0,), (0,)), ((), ())), preferred_element_type=jnp.float32
    )


def diag_solve(diag_factor, diag_inverse, diag_reduced):
    highest = lax.Precision.HIGH
    chol_proj = jnp.dot(diag_factor.T, diag_reduced, precision=highest)
    index_row = lax.broadcasted_iota(jnp.int32, chol_proj.shape, 0)
    index_col = lax.broadcasted_iota(jnp.int32, chol_proj.shape, 1)
    phi_lower = jnp.where(
        index_row > index_col,
        chol_proj,
        jnp.where(index_row == index_col, chol_proj - 0.5 * chol_proj, 0.0),
    )
    symmetric = 0.5 * (phi_lower + phi_lower.T)
    left_side = jnp.dot(diag_inverse.T, symmetric, precision=highest)
    return jnp.dot(left_side, diag_inverse, precision=highest)


def by_width(index, rows, width, action):
    group = (rows * (index + 1) - 1) // 128
    for j in range(width // 128):
        @pl.when(group == j)
        def _():
            action(128 * (j + 1))


def gather_kernel(n, line, n_gr, x_ref, p_ref, prior_ref, out_ref, cross_out, prior_out, precv, recv_piece,
                  cross_slots, psems, sems, local_sem):
    me = lax.axis_index("gc")
    row = lax.axis_index("gr")
    rows = x_ref.shape[2]
    lines = n // line
    pos = lax.rem(me, line)
    grp = me // line
    base = grp * line

    def line_peer(k):
        return base + lax.rem(pos + k, line)

    def cross_peer(k):
        return lax.rem(grp + k, lines) * line + pos

    part_rows, part_width = p_ref.shape[1], p_ref.shape[2]
    kept = lax.broadcasted_iota(jnp.int32, p_ref.shape[1:], 1) < 128 * ((p_ref.shape[1] * (me + 1) - 1) // 128 + 1)
    barrier = pltpu.get_barrier_semaphore()

    def greet(k, carry):
        pl.semaphore_signal(barrier, inc=1, device_id=(row, lax.rem(me + k, n)), device_id_type=MESH_ID)
        return carry

    def greet_gr(k, carry):
        pl.semaphore_signal(barrier, inc=1, device_id=(lax.rem(row + k, n_gr), me), device_id_type=MESH_ID)
        return carry

    lax.fori_loop(1, n, greet, 0)
    lax.fori_loop(1, n_gr, greet_gr, 0)
    pl.semaphore_wait(barrier, n + n_gr - 2)

    def part_copy(k, sender, cols):
        peer = lax.rem(me + k, n)
        return pltpu.make_async_remote_copy(
            src_ref=p_ref.at[peer, :, pl.ds(0, cols)],
            dst_ref=precv.at[sender, :, pl.ds(0, cols)],
            send_sem=psems.at[0, k],
            recv_sem=psems.at[1, sender],
            device_id=(row, peer),
            device_id_type=MESH_ID,
        )

    def send_parts(k, carry):
        by_width(lax.rem(me + k, n), part_rows, part_width, lambda cols: part_copy(k, me, cols).start())
        return carry

    lax.fori_loop(1, n, send_parts, 0)

    def prior_copy(k, sender):
        return pltpu.make_async_remote_copy(
            src_ref=prior_ref,
            dst_ref=prior_out.at[sender],
            send_sem=psems.at[6, k],
            recv_sem=psems.at[7, sender],
            device_id=(lax.rem(row + k, n_gr), me),
            device_id_type=MESH_ID,
        )

    def send_prior(k, carry):
        prior_copy(k, row).start()
        return carry

    lax.fori_loop(1, n_gr, send_prior, 0)
    own_prior = pltpu.make_async_copy(prior_ref, prior_out.at[row], psems.at[6, 0])
    own_prior.start()

    own = pltpu.make_async_copy(x_ref, out_ref.at[:, :, pl.ds(me * rows, rows), :], local_sem)
    own.start()

    def first(k, sender_pos):
        return pltpu.make_async_remote_copy(
            src_ref=x_ref,
            dst_ref=out_ref.at[:, :, pl.ds((base + sender_pos) * rows, rows), :],
            send_sem=sems.at[0, k],
            recv_sem=sems.at[1, sender_pos],
            device_id=(row, line_peer(k)),
            device_id_type=MESH_ID,
        )

    def send_first(k, carry):
        first(k, pos).start()
        return carry

    lax.fori_loop(1, line, send_first, 0)


    span = line * rows

    def forward(k, block_pos, sender_grp):
        slot = pl.ds((grp * line + block_pos) * rows, rows)
        return pltpu.make_async_remote_copy(
            src_ref=out_ref.at[:, :, slot, :],
            dst_ref=out_ref.at[:, :, slot, :],
            send_sem=sems.at[2 + block_pos, k],
            recv_sem=sems.at[1, line + sender_grp],
            device_id=(row, cross_peer(k)),
            device_id_type=MESH_ID,
        )

    def whole_line(sender_grp):
        return pltpu.make_async_remote_copy(
            src_ref=out_ref.at[:, :, pl.ds(sender_grp * span, span), :],
            dst_ref=out_ref.at[:, :, pl.ds(sender_grp * span, span), :],
            send_sem=sems.at[0, 0],
            recv_sem=sems.at[1, line + sender_grp],
            device_id=(row, cross_peer(1)),
            device_id_type=MESH_ID,
        )

    own.wait()

    def send_own(k, carry):
        forward(k, pos, grp).start()
        return carry

    lax.fori_loop(1, lines, send_own, 0)


    precv[me] = p_ref[me]

    def wait_parts(k, carry):
        sender = lax.rem(me + n - k, n)
        by_width(lax.rem(me + k, n), part_rows, part_width, lambda cols: part_copy(k, me, cols).wait_send())
        by_width(me, part_rows, part_width, lambda cols: part_copy(k, sender, cols).wait_recv())
        return carry

    lax.fori_loop(1, n, wait_parts, 0)

    def add_part(j, total):
        return total + precv[j].astype(jnp.float32)

    piece = lax.fori_loop(0, n, add_part, jnp.zeros(recv_piece.shape[1:], jnp.float32))
    recv_piece[row] = jnp.where(kept, piece, 0.0)

    def piece_copy(k, sender, cols):
        return pltpu.make_async_remote_copy(
            src_ref=recv_piece.at[row, :, pl.ds(0, cols)],
            dst_ref=recv_piece.at[sender, :, pl.ds(0, cols)],
            send_sem=psems.at[2, k],
            recv_sem=psems.at[3, sender],
            device_id=(lax.rem(row + k, n_gr), me),
            device_id_type=MESH_ID,
        )

    def send_piece(k, carry):
        by_width(me, part_rows, part_width, lambda cols: piece_copy(k, row, cols).start())
        return carry

    lax.fori_loop(1, n_gr, send_piece, 0)

    def relay(k, carry):
        sender_pos = lax.rem(pos + line - k, line)
        first(k, sender_pos).wait_recv()

        def out(j, inner):
            forward(j, sender_pos, grp).start()
            return inner

        return lax.fori_loop(1, lines, out, carry)

    lax.fori_loop(1, line, relay, 0)

    def wait_piece(k, carry):
        sender = lax.rem(row + n_gr - k, n_gr)
        by_width(me, part_rows, part_width, lambda cols: piece_copy(k, row, cols).wait_send())
        by_width(me, part_rows, part_width, lambda cols: piece_copy(k, sender, cols).wait_recv())
        return carry

    lax.fori_loop(1, n_gr, wait_piece, 0)

    def add_piece(j, total):
        return total + recv_piece[j]

    summed = lax.fori_loop(0, n_gr, add_piece, jnp.zeros(recv_piece.shape[1:], jnp.float32))
    cross_slots[me] = jnp.where(kept, summed, 0.0).astype(cross_slots.dtype)

    def cross_copy(k, sender, cols):
        return pltpu.make_async_remote_copy(
            src_ref=cross_slots.at[me, :, pl.ds(0, cols)],
            dst_ref=cross_slots.at[sender, :, pl.ds(0, cols)],
            send_sem=psems.at[4, k],
            recv_sem=psems.at[5, sender],
            device_id=(row, lax.rem(me + k, n)),
            device_id_type=MESH_ID,
        )

    def send_cross(k, carry):
        by_width(me, part_rows, part_width, lambda cols: cross_copy(k, me, cols).start())
        return carry

    lax.fori_loop(1, n, send_cross, 0)


    def wait_first(k, carry):
        first(k, pos).wait_send()
        return carry

    lax.fori_loop(1, line, wait_first, 0)

    def wait_sent(k, carry):
        def done(j, inner):
            forward(j, k, grp).wait_send()
            return inner

        return lax.fori_loop(1, lines, done, carry)

    lax.fori_loop(0, line, wait_sent, 0)

    def wait_lines(k, carry):
        whole_line(lax.rem(grp + lines - k, lines)).wait_recv()
        return carry

    lax.fori_loop(1, lines, wait_lines, 0)

    def wait_cross(k, carry):
        sender = lax.rem(me + n - k, n)
        by_width(me, part_rows, part_width, lambda cols: cross_copy(k, me, cols).wait_send())
        by_width(sender, part_rows, part_width, lambda cols: cross_copy(k, sender, cols).wait_recv())
        return carry

    lax.fori_loop(1, n, wait_cross, 0)
    cross_out[...] = cross_slots[...]

    def wait_prior(k, carry):
        prior_copy(k, row).wait_send()
        prior_copy(k, lax.rem(row + n_gr - k, n_gr)).wait_recv()
        return carry

    lax.fori_loop(1, n_gr, wait_prior, 0)
    own_prior.wait()


def gather_gc(block, part, prior_rows, n, line, n_gr):
    tiles, count, rows, width = block.shape
    vmem = pl.BlockSpec(memory_space=pltpu.VMEM)
    return pl.pallas_call(
        functools.partial(gather_kernel, n, line, n_gr),
        out_shape=(
            jax.ShapeDtypeStruct((tiles, count, rows * n, width), block.dtype),
            jax.ShapeDtypeStruct(part.shape, jnp.bfloat16),
            jax.ShapeDtypeStruct((n_gr,) + prior_rows.shape, prior_rows.dtype),
        ),
        in_specs=[pl.BlockSpec(memory_space=pl.ANY), vmem, pl.BlockSpec(memory_space=pl.ANY)],
        out_specs=(pl.BlockSpec(memory_space=pl.ANY), vmem, pl.BlockSpec(memory_space=pl.ANY)),
        scratch_shapes=[
            pltpu.VMEM(part.shape, part.dtype),
            pltpu.VMEM((n_gr,) + part.shape[1:], jnp.float32),
            pltpu.VMEM(part.shape, jnp.bfloat16),
            pltpu.SemaphoreType.DMA((8, max(n, n_gr))),
            pltpu.SemaphoreType.DMA((2 + line, line + n // line)),
            pltpu.SemaphoreType.DMA,
        ],
        compiler_params=pltpu.CompilerParams(collective_id=0, has_side_effects=True),
    )(block, part, prior_rows)


def reduce_kernel(n, crossing_ref, crossing_out, recv_crossing, sems):
    me = lax.axis_index("gr")
    col = lax.axis_index("gc")
    rows = crossing_out.shape[0]

    barrier = pltpu.get_barrier_semaphore()

    def greet_gr(k, carry):
        pl.semaphore_signal(barrier, inc=1, device_id=(lax.rem(me + k, n), col), device_id_type=MESH_ID)
        return carry

    lax.fori_loop(1, n, greet_gr, 0)
    pl.semaphore_wait(barrier, n - 1)

    def gr_copy(k, sender, src, dst, index):
        return pltpu.make_async_remote_copy(
            src_ref=src,
            dst_ref=dst.at[sender],
            send_sem=sems.at[index, k],
            recv_sem=sems.at[index + 1, sender],
            device_id=(lax.rem(me + k, n), col),
            device_id_type=MESH_ID,
        )

    def crossing_copy(k, sender):
        peer = lax.rem(me + k, n)
        src = crossing_ref.at[pl.ds(pl.multiple_of(peer * rows, rows), rows), :]
        return gr_copy(k, sender, src, recv_crossing, 0)

    def send(k, carry):
        crossing_copy(k, me).start()
        return carry

    lax.fori_loop(1, n, send, 0)
    recv_crossing[me] = crossing_ref[pl.ds(pl.multiple_of(me * rows, rows), rows), :]

    def wait(k, carry):
        sender = lax.rem(me + n - k, n)
        crossing_copy(k, me).wait_send()
        crossing_copy(k, sender).wait_recv()
        return carry

    lax.fori_loop(1, n, wait, 0)

    def add_crossing(j, total):
        return total + recv_crossing[j].astype(jnp.float32)

    crossing_out[...] = lax.fori_loop(0, n, add_crossing, jnp.zeros(crossing_out.shape, jnp.float32))


def reduce_gr(crossing_part, n):
    rows = crossing_part.shape[0] // n
    cols = crossing_part.shape[1]
    vmem = pl.BlockSpec(memory_space=pltpu.VMEM)
    return pl.pallas_call(
        functools.partial(reduce_kernel, n),
        out_shape=jax.ShapeDtypeStruct((rows, cols), jnp.float32),
        in_specs=[vmem],
        out_specs=vmem,
        scratch_shapes=[
            pltpu.VMEM((n, rows, cols), crossing_part.dtype),
            pltpu.SemaphoreType.DMA((2, n)),
        ],
        compiler_params=pltpu.CompilerParams(collective_id=1, has_side_effects=True),
    )(crossing_part)


def prior_factor_rows(prior_rows, below_shape):
    return prior_rows.reshape(-1, below_shape[3], below_shape[5])


def local(
    n_gc,
    n_gr,
    line,
    below_factor,
    panel_factor,
    prior_factor,
    diag_factor,
    diag_inverse,
    below_adjoint,
    panel_adjoint,
    prior_adjoint,
    diag_adjoint,
):
    tile_count = below_factor.shape[0]
    tile_rows = below_factor.shape[2]
    local_rows = tile_count * tile_rows
    local_cols = below_factor.shape[3] * below_factor.shape[5]
    own_rows = panel_factor.shape[2]
    width = panel_factor.shape[3]
    prior_local = prior_factor.shape[0]
    below_mat = below_factor.reshape(local_rows, local_cols)
    below_bar = below_adjoint.reshape(local_rows, local_cols)
    inverse_bf = diag_inverse.astype(jnp.bfloat16)
    own_grad = lax.dot_general(
        panel_adjoint.reshape(tile_count, own_rows, width),
        inverse_bf,
        (((2,), (0,)), ((), ())),
        preferred_element_type=jnp.float32,
    ).astype(jnp.bfloat16)
    panel_grad = own_grad.reshape(panel_adjoint.shape)
    own_part = lax.dot_general(
        own_grad,
        panel_factor.reshape(tile_count, own_rows, width),
        (((0, 1), (0, 1)), ((), ())),
        preferred_element_type=jnp.float32,
    ).astype(jnp.bfloat16)
    prior_here = prior_factor.reshape(prior_local, below_factor.shape[3], below_factor.shape[5])
    whole, cross_rows, prior_rows = gather_gc(
        panel_grad,
        own_part.reshape(n_gc, width // n_gc, width),
        prior_here,
        n_gc,
        line,
        n_gr,
    )
    grad_rows = whole.reshape(local_rows, width)
    crossing_part = row_product(grad_rows, below_mat).astype(jnp.bfloat16)
    crossing = reduce_gr(crossing_part, n_gr)
    summed = cross_rows.reshape(width, width).astype(jnp.float32)
    prior_whole = prior_rows.reshape(width, local_cols)
    diag_reduced = jnp.tril(diag_adjoint - summed)
    diag_gradient = diag_solve(diag_factor, diag_inverse, diag_reduced)
    below_prod = lax.dot_general(
        grad_rows.reshape(tile_count, tile_rows, width),
        prior_factor_rows(prior_rows, below_factor.shape),
        (((2,), (0,)), ((), ())),
        preferred_element_type=jnp.float32,
    ).reshape(below_adjoint.shape)
    below_new = (below_adjoint.astype(jnp.float32) - below_prod).astype(jnp.bfloat16)
    grid_row = lax.axis_index("gr")
    twice_rows = lax.dynamic_slice_in_dim(
        2.0 * diag_gradient, grid_row * prior_local, prior_local, 0
    ).astype(jnp.bfloat16)
    curvature = jnp.dot(twice_rows, prior_whole, preferred_element_type=jnp.float32)
    prior_bar = prior_adjoint.reshape(prior_local, local_cols).astype(jnp.float32)
    prior_new = (prior_bar - crossing - curvature).astype(jnp.bfloat16)
    return (
        below_new,
        panel_grad,
        prior_new.reshape(prior_adjoint.shape),
        diag_gradient,
    )


def line_length(mesh):
    column = list(mesh.devices[0])
    coords = [getattr(d, "coords", None) for d in column]
    if any(c is None for c in coords):
        return 8 if len(column) % 8 == 0 else len(column)
    first = coords[0][0]
    count = 0
    for c in coords:
        if c[0] != first:
            break
        count += 1
    return count if len(column) % count == 0 else len(column)


def solution(mesh):
    in_specs = (
        P(None, "gr", None, None, "gc", None),
        P(None, "gr", "gc", None),
        P("gr", None, "gc", None),
        P(),
        P(),
        P(None, "gr", None, None, "gc", None),
        P(None, "gr", "gc", None),
        P("gr", None, "gc", None),
        P(),
    )
    out_specs = (
        P(None, "gr", None, None, "gc", None),
        P(None, "gr", "gc", None),
        P("gr", None, "gc", None),
        P(),
    )
    return jax.shard_map(
        functools.partial(local, mesh.shape["gc"], mesh.shape["gr"], line_length(mesh)),
        mesh=mesh,
        in_specs=in_specs,
        out_specs=out_specs,
        check_vma=False,
    )
```
